32 devices in a mesh: dp: 8 (over z, y), fsdp: 4 (over x, core).
Axes of the slice: x: 2, y: 2, z: 4, core: 2. Of those that a mesh axis runs over, the one named last changes fastest.
Arguments:
- tokens: bfloat16 [16384, 1024], P(('dp', 'fsdp')), may hold values from -6 to 6
- seq_lengths: int32 [32, 4], P(('dp', 'fsdp')), may hold values from 0 to 512, as said below
- w_query: bfloat16 [1024, 256], P(('dp', 'fsdp')), may hold values from -0.1875 to 0.1875
- w_key: bfloat16 [1024, 256], P(('dp', 'fsdp')), may hold values from -0.1875 to 0.1875
- w_value: bfloat16 [1024, 1024], P(('dp', 'fsdp')), may hold values from -0.1875 to 0.1875
- w_output: bfloat16 [1024, 1024], P(None, ('dp', 'fsdp')), may hold values from -2 to 2
- w_gate: bfloat16 [1024, 2752], P(('dp', 'fsdp')), may hold values from -0.1875 to 0.1875
- w_up: bfloat16 [1024, 2752], P(('dp', 'fsdp')), may hold values from -0.1875 to 0.1875
- w_down: bfloat16 [2752, 1024], P(None, ('dp', 'fsdp')), may hold values from -0.15625 to 0.15625
- gain_attn: float32 [1024], P(('dp', 'fsdp')), may hold values from 0.1 to 1.9
- gain_mlp: float32 [1024], P(('dp', 'fsdp')), may hold values from 0.1 to 1.9
- cotangent: bfloat16 [16384, 1024], P(('dp', 'fsdp')), may hold values from -6 to 6
Outputs:
- layer_out: bfloat16 [16384, 1024], P(('dp', 'fsdp'))
- grad_tokens: bfloat16 [16384, 1024], P(('dp', 'fsdp'))
- grad_query: float32 [1024, 256], P(('dp', 'fsdp'))
- grad_key: float32 [1024, 256], P(('dp', 'fsdp'))
- grad_value: float32 [1024, 1024], P(('dp', 'fsdp'))
- grad_output: float32 [1024, 1024], P(None, ('dp', 'fsdp'))
- grad_gate: float32 [1024, 2752], P(('dp', 'fsdp'))
- grad_up: float32 [1024, 2752], P(('dp', 'fsdp'))
- grad_down: float32 [2752, 1024], P(None, ('dp', 'fsdp'))
- grad_gain_attn: float32 [1024], P(('dp', 'fsdp'))
- grad_gain_mlp: float32 [1024], P(('dp', 'fsdp'))
The draws below stay inside these ranges and needn't reach their ends.
Inputs may be any that keep to these rules, and one draw needn't show every extreme that they name: `seq_lengths`: row r lists the lengths of the sequences packed back to back from position 0 of buffer r; a length is 0 (an unused slot) or 128 or more, a row sums to at most 512, and positions past the sum are padding.
All inputs are finite; a program needn't handle non-finite values.
Results may differ from the reference program's by a relative error of at most 0.034.
Values may be sent and summed in bfloat16 or wider, within the bound.
No kernel may reach another device: no remote copies, remote signals or barrier semaphores. Data moves between devices by JAX's collectives and lax.ppermute only.
A program may use at most 192 MiB of HBM per device.

```python
import math
import jax
import jax.numpy as jnp
from jax import lax

D = 1024
H = 16
F = 16
DV = 64
FF = 2752
TOK_DEV = 512
SLOTS = 4
MIN_LEN = 128
BUFFERS = 32
TOKENS = 16384


def draw_seq_lengths(key, part):
    pad_key, length_key = jax.random.split(key)
    first_rows = jnp.arange(BUFFERS, dtype=jnp.int32) == 0
    padding = jnp.where(first_rows, 0, jax.random.randint(pad_key, (BUFFERS,), 0, TOK_DEV // 4 + 1))
    wanted = jax.random.randint(length_key, (BUFFERS, SLOTS), MIN_LEN, TOK_DEV + 1)
    wanted = wanted.at[0, 0].set(TOK_DEV)
    room = TOK_DEV - padding
    used = jnp.zeros((BUFFERS,), jnp.int32)
    columns = []
    for slot_index in range(SLOTS):
        remain = room - used
        length_now = jnp.where(remain >= MIN_LEN, jnp.minimum(remain, wanted[:, slot_index]), 0)
        used = used + length_now
        columns.append(length_now)
    return jnp.stack(columns, axis=1).astype(jnp.int32)


def shard_levels(stream_key, extent, pieces, low, largest):
    def one(position, shards_of):
        draws = jax.random.uniform(jax.random.fold_in(jax.random.fold_in(stream_key, 6), position), (shards_of,), jnp.float32, low / len(pieces), largest / len(pieces))
        return jnp.repeat(jnp.exp(draws), extent[position] // shards_of).reshape((-1,) + (1,) * (len(extent) - position - 1))

    level = one(*pieces[0])
    for cut in pieces[1:]:
        level = level * one(*cut)
    return level


def normal_values(key, dims, spread, most, pieces=(), kind=jnp.bfloat16):
    gain = shard_levels(key, dims, pieces, -0.22, 0.18) if pieces else 1.0
    values = jax.random.normal(key, dims, jnp.float32) * spread * gain
    return jnp.minimum(jnp.maximum(values, -most), most).astype(kind)


def setup_inputs(seed: int = 0) -> dict:
    splits = jax.random.split(jax.random.key(seed), 13)
    return {
        "tokens": normal_values(splits[0], (TOKENS, D), 1.0, 6.0, ((0, 32),)),
        "seq_lengths": draw_seq_lengths(jax.random.fold_in(splits[12], 71), 0),
        "w_query": normal_values(splits[2], (D, H * F), D ** -0.5, 0.1875, ((0, 32),)),
        "w_key": normal_values(splits[3], (D, H * F), D ** -0.5, 0.1875, ((0, 32),)),
        "w_value": normal_values(splits[4], (D, H * DV), D ** -0.5, 0.1875, ((0, 32),)),
        "w_output": normal_values(splits[5], (H * DV, D), (max(H * DV // 128, 1)) ** -0.5, 2.0, ((1, 32),)),
        "w_gate": normal_values(splits[6], (D, FF), D ** -0.5, 0.1875, ((0, 32),)),
        "w_up": normal_values(splits[7], (D, FF), D ** -0.5, 0.1875, ((0, 32),)),
        "w_down": normal_values(splits[8], (FF, D), (FF // 2) ** -0.5, 0.15625, ((1, 32),)),
        "gain_attn": jnp.clip(1.0 + 0.18 * jax.random.normal(splits[9], (D,), jnp.float32), 0.1, 1.9),
        "gain_mlp": jnp.clip(1.0 + 0.18 * jax.random.normal(splits[10], (D,), jnp.float32), 0.1, 1.9),
        "cotangent": normal_values(splits[11], (TOKENS, D), 1.0, 6.0, ((0, 32),)),
    }


@jax.custom_vjp
def low(v):
    return lax.optimization_barrier(v.astype(jnp.bfloat16)).astype(jnp.float32)

@jax.custom_vjp
def low_back(v):
    return v

def low_keep(v):
    return (low(v), None)

def low_pass(kept, grad):
    return (grad,)

def back_keep(v):
    return (v, None)

def back_low(kept, grad):
    return (low(grad),)
low.defvjp(low_keep, low_pass)
low_back.defvjp(back_keep, back_low)
EPS = 1e-05
HIGH = lax.Precision.HIGHEST

def buffer_masks(lengths):
    positions = jnp.arange(TOK_DEV, dtype=jnp.int32)
    ends = jnp.cumsum(lengths, dtype=jnp.int32)
    segment = lax.optimization_barrier(jnp.sum((positions[:, None] >= ends[None, :]).astype(jnp.int32), axis=1))
    valid_rows = (positions < ends[-1]).astype(jnp.float32)
    allowed = (positions[None, :] <= positions[:, None]) & (segment[None, :] == segment[:, None])
    mask_table = allowed.astype(jnp.float32) * valid_rows[:, None]
    return (mask_table, valid_rows)

def layer_rows(tokens_f, lengths, weight_tuple):
    query_w, key_w, value_w, output_w, gate_w, up_w, down_w, gain_one, gain_two = weight_tuple
    mask_table, valid_rows = buffer_masks(lengths)
    rows = tokens_f.shape[0]
    scale = 1.0 / math.sqrt(F)
    inverse_one = lax.rsqrt(lax.optimization_barrier(jnp.mean(tokens_f * tokens_f, axis=-1, keepdims=True)) + EPS)
    normed_one = low(tokens_f * inverse_one * gain_one)
    queries = low_back(low(jnp.dot(normed_one, query_w, precision=HIGH)))
    key_rows = low_back(low(jnp.dot(normed_one, key_w, precision=HIGH)))
    value_rows = low_back(low(jnp.dot(normed_one, value_w, precision=HIGH)))
    query_heads = queries.reshape(rows, H, F)
    key_heads = key_rows.reshape(rows, H, F)
    value_heads = value_rows.reshape(rows, H, DV)
    scores = low_back(jnp.einsum('thf,shf->hts', query_heads, key_heads, precision=HIGH) * scale)
    raw_weights = (1.0 + scores + 0.5 * scores * scores) * mask_table[None]
    totals = lax.optimization_barrier(jnp.sum(raw_weights, axis=-1, keepdims=True)) + (1.0 - valid_rows)[None, :, None]
    probs = low(raw_weights / totals)
    mixed = jnp.einsum('hts,shd->thd', probs, value_heads, precision=HIGH).reshape(rows, H * DV)
    mixed = low_back(low(mixed))
    resid = tokens_f + low_back(jnp.dot(mixed, output_w, precision=HIGH))
    inverse_two = lax.rsqrt(lax.optimization_barrier(jnp.mean(resid * resid, axis=-1, keepdims=True)) + EPS)
    normed_two = low(resid * inverse_two * gain_two)
    gate = low_back(jnp.dot(normed_two, gate_w, precision=HIGH))
    upper = low_back(jnp.dot(normed_two, up_w, precision=HIGH))
    hidden = low_back(low(jax.nn.silu(gate) * upper))
    return resid + jnp.dot(hidden, down_w, precision=HIGH)

def reference(tokens, seq_lengths, w_query, w_key, w_value, w_output, w_gate, w_up, w_down, gain_attn, gain_mlp, cotangent):
    weight_tuple = (w_query.astype(jnp.float32), w_key.astype(jnp.float32), w_value.astype(jnp.float32), w_output.astype(jnp.float32), w_gate.astype(jnp.float32), w_up.astype(jnp.float32), w_down.astype(jnp.float32), gain_attn.astype(jnp.float32), gain_mlp.astype(jnp.float32))
    tokens_f = tokens.astype(jnp.float32)

    def forward(tokens_all, weights_all):
        stacked = tokens_all.reshape(BUFFERS, TOK_DEV, D)

        def one_buffer(pair):
            return layer_rows(pair[0], pair[1], weights_all)
        result = lax.map(jax.checkpoint(one_buffer), (stacked, seq_lengths))
        return result.reshape(BUFFERS * TOK_DEV, D)
    output, pullback = jax.vjp(forward, tokens_f, weight_tuple)
    grad_input, grad_weights = pullback(cotangent.astype(jnp.float32))
    return (output.astype(jnp.bfloat16), grad_input.astype(jnp.bfloat16), grad_weights[0], grad_weights[1], grad_weights[2], grad_weights[3], grad_weights[4], grad_weights[5], grad_weights[6], grad_weights[7], grad_weights[8])
```

```python
import functools
import math

import jax
import jax.numpy as jnp
from jax import lax
from jax.experimental import pallas as pl
from jax.experimental.pallas import tpu as pltpu
from jax.sharding import PartitionSpec as P

H = 16
F = 16
EPS = 1e-05
AXES = ("dp", "fsdp")
LANES = 128
VMEM_BYTES = 64000000
F32 = jnp.float32
BF16 = jnp.bfloat16

VMEM_SPEC = pl.BlockSpec(memory_space=pltpu.VMEM)
SMEM_SPEC = pl.BlockSpec(memory_space=pltpu.SMEM)
ANY_SPEC = pl.BlockSpec(memory_space=pl.ANY)


def dot_nn(a, b):
    return lax.dot_general(a, b, (((1,), (0,)), ((), ())), preferred_element_type=F32)


def dot_nt(a, b):
    return lax.dot_general(a, b, (((1,), (1,)), ((), ())), preferred_element_type=F32)


def dot_tn(a, b):
    return lax.dot_general(a, b, (((0,), (0,)), ((), ())), preferred_element_type=F32)


class Layout:
    def __init__(self, mesh):
        dp, fsdp = mesh.shape["dp"], mesh.shape["fsdp"]
        self.count = dp * fsdp
        x_bits = int(math.log2(fsdp)) - 1
        y_bits = int(math.log2(dp)) // 3
        all_bits = int(math.log2(self.count))
        self.x = [1 << (1 + i) for i in range(x_bits)]
        self.y = [1 << (1 + x_bits + i) for i in range(y_bits)]
        self.z = [1 << i for i in range(1 + x_bits + y_bits, all_bits)]

    def swap(self, value, bit):
        return lax.ppermute(value, AXES, [(i, i ^ bit) for i in range(self.count)])


def masks_of(bits):
    masks = [0]
    for bit in bits:
        masks = masks + [m | bit for m in masks]
    return masks


def gather(lay, block_own, block_other):
    found = {0: jnp.stack([block_own, block_other])}
    for bit in reversed(lay.z):
        found.update({m | bit: lay.swap(v, bit) for m, v in list(found.items())})
    z_masks = masks_of(lay.z)
    pieces = []
    for half, order in ((0, lay.x + lay.y), (1, lay.y + lay.x)):
        held = jnp.stack([found[m][half] for m in z_masks])
        masks = [m | half for m in z_masks]
        for bit in order[:-1]:
            came = lay.swap(held, bit)
            held = jnp.concatenate([held, came], axis=0)
            masks = masks + [m | bit for m in masks]
        pieces.append((held, masks))
        pieces.append((lay.swap(held, order[-1]), [m | order[-1] for m in masks]))
    return pieces


def scatter_masks(lay):
    z_masks = masks_of(lay.z)
    arrays = []
    for half, order in ((0, lay.x + lay.y), (1, lay.y + lay.x)):
        masks = [m | half for m in z_masks]
        for bit in order[:-1]:
            masks = masks + [m | bit for m in masks]
        arrays.append(masks)
        arrays.append([m | order[-1] for m in masks])
    return arrays


def add_low(a, b):
    return (a.astype(F32) + b.astype(F32)).astype(BF16)


def reduce_blocks(lay, arrays):
    ends = []
    for half, order in ((0, lay.x + lay.y), (1, lay.y + lay.x)):
        kept, sent = arrays[2 * half], arrays[2 * half + 1]
        came = lay.swap(sent, order[-1])
        for bit in reversed(order[:-1]):
            n = kept.shape[0] // 2
            sent = add_low(kept[n:], came[n:])
            kept = add_low(kept[:n], came[:n])
            came = lay.swap(sent, bit)
        ends.append((kept, came))
    z_masks = masks_of(lay.z)

    def block(i):
        return jnp.stack([kept[i].astype(F32) + came[i].astype(F32) for kept, came in ends])

    held = {m: block(i) for i, m in enumerate(z_masks)}
    for bit in lay.z:
        for m in [m for m in held if m & bit]:
            came = lay.swap(held.pop(m).astype(BF16), bit)
            held[m ^ bit] = held[m ^ bit] + came.astype(F32)
    return held[0]


class Blocks:
    def __init__(self, lay, rows):
        self.lay = lay
        self.rows = rows
        self.direct = rows % 16 == 0
        self.shape = (lay.count, rows) if self.direct else (1, lay.count * rows)

    def order(self, index):
        return jnp.bitwise_xor(index, jnp.arange(self.lay.count))

    def arrays(self, pieces, index):
        if self.direct:
            return [a for a, _ in pieces]
        masks = [m for _, ms in pieces for m in ms]
        whole = jnp.concatenate([a for a, _ in pieces], axis=0)
        place = [0] * len(masks)
        for i, m in enumerate(masks):
            place[m] = i
        whole = jnp.take(whole, jnp.asarray(place)[self.order(index)], axis=0)
        return [whole.reshape(1, -1, whole.shape[-1])]

    def copies_in(self, index, refs, masks, out_ref, sem):
        if not self.direct:
            return [pltpu.make_async_copy(refs[0], out_ref, sem)]
        return [
            pltpu.make_async_copy(
                ref.at[i], out_ref.at[jnp.bitwise_xor(index, m)], sem
            )
            for ref, ms in zip(refs, masks)
            for i, m in enumerate(ms)
        ]

    def out_shapes(self, masks, columns):
        if self.direct:
            return [jax.ShapeDtypeStruct((len(m), self.rows, columns), BF16) for m in masks]
        return [jax.ShapeDtypeStruct((1, self.lay.count * self.rows, columns), BF16)]

    def copies_out(self, index, in_ref, refs, masks, sem):
        if not self.direct:
            return [pltpu.make_async_copy(in_ref, refs[0], sem)]
        return [
            pltpu.make_async_copy(
                in_ref.at[jnp.bitwise_xor(index, m)], ref.at[i], sem
            )
            for ref, ms in zip(refs, masks)
            for i, m in enumerate(ms)
        ]

    def split(self, outs, masks, index):
        if self.direct:
            return outs
        whole = outs[0].reshape(self.lay.count, self.rows, -1)
        whole = jnp.take(whole, self.order(index), axis=0)
        return [jnp.take(whole, jnp.asarray(m), axis=0) for m in masks]


def start_all(copies):
    for copy in copies:
        copy.start()


def whole(ref):
    value = ref[...]
    return value.reshape(-1, value.shape[-1])


def cost(flops, moved):
    return pl.CostEstimate(flops=int(flops), bytes_accessed=int(moved), transcendentals=0)


def params():
    return pltpu.CompilerParams(vmem_limit_bytes=VMEM_BYTES)


def row_chunks(total, size, body):
    def step(i, carry):
        body(pl.ds(pl.multiple_of(i * size, size), size))
        return carry

    lax.fori_loop(0, total // size, step, 0)


def make_mask(seq_ref, b, mask_ref):
    rows, cols = mask_ref.shape
    slots = seq_ref.shape[1]
    ends = []
    total = jnp.int32(0)
    for j in range(slots):
        total = total + seq_ref[b, j]
        ends.append(total)

    def body(at):
        t = lax.broadcasted_iota(jnp.int32, (at.size, cols), 0) + at.start
        s = lax.broadcasted_iota(jnp.int32, (at.size, cols), 1)
        seg_t = jnp.zeros_like(t)
        seg_s = jnp.zeros_like(s)
        for e in ends:
            seg_t = seg_t + (t >= e).astype(jnp.int32)
            seg_s = seg_s + (s >= e).astype(jnp.int32)
        seen = (s <= t) & (seg_t == seg_s) & (t < total)
        mask_ref[at, :] = jnp.where(seen, 0.5, 0.0).astype(F32)

    row_chunks(rows, 64, body)
    return total


def attn_fwd(blk, masks, index, seq, tok, arrays, dims):
    n_tok, width, buffers = tok.shape[0], tok.shape[1], seq.shape[0]
    length = n_tok // buffers
    nq, nv, cols = dims
    n_qkv = 2 * nq + nv
    n_in = len(arrays)

    def body(index_ref, seq_ref, tok_ref, *refs):
        w_in = refs[:n_in]
        normed_ref, qkv_ref, y_ref, dinv_ref, part_ref, gain_ref, w_ref = refs[n_in : n_in + 7]
        mask_ref, sem = refs[n_in + 7 :]
        copies = blk.copies_in(index_ref[0], w_in, masks, w_ref, sem)
        start_all(copies)
        pltpu.make_async_copy(w_ref, w_ref, sem).wait()
        w_gain = w_ref[:, :, n_qkv + nv :].reshape(width, LANES).astype(F32).T
        gain_ref[0:1, :] = w_gain[0:1] + w_gain[1:2]
        gain_ref[1:2, :] = w_gain[2:3] + w_gain[3:4]
        gain_ref[2:8, :] = jnp.zeros((6, width), F32)
        gain = gain_ref[0:1, :]

        def project(at):
            x = tok_ref[at, :].astype(F32)
            inverse = lax.rsqrt(jnp.mean(x * x, axis=-1, keepdims=True) + EPS)
            normed = (x * inverse * gain).astype(BF16)
            normed_ref[at, :] = normed
            w = w_ref[:, :, :n_qkv].reshape(width, n_qkv)
            qkv_ref[at, :] = dot_nn(normed, w).astype(BF16)

        row_chunks(n_tok, 256, project)

        for b in range(buffers):
            total = make_mask(seq_ref, b, mask_ref)
            base = b * length

            def pair(hp, carry):
                lane = lax.broadcasted_iota(jnp.int32, (1, LANES), 1)
                k = qkv_ref[base : base + length, nq : 2 * nq]
                v_at = pl.ds(pl.multiple_of(2 * nq + hp * LANES, LANES), LANES)
                v = qkv_ref[base : base + length, v_at]
                step = length // 2
                for tb in range(2):
                    rows = slice(base + tb * step, base + (tb + 1) * step)
                    seen = (tb + 1) * step
                    q = qkv_ref[rows, :nq] * jnp.asarray(0.25, BF16)
                    mask = mask_ref[tb * step : (tb + 1) * step, :seen]
                    row = lax.broadcasted_iota(jnp.int32, (step, 1), 0) + tb * step
                    pad = (row >= total).astype(F32)
                    found = []
                    for j in range(2):
                        k_h = jnp.where(lane // F == 2 * hp + j, k[:seen], jnp.zeros((), BF16))
                        v_h = jnp.where(lane // 64 == j, v[:seen], jnp.ones((), BF16))
                        one = dot_nt(q, k_h) + 1.0
                        weights = ((one * one + 1.0) * mask).astype(BF16)
                        mixed = dot_nn(weights, v_h)
                        inverse = 1.0 / (pltpu.roll(mixed, 64, 1) + pad)
                        found.append((mixed * inverse, inverse))
                    low = lane < 64
                    y_at = pl.ds(pl.multiple_of(hp * LANES, LANES), LANES)
                    y_ref[rows, y_at] = jnp.where(low, found[0][0], found[1][0]).astype(BF16)
                    dinv_ref[rows, y_at] = jnp.where(low, found[0][1], found[1][1])
                return carry

            lax.fori_loop(0, nv // LANES, pair, 0)

        def output(at):
            w = w_ref[:, :, n_qkv : n_qkv + nv].reshape(width, nv)
            part_ref[at, :] = dot_nt(y_ref[at, :], w).astype(BF16)

        row_chunks(n_tok, 256, output)

    out = lambda *s, t=BF16: jax.ShapeDtypeStruct(s, t)
    return pl.pallas_call(
        body,
        name="attn_fwd",
        out_shape=(
            out(n_tok, width),
            out(n_tok, n_qkv),
            out(n_tok, nv),
            out(n_tok, nv, t=F32),
            out(n_tok, width),
            out(8, width, t=F32),
            out(*blk.shape, cols),
        ),
        in_specs=[SMEM_SPEC, SMEM_SPEC, VMEM_SPEC] + [ANY_SPEC] * n_in,
        out_specs=(VMEM_SPEC,) * 7,
        scratch_shapes=[pltpu.VMEM((length, length), F32), pltpu.SemaphoreType.DMA],
        compiler_params=params(),
        cost_estimate=cost(1.5e10, 1e7),
    )(index, seq, tok, *arrays)


def residual(tok, part, came, gains):
    n_tok, width = tok.shape
    half = n_tok // 2

    def body(tok_ref, part_ref, came_ref, gain_ref, hres_ref, normed_ref):
        gain = gain_ref[1:2, :]

        def rows(at, other):
            x = tok_ref[at, :].astype(F32)
            x = x + (part_ref[at, :].astype(F32) + came_ref[other, :].astype(F32))
            hres_ref[at, :] = x
            inverse = lax.rsqrt(jnp.mean(x * x, axis=-1, keepdims=True) + EPS)
            normed_ref[at, :] = (x * inverse * gain).astype(BF16)

        def step(i, carry):
            lo = pl.ds(pl.multiple_of(i * 128, 128), 128)
            hi = pl.ds(pl.multiple_of(half + i * 128, 128), 128)
            rows(lo, hi)
            rows(hi, lo)
            return carry

        lax.fori_loop(0, half // 128, step, 0)

    return pl.pallas_call(
        body,
        name="residual",
        out_shape=(
            jax.ShapeDtypeStruct((n_tok, width), F32),
            jax.ShapeDtypeStruct((n_tok, width), BF16),
        ),
        in_specs=[VMEM_SPEC] * 4,
        out_specs=(VMEM_SPEC,) * 2,
        compiler_params=params(),
        cost_estimate=cost(1e7, 1.2e7),
    )(tok, part, came, gains)


def down_back(blk, masks, index, grad_out, arrays, cols):
    n_tok, width = grad_out.shape
    n_in = len(arrays)

    def body(index_ref, grad_ref, *refs):
        d_act_ref, w_ref, sem = refs[n_in:]
        start_all(blk.copies_in(index_ref[0], refs[:n_in], masks, w_ref, sem))
        pltpu.make_async_copy(w_ref, w_ref, sem).wait()

        def rows(at):
            d_act_ref[at, :] = dot_nn(grad_ref[at, :], whole(w_ref)).astype(BF16)

        row_chunks(n_tok, 256, rows)

    return pl.pallas_call(
        body,
        name="down_back",
        out_shape=(
            jax.ShapeDtypeStruct((n_tok, cols), BF16),
            jax.ShapeDtypeStruct((*blk.shape, cols), BF16),
        ),
        in_specs=[SMEM_SPEC, VMEM_SPEC] + [ANY_SPEC] * n_in,
        out_specs=(VMEM_SPEC,) * 2,
        scratch_shapes=[pltpu.SemaphoreType.DMA],
        compiler_params=params(),
        cost_estimate=cost(2 * n_tok * width * cols, 1e7),
    )(index, grad_out, *arrays)


def gated(blk, masks, index, normed, d_act, gate_arrays, up_arrays, cols):
    n_tok, width = normed.shape
    n_in = len(gate_arrays)

    def body(index_ref, normed_ref, d_act_ref, *refs):
        gate_in, up_in = refs[:n_in], refs[n_in : 2 * n_in]
        act_ref, d_gate_ref, d_up_ref, wg_ref, wu_ref, sems = refs[2 * n_in :]
        start_all(blk.copies_in(index_ref[0], gate_in, masks, wg_ref, sems.at[0]))
        start_all(blk.copies_in(index_ref[0], up_in, masks, wu_ref, sems.at[1]))
        pltpu.make_async_copy(wg_ref, wg_ref, sems.at[0]).wait()
        pltpu.make_async_copy(wu_ref, wu_ref, sems.at[1]).wait()

        def rows(at):
            x = normed_ref[at, :]
            gate = dot_nn(x, whole(wg_ref))
            up = dot_nn(x, whole(wu_ref))
            sig = 1.0 / (1.0 + jnp.exp(-gate))
            silu = gate * sig
            act_ref[at, :] = (silu * up).astype(BF16)
            d = d_act_ref[at, :].astype(F32)
            d_gate_ref[at, :] = (d * up * sig * (1.0 + gate * (1.0 - sig))).astype(BF16)
            d_up_ref[at, :] = (d * silu).astype(BF16)

        row_chunks(n_tok, 256, rows)

    out = jax.ShapeDtypeStruct((n_tok, cols), BF16)
    w_out = jax.ShapeDtypeStruct((*blk.shape, cols), BF16)
    return pl.pallas_call(
        body,
        name="gated",
        out_shape=(out, out, out, w_out, w_out),
        in_specs=[SMEM_SPEC, VMEM_SPEC, VMEM_SPEC] + [ANY_SPEC] * (2 * n_in),
        out_specs=(VMEM_SPEC,) * 5,
        scratch_shapes=[pltpu.SemaphoreType.DMA((2,))],
        compiler_params=params(),
        cost_estimate=cost(4 * n_tok * width * cols, 2e7),
    )(index, normed, d_act, *gate_arrays, *up_arrays)


def weight_grad(blk, masks, index, lefts, rights, extra=None, name="weight_grad"):
    n_tok, width = lefts[0].shape
    sizes = [r.shape[1] for r in rights]
    cols = sum(sizes) + (LANES if extra is not None else 0)
    out_shapes = blk.out_shapes(masks, cols)
    n_out = len(out_shapes)
    n = len(lefts)
    chunk = 256

    def body(index_ref, *refs):
        left_refs, right_refs = refs[:n], refs[n : 2 * n]
        rest = refs[2 * n :]
        if extra is not None:
            extra_ref, rest = rest[0], rest[1:]
        outs, total_ref, sem = rest[:n_out], rest[n_out], rest[n_out + 1]
        per = chunk // blk.rows if blk.direct else 1

        def step(i, carry):
            at = pl.ds(pl.multiple_of(i * chunk, chunk), chunk)
            start = 0
            for left, right, size in zip(left_refs, right_refs, sizes):
                value = dot_tn(left[:, at], right[...]).astype(BF16)
                if blk.direct:
                    total_ref[pl.ds(i * per, per), :, start : start + size] = value.reshape(
                        per, blk.rows, size
                    )
                else:
                    total_ref[0, at, start : start + size] = value
                start += size
            return carry

        lax.fori_loop(0, width // chunk, step, 0)
        if extra is not None:
            value = jnp.concatenate(
                [extra_ref[...], jnp.zeros((LANES - extra_ref.shape[0], width), F32)], axis=0
            )
            value = value.T.astype(BF16)
            total_ref[:, :, cols - LANES :] = value.reshape(*blk.shape, LANES)
        copies = blk.copies_out(index_ref[0], total_ref, outs, masks, sem)
        start_all(copies)
        pltpu.make_async_copy(total_ref, total_ref, sem).wait()

    extras = [] if extra is None else [extra]
    return pl.pallas_call(
        body,
        name=name,
        out_shape=tuple(out_shapes),
        in_specs=[SMEM_SPEC] + [VMEM_SPEC] * (2 * n + len(extras)),
        out_specs=(ANY_SPEC,) * n_out,
        scratch_shapes=[pltpu.VMEM((*blk.shape, cols), BF16), pltpu.SemaphoreType.DMA],
        compiler_params=params(),
        cost_estimate=cost(2 * n_tok * width * cols, 1e7),
    )(index, *lefts, *rights, *extras)


def sum_nt(lefts, rights, name):
    n_tok = lefts[0].shape[0]
    width = rights[0].shape[0] * rights[0].shape[1]
    n = len(lefts)

    def body(*refs):
        left_refs, right_refs, out_ref = refs[:n], refs[n : 2 * n], refs[2 * n]

        def rows(at):
            total = dot_nt(left_refs[0][at, :], whole(right_refs[0]))
            for left, right in zip(left_refs[1:], right_refs[1:]):
                total = total + dot_nt(left[at, :], whole(right))
            out_ref[at, :] = total.astype(BF16)

        row_chunks(n_tok, 256, rows)

    return pl.pallas_call(
        body,
        name=name,
        out_shape=jax.ShapeDtypeStruct((n_tok, width), BF16),
        in_specs=[VMEM_SPEC] * (2 * n),
        out_specs=VMEM_SPEC,
        compiler_params=params(),
        cost_estimate=cost(2 * n_tok * width * sum(x.shape[1] for x in lefts), 1e7),
    )(*lefts, *rights)


def norm_back(part, came, hres, grad_out, gains, w0, dims):
    n_tok, width = hres.shape
    half = n_tok // 2
    nq, nv, _ = dims
    n_qkv = 2 * nq + nv

    def body(part_ref, came_ref, hres_ref, c_ref, gain_ref, w_ref, dh_ref, do_ref, dy_ref, gg_ref):
        gain = gain_ref[1:2, :]
        gg_ref[...] = jnp.zeros_like(gg_ref)
        size = 256

        def rows(at, other, own):
            d = part_ref[at, :].astype(F32) + came_ref[other, :].astype(F32)
            h = hres_ref[at, :]
            inverse = lax.rsqrt(jnp.mean(h * h, axis=-1, keepdims=True) + EPS)
            hr = h * inverse
            gg_ref[...] += jnp.sum((d * hr).reshape(-1, 8, width), axis=0)
            dg = d * gain
            back = inverse * (dg - hr * jnp.mean(dg * hr, axis=-1, keepdims=True))
            dh = c_ref[at, :].astype(F32) + back
            if own:
                dh_ref[at, :] = dh
            low = dh.astype(BF16)
            do_ref[at, :] = low
            w = w_ref[:, :, n_qkv : n_qkv + nv].reshape(width, nv)
            dy_ref[at, :] = dot_nn(low, w).astype(BF16)

        def step(i, carry):
            lo = pl.ds(pl.multiple_of(i * size, size), size)
            hi = pl.ds(pl.multiple_of(half + i * size, size), size)
            rows(lo, hi, True)
            rows(hi, lo, False)
            return carry

        lax.fori_loop(0, half // size, step, 0)

    out = lambda *s, t=BF16: jax.ShapeDtypeStruct(s, t)
    return pl.pallas_call(
        body,
        name="norm_back",
        out_shape=(out(half, width, t=F32), out(n_tok, width), out(n_tok, nv), out(8, width, t=F32)),
        in_specs=[VMEM_SPEC] * 6,
        out_specs=(VMEM_SPEC,) * 4,
        compiler_params=params(),
        cost_estimate=cost(2 * n_tok * width * nv, 1.4e7),
    )(part, came, hres, grad_out, gains, w0)


def attn_bwd(seq, qkv, y, dy, dinv, dims):
    n_tok, buffers = qkv.shape[0], seq.shape[0]
    length = n_tok // buffers
    nq, nv, _ = dims

    def body(seq_ref, qkv_ref, y_ref, dy_ref, dinv_ref, out_ref, mask_ref, dq_acc, dk_acc, dv_acc):
        for b in range(buffers):
            make_mask(seq_ref, b, mask_ref)
            base = b * length
            dq_acc[...] = jnp.zeros_like(dq_acc)
            dk_acc[...] = jnp.zeros_like(dk_acc)

            def pair(hp, carry):
                lane = lax.broadcasted_iota(jnp.int32, (1, LANES), 1)
                zero = jnp.zeros((), BF16)
                k = qkv_ref[base : base + length, nq : 2 * nq]
                v_at = pl.ds(pl.multiple_of(2 * nq + hp * LANES, LANES), LANES)
                y_at = pl.ds(pl.multiple_of(hp * LANES, LANES), LANES)
                v = qkv_ref[base : base + length, v_at]
                dv_acc[...] = jnp.zeros_like(dv_acc)
                step = length // 2
                for tb in range(2):
                    rows = slice(base + tb * step, base + (tb + 1) * step)
                    here = slice(tb * step, (tb + 1) * step)
                    seen = (tb + 1) * step
                    q = qkv_ref[rows, :nq] * jnp.asarray(0.25, BF16)
                    mask = mask_ref[here, :seen]
                    dyn = dy_ref[rows, y_at].astype(F32) * dinv_ref[rows, y_at]
                    dot_y = dyn * y_ref[rows, y_at].astype(F32)
                    dyn = dyn.astype(BF16)
                    for j in range(2):
                        mine = lane // F == 2 * hp + j
                        side = lane // 64 == j
                        k_h = jnp.where(mine, k[:seen], zero)
                        v_h = jnp.where(side, v[:seen], zero)
                        one = dot_nt(q, k_h) + 1.0
                        half_one = one * mask
                        weights = (half_one * one + mask).astype(BF16)
                        d_p = dot_nt(dyn, v_h)
                        shift = jnp.sum(jnp.where(side, dot_y, 0.0), axis=-1, keepdims=True)
                        d_a = ((d_p - shift) * half_one).astype(BF16)
                        dv_acc[:seen, :] += dot_tn(weights, jnp.where(side, dyn, zero))
                        dq_acc[here, :] += dot_nn(d_a, k_h)
                        dk_acc[:seen, :] += dot_tn(d_a, jnp.where(mine, q, zero))
                out_ref[base : base + length, v_at] = dv_acc[...].astype(BF16)
                return carry

            lax.fori_loop(0, nv // LANES, pair, 0)
            out_ref[base : base + length, :nq] = (dq_acc[...] * 0.5).astype(BF16)
            out_ref[base : base + length, nq : 2 * nq] = (dk_acc[...] * 2.0).astype(BF16)

    return pl.pallas_call(
        body,
        name="attn_bwd",
        out_shape=jax.ShapeDtypeStruct(qkv.shape, BF16),
        in_specs=[SMEM_SPEC] + [VMEM_SPEC] * 4,
        out_specs=VMEM_SPEC,
        scratch_shapes=[
            pltpu.VMEM((length, length), F32),
            pltpu.VMEM((length, nq), F32),
            pltpu.VMEM((length, nq), F32),
            pltpu.VMEM((length, LANES), F32),
        ],
        compiler_params=params(),
        cost_estimate=cost(2e10, 6e6),
    )(seq, qkv, y, dy, dinv)


def norm_one_part(d_qkv, w0, tok, dims):
    n_tok, width = tok.shape
    nq, nv, _ = dims
    n_qkv = 2 * nq + nv

    def body(d_ref, w_ref, tok_ref, out_ref, gg_ref):
        gg_ref[...] = jnp.zeros_like(gg_ref)

        def rows(at):
            d = dot_nt(d_ref[at, :], w_ref[:, :, :n_qkv].reshape(width, n_qkv))
            out_ref[at, :] = d.astype(BF16)
            x = tok_ref[at, :].astype(F32)
            inverse = lax.rsqrt(jnp.mean(x * x, axis=-1, keepdims=True) + EPS)
            gg_ref[...] += jnp.sum((d * (x * inverse)).reshape(-1, 8, width), axis=0)

        row_chunks(n_tok, 256, rows)

    return pl.pallas_call(
        body,
        name="norm_one_part",
        out_shape=(
            jax.ShapeDtypeStruct((n_tok, width), BF16),
            jax.ShapeDtypeStruct((8, width), F32),
        ),
        in_specs=[VMEM_SPEC] * 3,
        out_specs=(VMEM_SPEC,) * 2,
        compiler_params=params(),
        cost_estimate=cost(2 * n_tok * width * n_qkv, 8e6),
    )(d_qkv, w0, tok)


def finish(part, came, tok, dh, gains, hres, out_part, out_came):
    rows_all, width = tok.shape

    def body(part_ref, came_ref, tok_ref, dh_ref, gain_ref, h_ref, op_ref, oc_ref, grad_ref, out_ref):
        gain = gain_ref[0:1, :]

        def rows(at):
            d = (part_ref[at, :].astype(F32) + came_ref[at, :].astype(F32)) * gain
            x = tok_ref[at, :].astype(F32)
            inverse = lax.rsqrt(jnp.mean(x * x, axis=-1, keepdims=True) + EPS)
            xr = x * inverse
            back = inverse * (d - xr * jnp.mean(d * xr, axis=-1, keepdims=True))
            grad_ref[at, :] = (dh_ref[at, :] + back).astype(BF16)
            both = op_ref[at, :].astype(F32) + oc_ref[at, :].astype(F32)
            out_ref[at, :] = (h_ref[at, :] + both).astype(BF16)

        row_chunks(rows_all, 128, rows)

    top = pl.BlockSpec((rows_all, width), lambda i: (0, 0))
    out = jax.ShapeDtypeStruct((rows_all, width), BF16)
    return pl.pallas_call(
        body,
        name="finish",
        grid=(1,),
        out_shape=(out, out),
        in_specs=[top, top, top, top, pl.BlockSpec((8, width), lambda i: (0, 0)), top, top, top],
        out_specs=(top, top),
        compiler_params=params(),
        cost_estimate=cost(1e7, 1e7),
    )(part, came, tok, dh, gains, hres, out_part, out_came)


def local(
    lay,
    tokens,
    seq_lengths,
    w_query,
    w_key,
    w_value,
    w_output,
    w_gate,
    w_up,
    w_down,
    gain_attn,
    gain_mlp,
    cotangent,
):
    me = lax.axis_index(AXES).astype(jnp.int32)
    core = me % 2
    index = me.reshape(1)
    rows, length = w_query.shape[0], tokens.shape[0]
    nq, nv, nf = w_query.shape[1] // 2, w_value.shape[1] // 2, w_gate.shape[1] // 2

    def halves(w):
        n = w.shape[1] // 2
        low, high = w[:, :n], w[:, n:]
        return jnp.where(core == 0, low, high), jnp.where(core == 0, high, low)

    def split_gain(g):
        high = lax.reduce_precision(g, 8, 7)
        return [high.astype(BF16)[:, None], (g - high).astype(BF16)[:, None]]

    gain_cols = split_gain(gain_attn) + split_gain(gain_mlp)
    gain_block = jnp.concatenate(gain_cols + [jnp.zeros((rows, LANES - 4), BF16)], axis=1)
    parts = [halves(w) for w in (w_query, w_key, w_value, w_output.T)]
    mine0 = jnp.concatenate([p[0] for p in parts] + [gain_block], axis=1)
    give0 = jnp.concatenate([p[1] for p in parts] + [gain_block], axis=1)
    other0 = lay.swap(give0, 1)
    ffn = [halves(w) for w in (w_down.T, w_gate, w_up)]
    others = lay.swap(jnp.stack([p[1] for p in ffn]), 1)

    seq = jnp.concatenate([seq_lengths, lay.swap(seq_lengths, 1)], axis=0)
    tok = jnp.concatenate([tokens, lay.swap(tokens, 1)], axis=0)
    grad_out = jnp.concatenate([cotangent, lay.swap(cotangent, 1)], axis=0)

    blk = Blocks(lay, rows)
    pieces0 = gather(lay, mine0, other0)
    pieces_d = gather(lay, ffn[0][0], others[0])
    pieces_g = gather(lay, ffn[1][0], others[1])
    pieces_u = gather(lay, ffn[2][0], others[2])
    in_masks = [m for _, m in pieces0]
    dims = (nq, nv, mine0.shape[1])

    normed_one, qkv, y, dinv, part_o, gains, w0 = attn_fwd(
        blk, in_masks, index, seq, tok, blk.arrays(pieces0, me), dims
    )
    came_o = lay.swap(part_o, 1)
    d_act, w_d = down_back(blk, in_masks, index, grad_out, blk.arrays(pieces_d, me), nf)
    hres, normed_two = residual(tok, part_o, came_o, gains)
    act, d_gate, d_up, w_g, w_u = gated(
        blk, in_masks, index, normed_two, d_act, blk.arrays(pieces_g, me), blk.arrays(pieces_u, me), nf
    )

    out_masks = scatter_masks(lay)

    def reduced(lefts, rights, extra=None, name="weight_grad"):
        outs = weight_grad(blk, out_masks, index, lefts, rights, extra, name)
        return reduce_blocks(lay, blk.split(outs, out_masks, me))

    sum_g = reduced([normed_two], [d_gate], name="grad_gate")
    part_n2 = sum_nt([d_gate, d_up], [w_g, w_u], "d_norm2")
    came_n2 = lay.swap(part_n2, 1)
    sum_u = reduced([normed_two], [d_up], name="grad_up")
    sum_d = reduced([grad_out], [act], name="grad_down")
    d_h, d_o, d_y, gg_mlp = norm_back(part_n2, came_n2, hres, grad_out, gains, w0, dims)
    part_out = sum_nt([act], [w_d], "down")
    came_out = lay.swap(part_out[length:], 1)
    d_qkv = attn_bwd(seq, qkv, y, d_y, dinv, dims)
    part_n1, gg_attn = norm_one_part(d_qkv, w0, tok, dims)
    came_n1 = lay.swap(part_n1[length:], 1)
    gg = jnp.stack([jnp.sum(gg_attn, axis=0), jnp.sum(gg_mlp, axis=0)] + [jnp.zeros_like(gg_mlp[0])] * 6)
    sum_0 = reduced([normed_one, d_o], [d_qkv, y], gg, name="grad_attn")
    grad_tokens, layer_out = finish(part_n1, came_n1, tokens, d_h, gains, hres, part_out, came_out)

    sums = [sum_0, sum_d, sum_g, sum_u]
    came = lay.swap(jnp.concatenate([s[1] for s in sums], axis=1), 1)
    mine = jnp.concatenate([s[0] for s in sums], axis=1)

    def joined(start, size):
        own, other = mine[:, start : start + size], came[:, start : start + size]
        return jnp.where(
            core == 0,
            jnp.concatenate([own, other], axis=1),
            jnp.concatenate([other, own], axis=1),
        )

    at = 2 * nq + 2 * nv
    base = at + LANES
    return (
        layer_out,
        grad_tokens,
        joined(0, nq),
        joined(nq, nq),
        joined(2 * nq, nv),
        joined(2 * nq + nv, nv).T,
        joined(base + nf, nf),
        joined(base + 2 * nf, nf),
        joined(base, nf).T,
        mine[:, at] + came[:, at],
        mine[:, at + 1],
    )


def solution(mesh):
    rows, cols, flat = P(AXES, None), P(None, AXES), P(AXES)
    return jax.shard_map(
        functools.partial(local, Layout(mesh)),
        mesh=mesh,
        in_specs=(rows, rows, rows, rows, rows, cols, rows, rows, cols, flat, flat, rows),
        out_specs=(rows, rows, rows, rows, rows, cols, rows, rows, cols, flat, flat),
        check_vma=False,
    )
```

```python
import functools
import math

import jax
import jax.numpy as jnp
from jax import lax
from jax.experimental import pallas as pl
from jax.experimental.pallas import tpu as pltpu
from jax.sharding import PartitionSpec as P

H = 16
F = 16
EPS = 1e-05
AXES = ("dp", "fsdp")
LANES = 128
F32 = jnp.float32
BF16 = jnp.bfloat16

VMEM_SPEC = pl.BlockSpec(memory_space=pltpu.VMEM)
SMEM_SPEC = pl.BlockSpec(memory_space=pltpu.SMEM)
ANY_SPEC = pl.BlockSpec(memory_space=pl.ANY)


def dot_nn(a, b):
    return lax.dot_general(a, b, (((1,), (0,)), ((), ())), preferred_element_type=F32)


def dot_nt(a, b):
    return lax.dot_general(a, b, (((1,), (1,)), ((), ())), preferred_element_type=F32)


def dot_tn(a, b):
    return lax.dot_general(a, b, (((0,), (0,)), ((), ())), preferred_element_type=F32)


class Layout:
    def __init__(self, mesh):
        dp, fsdp = mesh.shape["dp"], mesh.shape["fsdp"]
        self.count = dp * fsdp
        x_bits = int(math.log2(fsdp)) - 1
        y_bits = int(math.log2(dp)) // 3
        all_bits = int(math.log2(self.count))
        self.x = [1 << (1 + i) for i in range(x_bits)]
        self.y = [1 << (1 + x_bits + i) for i in range(y_bits)]
        self.z = [1 << i for i in range(1 + x_bits + y_bits, all_bits)]

    def swap(self, value, bit):
        return lax.ppermute(value, AXES, [(i, i ^ bit) for i in range(self.count)])


def masks_of(bits):
    masks = [0]
    for bit in bits:
        masks = masks + [m | bit for m in masks]
    return masks


class Order:
    def __init__(self):
        self.last = None

    def __call__(self, *values):
        held = values if self.last is None else (*values, self.last)
        held = lax.optimization_barrier(held)
        self.last = held[0]
        return held[: len(values)] if len(values) > 1 else held[0]


def behind(value, order=None):
    return value if order is None else order(value)


def plane_masks(lay, base):
    found = []
    for half, bits in enumerate((lay.x + lay.y, lay.y + lay.x)):
        masks = [m | half for m in base]
        for bit in bits:
            masks = masks + [m | bit for m in masks]
        found.append(masks)
    return found


def split_masks(lay):
    return [
        part
        for masks in plane_masks(lay, masks_of(lay.z))
        for part in (masks[: len(masks) // 2], masks[len(masks) // 2 :])
    ]


class GatherZ:
    def __init__(self, lay, block):
        self.lay = lay
        self.bits = list(reversed(lay.z))
        self.found = {0: block}

    def first(self, *order):
        bit = self.bits[0]
        self.found[bit] = self.lay.swap(behind(self.found[0], *order), bit)

    def second(self, *order):
        for bit in self.bits[1:]:
            self.found[bit] = self.lay.swap(behind(self.found[0], *order), bit)

    def third(self, order, everything=False):
        if everything:
            for bit, value in zip(self.bits, order(*[self.found[bit] for bit in self.bits])):
                self.found[bit] = value
        else:
            self.found[self.bits[0]] = order(self.found[self.bits[0]])
        for i, bit in enumerate(self.bits[1:], 1):
            for m in masks_of(self.bits[:i])[1:]:
                self.found[m | bit] = self.lay.swap(self.found[m], bit)

    def done(self, order):
        masks = masks_of(self.lay.z)
        return order(*[self.found[m] for m in masks])


class GatherPlane:
    def __init__(self, lay, keep, other):
        self.lay, self.keep, self.other = lay, keep, other
        self.orders = (lay.x + lay.y, lay.y + lay.x)
        self.came = [lay.swap(h, bits[0]) for h, bits in zip((keep, other), self.orders)]

    def second(self, order):
        came = order(*self.came)
        self.held, self.came = [], []
        for held, got, bits in zip((self.keep, self.other), came, self.orders):
            held = jnp.concatenate([held, got], axis=0)
            for bit in bits[1:-1]:
                held = jnp.concatenate([held, self.lay.swap(held, bit)], axis=0)
            self.held.append(held)
            self.came.append(self.lay.swap(held, bits[-1]))

    def arrays(self):
        return [self.held[0], self.came[0], self.held[1], self.came[1]]

    def joined(self, order):
        came = order(*self.came)
        return jnp.concatenate([self.held[0], came[0], self.held[1], came[1]], axis=0)


def add_low(a, b):
    return (a.astype(F32) + b.astype(F32)).astype(BF16)


def fold(pairs, name="fold"):
    n = len(pairs)

    def body(*refs):
        ins, outs = refs[: 2 * n], refs[2 * n :]
        step = pl.program_id(0)
        for i in range(n):
            value = add_low(ins[2 * i][...], ins[2 * i + 1][...])

            def put(ref, value=value):
                ref[...] = value

            pl.when(step == 0)(functools.partial(put, outs[2 * i + 1]))
            pl.when(step == 1)(functools.partial(put, outs[2 * i]))

    def half(a):
        return (a.shape[0] // 2, *a.shape[1:])

    def spec(a, there):
        rest = (0,) * (a.ndim - 1)
        return pl.BlockSpec(half(a), (lambda i: (1 - i, *rest)) if there else (lambda i: (0, *rest)))

    flat = [a for pair in pairs for a in pair]
    outs = pl.pallas_call(
        body,
        name=name,
        grid=(2,),
        out_shape=tuple(jax.ShapeDtypeStruct(half(a), BF16) for a in flat),
        in_specs=[spec(a, True) for a in flat],
        out_specs=tuple(spec(a, False) for a in flat),
        compiler_params=params(FOLD_MEGABYTES),
        cost_estimate=cost(name),
    )(*flat)
    return [(outs[2 * i], outs[2 * i + 1]) for i in range(n)]


def fold_plane(pairs, wanted):
    shape = (len(wanted) // 2, 2, *pairs[0][0].shape[1:])
    n = shape[0]

    def body(*refs):
        ins, outs = refs[:4], refs[4:]
        for place, i in enumerate(wanted):
            for h in range(2):
                outs[place // n][place % n, h] = add_low(ins[2 * h][i], ins[2 * h + 1][i])

    return pl.pallas_call(
        body,
        name="fold_plane",
        out_shape=(jax.ShapeDtypeStruct(shape, BF16),) * 2,
        in_specs=[VMEM_SPEC] * 4,
        out_specs=(VMEM_SPEC,) * 2,
        compiler_params=params(FOLD_MEGABYTES),
        cost_estimate=cost("fold_plane"),
    )(*[a for pair in pairs for a in pair])


class ReducePlane:
    def __init__(self, lay, arrays):
        self.lay = lay
        self.kept = [arrays[0], arrays[2]]
        self.orders = (lay.x + lay.y, lay.y + lay.x)
        self.came = [lay.swap(a, bits[-1]) for a, bits in zip(arrays[1::2], self.orders)]

    def second(self, order):
        for level in reversed(range(len(self.orders[0]) - 1)):
            came = order(*self.came)
            found = fold(list(zip(self.kept, came)))
            self.kept = [kept for kept, _ in found]
            self.came = [
                self.lay.swap(sent, bits[level]) for (_, sent), bits in zip(found, self.orders)
            ]

    def pairs(self, order):
        return list(zip(self.kept, order(*self.came)))


class ReduceZ:
    def __init__(self, lay, kept, sent):
        self.lay = lay
        self.bits = list(lay.z)
        self.kept = kept
        self.came = lay.swap(sent, self.bits[0])

    def second(self, order):
        while len(self.bits) > 1:
            self.bits.pop(0)
            ((self.kept, sent),) = fold([(self.kept, order(self.came))], "fold_z")
            self.came = self.lay.swap(sent, self.bits[0])

    def last(self, order):
        return self.kept, order(self.came)


def add_up(ends):
    rows = ends[0][0].shape[2]
    cols = sum(kept.shape[3] for kept, _ in ends)

    def body(*refs):
        at = 0
        for i, (kept, _) in enumerate(ends):
            width = kept.shape[3]
            total = refs[2 * i][0].astype(F32) + refs[2 * i + 1][0].astype(F32)
            refs[-2][:, at : at + width] = total[0]
            refs[-1][:, at : at + width] = total[1]
            at += width

    return pl.pallas_call(
        body,
        name="add_up",
        out_shape=(jax.ShapeDtypeStruct((rows, cols), F32),) * 2,
        in_specs=[VMEM_SPEC] * (2 * len(ends)),
        out_specs=(VMEM_SPEC,) * 2,
        compiler_params=params(FOLD_MEGABYTES),
        cost_estimate=cost("add_up"),
    )(*[a for end in ends for a in end])


def wait_for(order, *streams):
    values = [v for s in streams for v in (s.came if isinstance(s.came, list) else [s.came])]
    values = list(order(*values))
    for s in streams:
        if isinstance(s.came, list):
            s.came = [values.pop(0) for _ in s.came]
        else:
            s.came = values.pop(0)


def low_first(lay):
    bits = lay.z
    masks = [0]
    for bit in reversed(bits):
        masks = masks + [m | bit for m in masks]
    return masks


class Blocks:
    def __init__(self, lay, rows):
        self.lay = lay
        self.rows = rows
        self.direct = rows % 16 == 0
        self.shape = (lay.count, rows) if self.direct else (1, lay.count * rows)

    def order(self, index):
        return jnp.bitwise_xor(index, jnp.arange(self.lay.count))

    def arrays(self, arrays, masks, index):
        if self.direct:
            return arrays
        masks = [m for ms in masks for m in ms]
        whole = jnp.concatenate(arrays, axis=0)
        place = [0] * len(masks)
        for i, m in enumerate(masks):
            place[m] = i
        whole = jnp.take(whole, jnp.asarray(place)[self.order(index)], axis=0)
        return [whole.reshape(1, -1, whole.shape[-1])]

    def copies_in(self, index, refs, masks, out_ref, sem, start, cols):
        at = pl.ds(start, cols)
        if not self.direct:
            return [pltpu.make_async_copy(refs[0].at[:, :, at], out_ref, sem)]
        return [
            pltpu.make_async_copy(
                ref.at[i, :, at], out_ref.at[jnp.bitwise_xor(index, m)], sem
            )
            for ref, ms in zip(refs, masks)
            for i, m in enumerate(ms)
        ]

    def out_shapes(self, masks, columns):
        if self.direct:
            return [jax.ShapeDtypeStruct((len(m), self.rows, columns), BF16) for m in masks]
        return [jax.ShapeDtypeStruct((1, self.lay.count * self.rows, columns), BF16)]

    def copies_out(self, index, in_ref, refs, masks, sem):
        if not self.direct:
            return [pltpu.make_async_copy(in_ref, refs[0], sem)]
        return [
            pltpu.make_async_copy(
                in_ref.at[jnp.bitwise_xor(index, m)], ref.at[i], sem
            )
            for ref, ms in zip(refs, masks)
            for i, m in enumerate(ms)
        ]

    def split(self, outs, masks, index):
        if self.direct:
            return outs
        whole = outs[0].reshape(self.lay.count, self.rows, -1)
        whole = jnp.take(whole, self.order(index), axis=0)
        return [jnp.take(whole, jnp.asarray(m), axis=0) for m in masks]


def start_all(copies):
    for copy in copies:
        copy.start()


WEIGHTS = {}
FOLD_MEGABYTES = 60


def cost(name):
    return pl.CostEstimate(
        flops=int(WEIGHTS.get(name, 0) * 1e9) + 1, bytes_accessed=1, transcendentals=0
    )


def params(megabytes):
    return pltpu.CompilerParams(vmem_limit_bytes=megabytes << 20)


def rows_spec(size, cols, last=None):
    return pl.BlockSpec((size, cols), lambda i: (i if last is None else jnp.minimum(i, last), 0))


def piece_of(i, pieces, steps, turn):
    block = lax.rem(i + steps // 2, steps) if turn else i
    return block // (steps // pieces), lax.rem(block, steps // pieces)


def piece_specs(pieces, steps, size, width, turn=False):
    def spec(q):
        def at(i):
            piece, block = piece_of(i, pieces, steps, turn)
            last = steps // pieces - 1
            return (jnp.where(piece == q, block, jnp.where(piece < q, 0, last)), 0)

        return pl.BlockSpec((size, width), at)

    return [spec(q) for q in range(pieces)]


def with_piece(refs, steps, body, turn=False):
    piece, _ = piece_of(pl.program_id(0), len(refs), steps, turn)
    for q, ref in enumerate(refs):
        pl.when(piece == q)(functools.partial(body, ref))


def row_chunks(total, size, body):
    def step(i, carry):
        body(pl.ds(pl.multiple_of(i * size, size), size))
        return carry

    lax.fori_loop(0, total // size, step, 0)


def make_mask(seq_ref, b, mask_ref):
    rows, cols = mask_ref.shape
    slots = seq_ref.shape[1]
    ends = []
    total = jnp.int32(0)
    for j in range(slots):
        total = total + seq_ref[b, j]
        ends.append(total)

    def body(at):
        t = lax.broadcasted_iota(jnp.int32, (at.size, cols), 0) + at.start
        s = lax.broadcasted_iota(jnp.int32, (at.size, cols), 1)
        seg_t = jnp.zeros_like(t)
        seg_s = jnp.zeros_like(s)
        for e in ends:
            seg_t = seg_t + (t >= e).astype(jnp.int32)
            seg_s = seg_s + (s >= e).astype(jnp.int32)
        seen = (s <= t) & (seg_t == seg_s) & (t < total)
        mask_ref[at, :] = jnp.where(seen, 0.5, 0.0).astype(F32)

    row_chunks(rows, 64, body)
    return total


class Weights:
    def __init__(self, blk, arrays, masks, index):
        self.blk, self.masks = blk, masks
        self.arrays = blk.arrays(arrays, masks, index)
        self.count = len(self.arrays)
        self.specs = [ANY_SPEC] * self.count

    def scratch(self, cols):
        return [pltpu.VMEM((*self.blk.shape, cols), BF16), pltpu.SemaphoreType.DMA]

    def load(self, index_ref, refs, w_ref, sem, start=0):
        cols = w_ref.shape[-1]
        start_all(self.blk.copies_in(index_ref[0], refs, self.masks, w_ref, sem, start, cols))

    def wait(self, w_ref, sem):
        pltpu.make_async_copy(w_ref, w_ref, sem).wait()


def prepare(core, groups, gains):
    rows = groups[0][0].shape[0]
    flat = [w for group in groups for w in group]
    padded = [w.shape[1] // 2 + -(w.shape[1] // 2) % LANES for w in flat]
    n_in = len(flat)
    widths, at = [], 0
    for group in groups:
        widths.append(sum(padded[at : at + len(group)]))
        at += len(group)
    widths[0] += LANES

    def body(core_ref, one_ref, two_ref, *refs):
        ins, keeps, give_ref = refs[:n_in], refs[n_in:-1], refs[-1]
        first = core_ref[0] == 0
        place, start = 0, 0
        for number, (group, keep_ref) in enumerate(zip(groups, keeps)):
            at = 0
            for _ in group:
                value = ins[place][...]
                half = value.shape[1] // 2
                low, high = value[:, :half].astype(F32), value[:, half:].astype(F32)
                spare = padded[place] - half
                for ref, base, one, two in (
                    (keep_ref, 0, low, high),
                    (give_ref, start, high, low),
                ):
                    ref[:, base + at : base + at + half] = jnp.where(first, one, two).astype(BF16)
                    if spare:
                        zeros = jnp.zeros((rows, spare), BF16)
                        ref[:, base + at + half : base + at + half + spare] = zeros
                at += padded[place]
                place += 1
            if number == 0:
                lines = []
                for ref in (one_ref, two_ref):
                    gain = ref[...]
                    high = gain.astype(BF16).astype(F32)
                    lines += [high, gain - high]
                lines = jnp.concatenate(lines + [jnp.zeros((LANES - 4, rows), F32)], axis=0)
                turned = lines.T.astype(BF16)
                keep_ref[:, at : at + LANES] = turned
                give_ref[:, at : at + LANES] = turned
                at += LANES
            start += at

    out = [jax.ShapeDtypeStruct((rows, n), BF16) for n in [*widths, sum(widths)]]
    return pl.pallas_call(
        body,
        name="prepare",
        out_shape=tuple(out),
        in_specs=[SMEM_SPEC] + [VMEM_SPEC] * (n_in + 2),
        out_specs=(VMEM_SPEC,) * len(out),
        compiler_params=params(60),
    )(core, *[g[None] for g in gains], *flat)


def conclude(core, mine, came, places):
    rows = mine.shape[0]
    n = len(places) - 1

    def body(core_ref, mine_ref, came_ref, *refs):
        first = core_ref[0] == 0
        for (at, half), ref in zip(places[:n], refs):
            own, other = mine_ref[:, at : at + half], came_ref[:, at : at + half]
            ref[:, :half] = jnp.where(first, own, other)
            ref[:, half:] = jnp.where(first, other, own)
        at = places[n][0]
        own = mine_ref[:, at : at + LANES].T
        other = came_ref[:, at : at + LANES].T
        refs[n][...] = own[0:1] + other[0:1]
        refs[n + 1][...] = own[1:2]

    out = [jax.ShapeDtypeStruct((rows, 2 * half), F32) for _, half in places[:n]]
    out += [jax.ShapeDtypeStruct((1, rows), F32)] * 2
    return pl.pallas_call(
        body,
        name="conclude",
        out_shape=tuple(out),
        in_specs=[SMEM_SPEC, VMEM_SPEC, VMEM_SPEC],
        out_specs=(VMEM_SPEC,) * len(out),
        compiler_params=params(60),
    )(core, mine, came)


def attn_fwd(weights, index, seq, tok, dims):
    n_tok, width, buffers = tok.shape[0], tok.shape[1], seq.shape[0]
    length = n_tok // buffers
    nq, nv, cols = dims
    n_qkv = 2 * nq + nv
    n_in = weights.count

    def body(index_ref, seq_ref, tok_ref, *refs):
        w_in = refs[:n_in]
        normed_ref, qkv_ref, y_ref, dinv_ref, gain_ref = refs[n_in : n_in + 5]
        part_refs = refs[n_in + 5 : n_in + 5 + 2 * buffers]
        mask_ref, w_ref, sem = refs[n_in + 5 + 2 * buffers :]
        weights.load(index_ref, w_in, w_ref, sem)
        weights.wait(w_ref, sem)
        w_gain = w_ref[:, :, n_qkv + nv :].reshape(width, LANES).astype(F32).T
        gain_ref[0:1, :] = w_gain[0:1] + w_gain[1:2]
        gain_ref[1:2, :] = w_gain[2:3] + w_gain[3:4]
        gain_ref[2:8, :] = jnp.zeros((6, width), F32)
        gain = gain_ref[0:1, :]

        def project(at):
            x = tok_ref[at, :].astype(F32)
            inverse = lax.rsqrt(jnp.mean(x * x, axis=-1, keepdims=True) + EPS)
            normed = (x * inverse * gain).astype(BF16)
            normed_ref[at, :] = normed
            w = w_ref[:, :, :n_qkv].reshape(width, n_qkv)
            qkv_ref[at, :] = dot_nn(normed, w).astype(BF16)

        row_chunks(n_tok, 256, project)

        for b in range(buffers):
            total = make_mask(seq_ref, b, mask_ref)
            base = b * length

            def pair(hp, carry):
                lane = lax.broadcasted_iota(jnp.int32, (1, LANES), 1)
                k = qkv_ref[base : base + length, nq : 2 * nq]
                v_at = pl.ds(pl.multiple_of(2 * nq + hp * LANES, LANES), LANES)
                v = qkv_ref[base : base + length, v_at]
                step = length // 2
                for tb in range(2):
                    rows = slice(base + tb * step, base + (tb + 1) * step)
                    seen = (tb + 1) * step
                    q = qkv_ref[rows, :nq] * jnp.asarray(0.25, BF16)
                    mask = mask_ref[tb * step : (tb + 1) * step, :seen]
                    row = lax.broadcasted_iota(jnp.int32, (step, 1), 0) + tb * step
                    pad = (row >= total).astype(F32)
                    found = []
                    for j in range(2):
                        k_h = jnp.where(lane // F == 2 * hp + j, k[:seen], jnp.zeros((), BF16))
                        v_h = jnp.where(lane // 64 == j, v[:seen], jnp.ones((), BF16))
                        one = dot_nt(q, k_h) + 1.0
                        share = ((one * one + 1.0) * mask).astype(BF16)
                        mixed = dot_nn(share, v_h)
                        inverse = 1.0 / (pltpu.roll(mixed, 64, 1) + pad)
                        found.append((mixed * inverse, inverse))
                    low = lane < 64
                    y_at = pl.ds(pl.multiple_of(hp * LANES, LANES), LANES)
                    y_ref[rows, y_at] = jnp.where(low, found[0][0], found[1][0]).astype(BF16)
                    dinv_ref[rows, y_at] = jnp.where(low, found[0][1], found[1][1])
                return carry

            lax.fori_loop(0, nv // LANES, pair, 0)
            w = w_ref[:, :, n_qkv : n_qkv + nv].reshape(width, nv)
            part = dot_nt(y_ref[base : base + length, :], w).astype(BF16)
            part_refs[2 * b][...] = part[: length // 2]
            part_refs[2 * b + 1][...] = part[length // 2 :]

    out = lambda *s, t=BF16: jax.ShapeDtypeStruct(s, t)
    return pl.pallas_call(
        body,
        name="attn_fwd",
        out_shape=(
            out(n_tok, width),
            out(n_tok, n_qkv),
            out(n_tok, nv),
            out(n_tok, nv, t=F32),
            out(8, width, t=F32),
            *(out(length // 2, width) for _ in range(2 * buffers)),
        ),
        in_specs=[SMEM_SPEC, SMEM_SPEC, VMEM_SPEC] + weights.specs,
        out_specs=(VMEM_SPEC,) * (5 + 2 * buffers),
        scratch_shapes=[pltpu.VMEM((length, length), F32)] + weights.scratch(cols),
        compiler_params=params(60),
        cost_estimate=cost("attn_fwd"),
    )(index, seq, tok, *weights.arrays)


def residual(tok, part, came, gains):
    n_tok, width = tok.shape
    steps = 4
    size = n_tok // steps

    n = len(part)

    def body(tok_ref, *refs):
        part_refs, came_refs = refs[:n], refs[n : 2 * n]
        gain_ref, hres_ref, normed_ref = refs[2 * n :]
        gain = gain_ref[1:2, :]

        def rows(at, part_ref, came_ref):
            x = tok_ref[at, :].astype(F32)
            x = x + (part_ref[at, :].astype(F32) + came_ref[at, :].astype(F32))
            hres_ref[at, :] = x
            inverse = lax.rsqrt(jnp.mean(x * x, axis=-1, keepdims=True) + EPS)
            normed_ref[at, :] = (x * inverse * gain).astype(BF16)

        pairs = list(zip(part_refs, came_refs[n // 2 :] + came_refs[: n // 2]))
        with_piece(pairs, steps, lambda pair: row_chunks(size, 64, lambda at: rows(at, *pair)))

    at = rows_spec(size, width)
    return pl.pallas_call(
        body,
        name="residual",
        grid=(steps,),
        out_shape=(
            jax.ShapeDtypeStruct((n_tok, width), F32),
            jax.ShapeDtypeStruct((n_tok, width), BF16),
        ),
        in_specs=[at]
        + piece_specs(n, steps, size, width)
        + piece_specs(n, steps, size, width, True)
        + [pl.BlockSpec((8, width), lambda i: (0, 0))],
        out_specs=(at, at),
        compiler_params=params(60),
        cost_estimate=cost("residual"),
    )(tok, *part, *came, gains)


def down_back(weights, index, grad_out, cols):
    n_tok, width = grad_out.shape
    n_in = weights.count
    steps = 4
    size = n_tok // steps

    def body(index_ref, grad_ref, *refs):
        out_ref, w_ref, sem = refs[n_in:]

        @pl.when(pl.program_id(0) == 0)
        def _():
            weights.load(index_ref, refs[:n_in], w_ref, sem)
            weights.wait(w_ref, sem)

        w = w_ref[...].reshape(width, cols)
        out_ref[...] = dot_nn(grad_ref[...], w).astype(BF16)

    return pl.pallas_call(
        body,
        name="down_back",
        grid=(steps,),
        out_shape=jax.ShapeDtypeStruct((n_tok, cols), BF16),
        in_specs=[SMEM_SPEC, rows_spec(size, width)] + weights.specs,
        out_specs=rows_spec(size, cols),
        scratch_shapes=weights.scratch(cols),
        compiler_params=params(60),
        cost_estimate=cost("down_back"),
    )(index, grad_out, *weights.arrays)


def gated(weights, index, normed, d_act, stride):
    n_tok, width = normed.shape
    cols = d_act.shape[1]
    n_in = weights.count
    steps = 4
    size = n_tok // steps

    def body(index_ref, normed_ref, d_act_ref, *refs):
        act_ref, d_gate_ref, d_up_ref, w_ref, sem = refs[n_in:]

        @pl.when(pl.program_id(0) == 0)
        def _():
            weights.load(index_ref, refs[:n_in], w_ref, sem)
            weights.wait(w_ref, sem)

        x = normed_ref[...]
        gate = dot_nn(x, w_ref[:, :, :cols].reshape(width, cols))
        up = dot_nn(x, w_ref[:, :, stride : stride + cols].reshape(width, cols))
        sig = 1.0 / (1.0 + jnp.exp(-gate))
        silu = gate * sig
        act_ref[...] = (silu * up).astype(BF16)
        d = d_act_ref[...].astype(F32)
        d_gate_ref[...] = (d * up * sig * (1.0 + gate * (1.0 - sig))).astype(BF16)
        d_up_ref[...] = (d * silu).astype(BF16)

    out = jax.ShapeDtypeStruct((n_tok, cols), BF16)
    at = rows_spec(size, cols)
    return pl.pallas_call(
        body,
        name="gated",
        grid=(steps,),
        out_shape=(out, out, out),
        in_specs=[SMEM_SPEC, rows_spec(size, width), at] + weights.specs,
        out_specs=(at, at, at),
        scratch_shapes=weights.scratch(2 * stride),
        compiler_params=params(60),
        cost_estimate=cost("gated"),
    )(index, normed, d_act, *weights.arrays)


def weight_grad(blk, masks, index, lefts, rights, gain=None, name="weight_grad"):
    n_tok, width = lefts[0].shape
    sizes = [r.shape[1] for r in rights]
    cols = sum(sizes) + (LANES if gain is not None else 0)
    out_shapes = blk.out_shapes(masks, cols)
    n_out = len(out_shapes)
    n = len(lefts)
    chunk = 256

    extras, specs, scratch = [], [], []
    if gain is not None:
        weights, gains, other = gain
        extras = [gains, other, *weights.arrays]
        specs = [pl.BlockSpec((8, chunk), lambda i: (0, i))] * 2 + weights.specs
        scratch = weights.scratch(sizes[0])

    def body(index_ref, *refs):
        left_refs, right_refs = refs[:n], refs[n : 2 * n]
        ins = refs[2 * n : 2 * n + len(extras)]
        outs, total_ref, sem = (*refs[2 * n + len(extras) :],)[:n_out], refs[-2 - len(scratch)], refs[-1 - len(scratch)]
        per = chunk // blk.rows if blk.direct else 1
        i = pl.program_id(0)

        def put(value, start):
            size = value.shape[1]
            if blk.direct:
                total_ref[pl.ds(i * per, per), :, start : start + size] = value.reshape(
                    per, blk.rows, size
                )
            else:
                at = pl.ds(pl.multiple_of(i * chunk, chunk), chunk)
                total_ref[0, at, start : start + size] = value

        if gain is not None:
            w_ref, w_sem = refs[-2], refs[-1]

            @pl.when(i == 0)
            def _():
                weights.load(index_ref, ins[2:], w_ref, w_sem)
                weights.wait(w_ref, w_sem)

        start = 0
        for left, right, size in zip(left_refs, right_refs, sizes):
            value = dot_tn(left[...], right[...])
            put(value.astype(BF16), start)
            if gain is not None and start == 0:
                if blk.direct:
                    w = w_ref[pl.ds(i * per, per), :, :].reshape(chunk, size)
                else:
                    w = w_ref[0, pl.ds(pl.multiple_of(i * chunk, chunk), chunk), :]
                one = jnp.sum(value * w.astype(F32), axis=-1, keepdims=True)
                two = jnp.sum(ins[1][...], axis=0, keepdims=True)
                rows = jnp.concatenate([ins[0][0:1, :], two, jnp.zeros((LANES - 2, chunk), F32)])
                turned = rows.T
                lane = lax.broadcasted_iota(jnp.int32, turned.shape, 1)
                put(jnp.where(lane == 0, one / turned, turned).astype(BF16), cols - LANES)
            start += size

        @pl.when(i == width // chunk - 1)
        def _():
            start_all(blk.copies_out(index_ref[0], total_ref, outs, masks, sem))
            pltpu.make_async_copy(total_ref, total_ref, sem).wait()

    return pl.pallas_call(
        body,
        name=name,
        grid=(width // chunk,),
        out_shape=tuple(out_shapes),
        in_specs=[SMEM_SPEC]
        + [pl.BlockSpec((n_tok, chunk), lambda i: (0, i))] * n
        + [pl.BlockSpec(r.shape, lambda i: (0, 0)) for r in rights]
        + specs,
        out_specs=(ANY_SPEC,) * n_out,
        scratch_shapes=[pltpu.VMEM((*blk.shape, cols), BF16), pltpu.SemaphoreType.DMA] + scratch,
        compiler_params=params(60),
        cost_estimate=cost(name),
    )(index, *lefts, *rights, *extras)


def sum_nt(weights, index, lefts, starts, total, pieces, name, base=0):
    n_tok, cols = lefts[0].shape
    width = weights.blk.shape[0] * weights.blk.shape[1]
    n, n_in = len(lefts), weights.count
    steps = 4
    size = n_tok // steps

    def body(index_ref, *refs):
        left_refs = refs[:n]
        out_refs, (w_ref, sem) = refs[n + n_in : -2], refs[-2:]

        @pl.when(pl.program_id(0) == 0)
        def _():
            weights.load(index_ref, refs[n : n + n_in], w_ref, sem, base)
            weights.wait(w_ref, sem)

        value = None
        for left, start in zip(left_refs, starts):
            term = dot_nt(left[...], w_ref[:, :, start : start + cols].reshape(width, cols))
            value = term if value is None else value + term
        value = value.astype(BF16)

        def put(ref):
            ref[...] = value

        with_piece(out_refs, steps, put)

    return pl.pallas_call(
        body,
        name=name,
        grid=(steps,),
        out_shape=(jax.ShapeDtypeStruct((n_tok // pieces, width), BF16),) * pieces,
        in_specs=[SMEM_SPEC] + [rows_spec(size, cols)] * n + weights.specs,
        out_specs=tuple(piece_specs(pieces, steps, size, width)),
        scratch_shapes=weights.scratch(total),
        compiler_params=params(60),
        cost_estimate=cost(name),
    )(index, *lefts, *weights.arrays)


def norm_back(weights, index, part, came, hres, grad_out, gains, dims):
    n_tok, width = hres.shape
    nq, nv, _ = dims
    n_qkv = 2 * nq + nv
    n_in = weights.count
    steps = 4
    size = n_tok // steps

    n = len(part)

    def body(index_ref, hres_ref, c_ref, gain_ref, *refs):
        part_refs, came_refs, refs = refs[:n], refs[n : 2 * n], refs[2 * n :]
        dh_ref, do_ref, dy_ref, gg_ref, w_ref, sem = refs[n_in:]
        gain = gain_ref[1:2, :]
        i = pl.program_id(0)

        @pl.when(i == 0)
        def _():
            weights.load(index_ref, refs[:n_in], w_ref, sem, n_qkv)
            gg_ref[...] = jnp.zeros_like(gg_ref)

        def rows(at, part_ref, came_ref):
            d = part_ref[at, :].astype(F32) + came_ref[at, :].astype(F32)
            h = hres_ref[at, :]
            inverse = lax.rsqrt(jnp.mean(h * h, axis=-1, keepdims=True) + EPS)
            hr = h * inverse
            gg_ref[...] += jnp.sum((d * hr).reshape(-1, 8, width), axis=0)
            dg = d * gain
            back = inverse * (dg - hr * jnp.mean(dg * hr, axis=-1, keepdims=True))
            dh = c_ref[at, :].astype(F32) + back

            @pl.when(i < steps // 2)
            def _():
                dh_ref[at, :] = dh

            do_ref[at, :] = dh.astype(BF16)

        pairs = list(zip(part_refs, came_refs[n // 2 :] + came_refs[: n // 2]))
        with_piece(pairs, steps, lambda pair: row_chunks(size, 64, lambda at: rows(at, *pair)))

        @pl.when(i == 0)
        def _():
            weights.wait(w_ref, sem)

        dy_ref[...] = dot_nn(do_ref[...], w_ref[...].reshape(width, nv)).astype(BF16)

    out = lambda *s, t=BF16: jax.ShapeDtypeStruct(s, t)
    at = rows_spec(size, width)
    keep = pl.BlockSpec((8, width), lambda i: (0, 0))
    return pl.pallas_call(
        body,
        name="norm_back",
        grid=(steps,),
        out_shape=(
            out(n_tok // 2, width, t=F32),
            out(n_tok, width),
            out(n_tok, nv),
            out(8, width, t=F32),
        ),
        in_specs=[SMEM_SPEC, at, at, keep]
        + piece_specs(n, steps, size, width)
        + piece_specs(n, steps, size, width, True)
        + weights.specs,
        out_specs=(
            rows_spec(size, width, last=steps // 2 - 1),
            at,
            rows_spec(size, nv),
            keep,
        ),
        scratch_shapes=weights.scratch(nv),
        compiler_params=params(60),
        cost_estimate=cost("norm_back"),
    )(index, hres, grad_out, gains, *part, *came, *weights.arrays)


def attn_bwd(seq, qkv, y, dy, dinv, dims):
    n_tok, buffers = qkv.shape[0], seq.shape[0]
    length = n_tok // buffers
    nq, nv, _ = dims

    def body(seq_ref, qkv_ref, y_ref, dy_ref, dinv_ref, out_ref, mask_ref, dq_acc, dk_acc, dv_acc):
        for b in range(buffers):
            make_mask(seq_ref, b, mask_ref)
            base = b * length
            dq_acc[...] = jnp.zeros_like(dq_acc)
            dk_acc[...] = jnp.zeros_like(dk_acc)

            def pair(hp, carry):
                lane = lax.broadcasted_iota(jnp.int32, (1, LANES), 1)
                zero = jnp.zeros((), BF16)
                k = qkv_ref[base : base + length, nq : 2 * nq]
                v_at = pl.ds(pl.multiple_of(2 * nq + hp * LANES, LANES), LANES)
                y_at = pl.ds(pl.multiple_of(hp * LANES, LANES), LANES)
                v = qkv_ref[base : base + length, v_at]
                dv_acc[...] = jnp.zeros_like(dv_acc)
                step = length // 2
                for tb in range(2):
                    rows = slice(base + tb * step, base + (tb + 1) * step)
                    here = slice(tb * step, (tb + 1) * step)
                    seen = (tb + 1) * step
                    q = qkv_ref[rows, :nq] * jnp.asarray(0.25, BF16)
                    mask = mask_ref[here, :seen]
                    dyn = dy_ref[rows, y_at].astype(F32) * dinv_ref[rows, y_at]
                    dot_y = dyn * y_ref[rows, y_at].astype(F32)
                    dyn = dyn.astype(BF16)
                    for j in range(2):
                        mine = lane // F == 2 * hp + j
                        side = lane // 64 == j
                        k_h = jnp.where(mine, k[:seen], zero)
                        v_h = jnp.where(side, v[:seen], zero)
                        one = dot_nt(q, k_h) + 1.0
                        half_one = one * mask
                        weights = (half_one * one + mask).astype(BF16)
                        d_p = dot_nt(dyn, v_h)
                        shift = jnp.sum(jnp.where(side, dot_y, 0.0), axis=-1, keepdims=True)
                        d_a = ((d_p - shift) * half_one).astype(BF16)
                        dv_acc[:seen, :] += dot_tn(weights, jnp.where(side, dyn, zero))
                        dq_acc[here, :] += dot_nn(d_a, k_h)
                        dk_acc[:seen, :] += dot_tn(d_a, jnp.where(mine, q, zero))
                out_ref[base : base + length, v_at] = dv_acc[...].astype(BF16)
                return carry

            lax.fori_loop(0, nv // LANES, pair, 0)
            out_ref[base : base + length, :nq] = (dq_acc[...] * 0.5).astype(BF16)
            out_ref[base : base + length, nq : 2 * nq] = (dk_acc[...] * 2.0).astype(BF16)

    return pl.pallas_call(
        body,
        name="attn_bwd",
        out_shape=jax.ShapeDtypeStruct(qkv.shape, BF16),
        in_specs=[SMEM_SPEC] + [VMEM_SPEC] * 4,
        out_specs=VMEM_SPEC,
        scratch_shapes=[
            pltpu.VMEM((length, length), F32),
            pltpu.VMEM((length, nq), F32),
            pltpu.VMEM((length, nq), F32),
            pltpu.VMEM((length, LANES), F32),
        ],
        compiler_params=params(60),
        cost_estimate=cost("attn_bwd"),
    )(seq, qkv, y, dy, dinv)


def norm_one_part(weights, index, d_qkv):
    n_tok, n_qkv = d_qkv.shape
    width = weights.blk.shape[0] * weights.blk.shape[1]
    n_in = weights.count
    steps = 4
    size = n_tok // steps

    def body(index_ref, d_ref, *refs):
        *out_refs, w_ref, sem = refs[n_in:]

        @pl.when(pl.program_id(0) == 0)
        def _():
            weights.load(index_ref, refs[:n_in], w_ref, sem)
            weights.wait(w_ref, sem)

        d = dot_nt(d_ref[...], w_ref[...].reshape(width, n_qkv))

        def put(ref):
            ref[...] = d.astype(BF16)

        with_piece(out_refs, steps, put)

    return pl.pallas_call(
        body,
        name="norm_one_part",
        grid=(steps,),
        out_shape=(
            jax.ShapeDtypeStruct((n_tok // 2, width), BF16),
            jax.ShapeDtypeStruct((n_tok // 2, width), BF16),
        ),
        in_specs=[SMEM_SPEC, rows_spec(size, n_qkv)] + weights.specs,
        out_specs=tuple(piece_specs(2, steps, size, width)),
        scratch_shapes=weights.scratch(n_qkv),
        compiler_params=params(60),
        cost_estimate=cost("norm_one_part"),
    )(index, d_qkv, *weights.arrays)


def finish(part, came, tok, dh, gains, hres, out_part, out_came):
    n_tok, width = tok.shape
    steps = 4
    size = n_tok // steps

    def body(part_ref, came_ref, tok_ref, dh_ref, gain_ref, h_ref, op_ref, oc_ref, grad_ref, out_ref):
        gain = gain_ref[0:1, :]

        def rows(at):
            d = (part_ref[at, :].astype(F32) + came_ref[at, :].astype(F32)) * gain
            x = tok_ref[at, :].astype(F32)
            inverse = lax.rsqrt(jnp.mean(x * x, axis=-1, keepdims=True) + EPS)
            xr = x * inverse
            back = inverse * (d - xr * jnp.mean(d * xr, axis=-1, keepdims=True))
            grad_ref[at, :] = (dh_ref[at, :] + back).astype(BF16)
            both = op_ref[at, :].astype(F32) + oc_ref[at, :].astype(F32)
            out_ref[at, :] = (h_ref[at, :] + both).astype(BF16)

        row_chunks(size, 64, rows)

    at = rows_spec(size, width)
    out = jax.ShapeDtypeStruct((n_tok, width), BF16)
    return pl.pallas_call(
        body,
        name="finish",
        grid=(steps,),
        out_shape=(out, out),
        in_specs=[at, at, at, at, pl.BlockSpec((8, width), lambda i: (0, 0)), at, at, at],
        out_specs=(at, at),
        compiler_params=params(60),
        cost_estimate=cost("finish"),
    )(part, came, tok, dh, gains, hres, out_part, out_came)


def local(
    lay,
    tokens,
    seq_lengths,
    w_query,
    w_key,
    w_value,
    w_output,
    w_gate,
    w_up,
    w_down,
    gain_attn,
    gain_mlp,
    cotangent,
):
    me = lax.axis_index(AXES).astype(jnp.int32)
    core = me % 2
    index = me.reshape(1)
    rows, length = w_query.shape[0], tokens.shape[0]
    nq, nv, nf = w_query.shape[1] // 2, w_value.shape[1] // 2, w_gate.shape[1] // 2
    stride = nf + -nf % LANES
    order = Order()
    blk = Blocks(lay, rows)
    masks = split_masks(lay)
    both = sum(plane_masks(lay, [0]), [])
    masks_z = [[m | z for m in both] for z in masks_of(lay.z)]
    dims = (nq, nv, 2 * nq + 2 * nv + LANES)

    keep_0, keep_gu, keep_d, give = prepare(
        core.reshape(1),
        [[w_query, w_key, w_value, w_output.T], [w_gate, w_up], [w_down.T]],
        [gain_attn, gain_mlp],
    )
    came = lay.swap(give, 1)
    tok_other, seq_other = lay.swap(tokens, 1), lay.swap(seq_lengths, 1)
    cot_other = lay.swap(cotangent, 1)
    came = order(came)
    at_d = dims[2] + 2 * stride

    z_0 = GatherZ(lay, jnp.stack([keep_0, came[:, : dims[2]]]))
    z_0.first()
    z_0.second()
    p_d = GatherPlane(lay, keep_d[None], came[None, :, at_d:])
    tok_other, seq_other, cot_other = order(tok_other, seq_other, cot_other)
    z_gu = GatherZ(lay, order(jnp.stack([keep_gu, came[:, dims[2] : at_d]])))
    z_gu.first()
    z_0.third(order)
    p_d.second(order)

    def halves(z):
        blocks = z.done(order)
        return [jnp.stack([b[h] for b in blocks]) for h in range(2)]

    p_0 = GatherPlane(lay, *halves(z_0))
    z_gu.second(order)
    held_d = p_d.joined(order)
    p_0.second(order)
    z_gu.third(order)
    z_d = GatherZ(lay, order(held_d))
    z_d.first()
    halves_gu = halves(z_gu)
    *arrays_0, keep_gu, other_gu = order(*p_0.arrays(), *halves_gu)
    p_gu = GatherPlane(lay, keep_gu, other_gu)
    z_d.second(order)
    w_0 = Weights(blk, arrays_0, masks, me)
    seq = jnp.concatenate([seq_lengths, seq_other], axis=0)
    tok = order(jnp.concatenate([tokens, tok_other], axis=0))
    grad_out = order(jnp.concatenate([cotangent, cot_other], axis=0))
    z_d.third(order, True)
    p_gu.second(order)
    tok = order(tok)

    def swap_all(values):
        return [lay.swap(v, 1) for v in values]

    normed_one, qkv, y, dinv, gains, *part_o = attn_fwd(w_0, index, seq, tok, dims)
    part_o = order(*part_o)
    came_o = swap_all(part_o)
    w_d = Weights(blk, z_d.done(order), masks_z, me)
    d_act = order(down_back(w_d, index, grad_out, stride))
    w_gu = Weights(blk, order(*p_gu.arrays()), masks, me)
    came_o = order(*came_o)
    hres, normed_two = residual(tok, part_o, came_o, gains)
    normed_two = order(normed_two)
    act, d_gate, d_up = order(*gated(w_gu, index, normed_two, d_act, stride))

    def grad(lefts, rights, gain=None, name="weight_grad"):
        outs = weight_grad(blk, masks, index, lefts, rights, gain, name)
        return blk.split(order(*outs), masks, me)

    wanted = [masks_of(lay.z).index(m) for m in low_first(lay)]

    def along_z(stream):
        return ReduceZ(lay, *fold_plane(stream.pairs(order), wanted))

    r_g = ReducePlane(lay, grad([normed_two], [d_gate], name="grad_gate"))
    d_up = order(d_up)
    part_n2 = order(*sum_nt(w_gu, index, [d_gate, d_up], [0, stride], 2 * stride, 2, "d_norm2"))
    came_n2 = swap_all(part_n2)
    r_g.second(order)
    act = order(act)
    r_d = ReducePlane(lay, grad([grad_out], [act], name="grad_down"))
    came_n2 = order(*came_n2)
    d_h, d_o, d_y, gg_mlp = norm_back(w_0, index, part_n2, came_n2, hres, grad_out, gains, dims)
    d_y = order(d_y)
    outs_u = grad([normed_two, d_o], [d_up, y], name="grad_up")
    zr_g = along_z(r_g)
    r_u = ReducePlane(lay, order(*outs_u))
    d_qkv = order(attn_bwd(seq, qkv, y, order(d_y), dinv, dims))
    wait_for(order, r_d, zr_g)
    r_d.second(order)
    wait_for(order, r_u)
    r_u.second(order)
    zr_g.second(order)
    d_qkv = order(d_qkv)
    outs_0 = grad([normed_one], [d_qkv], (w_0, gains, gg_mlp), name="grad_attn")
    zr_d = along_z(r_d)
    r_0 = ReducePlane(lay, order(*outs_0))
    part_n1 = order(*norm_one_part(w_0, index, order(d_qkv)))
    wait_for(order, zr_g, zr_d, r_u, r_0)
    r_0.second(order)
    zr_u = along_z(r_u)
    zr_d.second(order)
    part_out = order(*sum_nt(w_d, index, [order(act)], [0], stride, 2, "down"))
    came_rows = swap_all(order(part_n1[1], part_out[1]))
    wait_for(order, zr_u, r_0)
    zr_0 = along_z(r_0)
    zr_u.second(order)
    came_rows = order(*came_rows)
    grad_tokens, layer_out = finish(
        part_n1[0], came_rows[0], tokens, d_h, gains, hres, part_out[0], came_rows[1]
    )
    grad_tokens = order(grad_tokens)
    zr_0.second(order)
    end_d = zr_d.last(order)
    end_g = zr_g.last(order)
    end_u = zr_u.last(order)
    end_0 = zr_0.last(order)
    mine, give = add_up([end_0, end_d, end_g, end_u])
    came = lay.swap(give, 1)
    at = 2 * nq + nv
    at_d = at + LANES
    at_gu = at_d + stride
    places = [
        (0, nq),
        (nq, nq),
        (2 * nq, nv),
        (at_gu + 2 * stride, nv),
        (at_gu, nf),
        (at_gu + stride, nf),
        (at_d, nf),
        (at, LANES),
    ]
    *grads, g_one, g_two = conclude(core.reshape(1), mine, came, places)
    grads[3], grads[6] = grads[3].T, grads[6].T
    return (layer_out, grad_tokens, *grads, g_one[0], g_two[0])


def solution(mesh):
    rows, cols, flat = P(AXES, None), P(None, AXES), P(AXES)
    return jax.shard_map(
        functools.partial(local, Layout(mesh)),
        mesh=mesh,
        in_specs=(rows, rows, rows, rows, rows, cols, rows, rows, cols, flat, flat, rows),
        out_specs=(rows, rows, rows, rows, rows, cols, rows, rows, cols, flat, flat),
        check_vma=False,
    )
```

```python
import functools
import math

import jax
import jax.numpy as jnp
from jax import lax
from jax.experimental import pallas as pl
from jax.experimental.pallas import tpu as pltpu
from jax.sharding import PartitionSpec as P

H = 16
F = 16
EPS = 1e-05
AXES = ("dp", "fsdp")
LANES = 128
F32 = jnp.float32
BF16 = jnp.bfloat16

VMEM_SPEC = pl.BlockSpec(memory_space=pltpu.VMEM)
SMEM_SPEC = pl.BlockSpec(memory_space=pltpu.SMEM)
ANY_SPEC = pl.BlockSpec(memory_space=pl.ANY)


def dot_nn(a, b):
    return lax.dot_general(a, b, (((1,), (0,)), ((), ())), preferred_element_type=F32)


def dot_nt(a, b):
    return lax.dot_general(a, b, (((1,), (1,)), ((), ())), preferred_element_type=F32)


def dot_tn(a, b):
    return lax.dot_general(a, b, (((0,), (0,)), ((), ())), preferred_element_type=F32)


class Layout:
    def __init__(self, mesh):
        dp, fsdp = mesh.shape["dp"], mesh.shape["fsdp"]
        self.count = dp * fsdp
        x_bits = int(math.log2(fsdp)) - 1
        y_bits = int(math.log2(dp)) // 3
        all_bits = int(math.log2(self.count))
        self.x = [1 << (1 + i) for i in range(x_bits)]
        self.y = [1 << (1 + x_bits + i) for i in range(y_bits)]
        self.z = [1 << i for i in range(1 + x_bits + y_bits, all_bits)]

    def swap(self, value, bit):
        return lax.ppermute(value, AXES, [(i, i ^ bit) for i in range(self.count)])


def masks_of(bits):
    masks = [0]
    for bit in bits:
        masks = masks + [m | bit for m in masks]
    return masks


class Order:
    def __init__(self):
        self.last = None

    def __call__(self, *values):
        held = values if self.last is None else (*values, self.last)
        held = lax.optimization_barrier(held)
        self.last = held[0]
        return held[: len(values)] if len(values) > 1 else held[0]


def behind(value, order=None):
    return value if order is None else order(value)


def plane_masks(lay, base):
    found = []
    for half, bits in enumerate((lay.x + lay.y, lay.y + lay.x)):
        masks = [m | half for m in base]
        for bit in bits:
            masks = masks + [m | bit for m in masks]
        found.append(masks)
    return found


def split_masks(lay):
    return [
        part
        for masks in plane_masks(lay, masks_of(lay.z))
        for part in (masks[: len(masks) // 2], masks[len(masks) // 2 :])
    ]


class GatherZ:
    def __init__(self, lay, block):
        self.lay = lay
        self.bits = list(reversed(lay.z))
        self.found = {0: block}

    def first(self, *order):
        bit = self.bits[0]
        self.found[bit] = self.lay.swap(behind(self.found[0], *order), bit)

    def second(self, *order):
        for bit in self.bits[1:]:
            self.found[bit] = self.lay.swap(behind(self.found[0], *order), bit)

    def third(self, order, everything=False):
        if everything:
            for bit, value in zip(self.bits, order(*[self.found[bit] for bit in self.bits])):
                self.found[bit] = value
        else:
            self.found[self.bits[0]] = order(self.found[self.bits[0]])
        for i, bit in enumerate(self.bits[1:], 1):
            for m in masks_of(self.bits[:i])[1:]:
                self.found[m | bit] = self.lay.swap(self.found[m], bit)

    def done(self, order):
        masks = masks_of(self.lay.z)
        return order(*[self.found[m] for m in masks])


class GatherPlane:
    def __init__(self, lay, *halves):
        self.lay, self.halves = lay, halves
        self.orders = (lay.x + lay.y, lay.y + lay.x)
        self.came = [lay.swap(h, bits[0]) for h, bits in zip(halves, self.orders)]

    def second(self, order):
        came = order(*self.came)
        self.held, self.came = [], []
        for held, got, bits in zip(self.halves, came, self.orders):
            held = jnp.concatenate([held, got], axis=0)
            for bit in bits[1:-1]:
                held = jnp.concatenate([held, self.lay.swap(held, bit)], axis=0)
            self.held.append(held)
            self.came.append(self.lay.swap(held, bits[-1]))

    def arrays(self):
        return [self.held[0], self.came[0], self.held[1], self.came[1]]

    def joined(self, order):
        came = order(*self.came)
        return jnp.concatenate([self.held[0], came[0], self.held[1], came[1]], axis=0)


def add_low(a, b):
    return (a.astype(F32) + b.astype(F32)).astype(BF16)


def fold(pairs, name="fold"):
    n = len(pairs)

    def body(*refs):
        ins, outs = refs[: 2 * n], refs[2 * n :]
        step = pl.program_id(0)
        for i in range(n):
            value = add_low(ins[2 * i][...], ins[2 * i + 1][...])

            def put(ref, value=value):
                ref[...] = value

            pl.when(step == 0)(functools.partial(put, outs[2 * i + 1]))
            pl.when(step == 1)(functools.partial(put, outs[2 * i]))

    def half(a):
        return (a.shape[0] // 2, *a.shape[1:])

    def spec(a, there):
        rest = (0,) * (a.ndim - 1)
        return pl.BlockSpec(half(a), (lambda i: (1 - i, *rest)) if there else (lambda i: (0, *rest)))

    flat = [a for pair in pairs for a in pair]
    outs = pl.pallas_call(
        body,
        name=name,
        grid=(2,),
        out_shape=tuple(jax.ShapeDtypeStruct(half(a), BF16) for a in flat),
        in_specs=[spec(a, True) for a in flat],
        out_specs=tuple(spec(a, False) for a in flat),
        compiler_params=params(FOLD_MEGABYTES),
        cost_estimate=cost(name),
    )(*flat)
    return [(outs[2 * i], outs[2 * i + 1]) for i in range(n)]


def fold_plane(pairs, wanted):
    shape = (len(wanted) // 2, 2, *pairs[0][0].shape[1:])
    n = shape[0]

    def body(*refs):
        ins, outs = refs[:4], refs[4:]
        for place, i in enumerate(wanted):
            for h in range(2):
                outs[place // n][place % n, h] = add_low(ins[2 * h][i], ins[2 * h + 1][i])

    return pl.pallas_call(
        body,
        name="fold_plane",
        out_shape=(jax.ShapeDtypeStruct(shape, BF16),) * 2,
        in_specs=[VMEM_SPEC] * 4,
        out_specs=(VMEM_SPEC,) * 2,
        compiler_params=params(FOLD_MEGABYTES),
        cost_estimate=cost("fold_plane"),
    )(*[a for pair in pairs for a in pair])


class ReducePlane:
    def __init__(self, lay, arrays):
        self.lay = lay
        self.kept = [arrays[0], arrays[2]]
        self.orders = (lay.x + lay.y, lay.y + lay.x)
        self.came = [lay.swap(a, bits[-1]) for a, bits in zip(arrays[1::2], self.orders)]

    def second(self, order):
        for level in reversed(range(len(self.orders[0]) - 1)):
            came = order(*self.came)
            found = fold(list(zip(self.kept, came)))
            self.kept = [kept for kept, _ in found]
            self.came = [
                self.lay.swap(sent, bits[level]) for (_, sent), bits in zip(found, self.orders)
            ]

    def pairs(self, order):
        return list(zip(self.kept, order(*self.came)))


class ReduceZ:
    def __init__(self, lay, kept, sent):
        self.lay = lay
        self.bits = list(lay.z)
        self.kept = kept
        self.came = lay.swap(sent, self.bits[0])

    def second(self, order):
        while len(self.bits) > 1:
            self.bits.pop(0)
            ((self.kept, sent),) = fold([(self.kept, order(self.came))], "fold_z")
            self.came = self.lay.swap(sent, self.bits[0])

    def last(self, order):
        return self.kept, order(self.came)


def add_up(core, ends):
    rows = ends[0][0].shape[2]
    cols = sum(kept.shape[3] for kept, _ in ends)

    def body(core_ref, *refs):
        first = core_ref[0] == 0
        at = 0
        for i, (kept, _) in enumerate(ends):
            width = kept.shape[3]
            total = refs[2 * i][0].astype(F32) + refs[2 * i + 1][0].astype(F32)
            refs[-2][:, at : at + width] = jnp.where(first, total[0], total[1])
            refs[-1][:, at : at + width] = jnp.where(first, total[1], total[0])
            at += width

    return pl.pallas_call(
        body,
        name="add_up",
        out_shape=(jax.ShapeDtypeStruct((rows, cols), F32),) * 2,
        in_specs=[SMEM_SPEC] + [VMEM_SPEC] * (2 * len(ends)),
        out_specs=(VMEM_SPEC,) * 2,
        compiler_params=params(FOLD_MEGABYTES),
        cost_estimate=cost("add_up"),
    )(core, *[a for end in ends for a in end])


def wait_for(order, *streams):
    values = [v for s in streams for v in (s.came if isinstance(s.came, list) else [s.came])]
    values = list(order(*values))
    for s in streams:
        if isinstance(s.came, list):
            s.came = [values.pop(0) for _ in s.came]
        else:
            s.came = values.pop(0)


def low_first(lay):
    bits = lay.z
    masks = [0]
    for bit in reversed(bits):
        masks = masks + [m | bit for m in masks]
    return masks


WEIGHTS = {}
FOLD_MEGABYTES = 16


def cost(name):
    return pl.CostEstimate(
        flops=int(WEIGHTS.get(name, 0) * 1e9) + 1, bytes_accessed=1, transcendentals=0
    )


def near(*values):
    return [pltpu.with_memory_space_constraint(v, pltpu.VMEM) for v in values]


def params(megabytes):
    return pltpu.CompilerParams(vmem_limit_bytes=megabytes << 20)


def rows_spec(size, cols, last=None):
    return pl.BlockSpec((size, cols), lambda i: (i if last is None else jnp.minimum(i, last), 0))


def piece_of(i, pieces, steps, turn):
    block = lax.rem(i + steps // 2, steps) if turn else i
    return block // (steps // pieces), lax.rem(block, steps // pieces)


def piece_specs(pieces, steps, size, width, turn=False):
    def spec(q):
        def at(i):
            piece, block = piece_of(i, pieces, steps, turn)
            last = steps // pieces - 1
            return (jnp.where(piece == q, block, jnp.where(piece < q, 0, last)), 0)

        return pl.BlockSpec((size, width), at)

    return [spec(q) for q in range(pieces)]


def with_piece(refs, steps, body, turn=False):
    piece, _ = piece_of(pl.program_id(0), len(refs), steps, turn)
    for q, ref in enumerate(refs):
        pl.when(piece == q)(functools.partial(body, ref))


def row_chunks(total, size, body):
    def step(i, carry):
        body(pl.ds(pl.multiple_of(i * size, size), size))
        return carry

    lax.fori_loop(0, total // size, step, 0)


def make_mask(seq_ref, b, mask_ref):
    rows, cols = mask_ref.shape
    slots = seq_ref.shape[1]
    ends = []
    total = jnp.int32(0)
    for j in range(slots):
        total = total + seq_ref[b, j]
        ends.append(total)

    def body(at):
        t = lax.broadcasted_iota(jnp.int32, (at.size, cols), 0) + at.start
        s = lax.broadcasted_iota(jnp.int32, (at.size, cols), 1)
        seg_t = jnp.zeros_like(t)
        seg_s = jnp.zeros_like(s)
        for e in ends:
            seg_t = seg_t + (t >= e).astype(jnp.int32)
            seg_s = seg_s + (s >= e).astype(jnp.int32)
        seen = (s <= t) & (seg_t == seg_s) & (t < total)
        mask_ref[at, :] = jnp.where(seen, 0.5, 0.0).astype(F32)

    row_chunks(rows, 64, body)
    return total


def stacked(refs, start, size):
    return jnp.concatenate([r[:, start : start + size] for r in refs], axis=0)


def whole_specs(arrays):
    return [pl.BlockSpec(a.shape, lambda i: (0,) * a.ndim) for a in arrays]


def shuffle(index, masks, values):
    n, width = values[0].shape
    rows = width // len(masks)
    steps = n // 256
    count = len(values)

    def body(index_ref, masks_ref, *refs):
        ins, outs, order_ref = refs[:count], refs[count:-1], refs[-1]

        @pl.when(pl.program_id(0) == 0)
        def _():
            def fill(at):
                r = lax.broadcasted_iota(jnp.int32, (at.size, width), 0) + at.start
                c = lax.broadcasted_iota(jnp.int32, (at.size, width), 1)
                block = jnp.bitwise_xor(masks_ref[...], index_ref[0])
                here = (r // rows == block) & (r % rows == c % rows)
                order_ref[at, :] = jnp.where(here, 1.0, 0.0).astype(BF16)

            row_chunks(width, 128, fill)

        for i, o in zip(ins, outs):
            o[...] = dot_nn(i[...], order_ref[...]).astype(BF16)

    table = jnp.repeat(jnp.asarray(masks, jnp.int32), rows)[None]
    at = rows_spec(256, width)
    keep = pl.BlockSpec((width, width), lambda i: (0, 0))
    return pl.pallas_call(
        body,
        name="shuffle",
        grid=(steps,),
        out_shape=(*[pltpu.VMEM(v.shape, BF16) for v in values], pltpu.VMEM((width, width), BF16)),
        in_specs=[SMEM_SPEC, pl.BlockSpec((1, width), lambda i: (0, 0))] + [at] * count,
        out_specs=(*[at] * count, keep),
        compiler_params=params(20),
        cost_estimate=cost("shuffle"),
    )(index, table, *values)


def prepare(core, groups, gains):
    rows = groups[0][0].shape[0]
    flat = [w for group in groups for w in group]
    padded = [w.shape[1] // 2 + -(w.shape[1] // 2) % LANES for w in flat]
    n_in = len(flat)
    widths, at = [], 0
    for group in groups:
        widths.append(sum(padded[at : at + len(group)]))
        at += len(group)
    widths[0] += LANES

    def body(core_ref, one_ref, two_ref, *refs):
        ins, keeps, give_ref = refs[:n_in], refs[n_in:-1], refs[-1]
        first = core_ref[0] == 0
        place, start = 0, 0
        for number, (group, keep_ref) in enumerate(zip(groups, keeps)):
            at = 0
            for _ in group:
                value = ins[place][...]
                half = value.shape[1] // 2
                low, high = value[:, :half].astype(F32), value[:, half:].astype(F32)
                spare = padded[place] - half
                for ref, base, one, two in (
                    (keep_ref, 0, low, high),
                    (give_ref, start, high, low),
                ):
                    ref[:, base + at : base + at + half] = jnp.where(first, one, two).astype(BF16)
                    if spare:
                        zeros = jnp.zeros((rows, spare), BF16)
                        ref[:, base + at + half : base + at + half + spare] = zeros
                at += padded[place]
                place += 1
            if number == 0:
                lines = []
                for ref in (one_ref, two_ref):
                    gain = ref[...]
                    high = gain.astype(BF16).astype(F32)
                    lines += [high, gain - high]
                lines = jnp.concatenate(lines + [jnp.zeros((LANES - 4, rows), F32)], axis=0)
                turned = lines.T.astype(BF16)
                keep_ref[:, at : at + LANES] = turned
                give_ref[:, at : at + LANES] = turned
                at += LANES
            start += at

    out = [jax.ShapeDtypeStruct((rows, n), BF16) for n in [*widths, sum(widths)]]
    return pl.pallas_call(
        body,
        name="prepare",
        out_shape=tuple(out),
        in_specs=[SMEM_SPEC] + [VMEM_SPEC] * (n_in + 2),
        out_specs=(VMEM_SPEC,) * len(out),
        compiler_params=params(16),
    )(core, *[g[None] for g in gains], *flat)


def conclude(core, mine, came, places):
    rows = mine.shape[0]
    n = len(places) - 1

    def body(core_ref, mine_ref, came_ref, *refs):
        first = core_ref[0] == 0
        for (at, half), ref in zip(places[:n], refs):
            own, other = mine_ref[:, at : at + half], came_ref[:, at : at + half]
            ref[:, :half] = jnp.where(first, own, other)
            ref[:, half:] = jnp.where(first, other, own)
        at = places[n][0]
        own = mine_ref[:, at : at + LANES].T
        other = came_ref[:, at : at + LANES].T
        refs[n][...] = own[0:1] + other[0:1]
        refs[n + 1][...] = own[1:2]

    out = [jax.ShapeDtypeStruct((rows, 2 * half), F32) for _, half in places[:n]]
    out += [jax.ShapeDtypeStruct((1, rows), F32)] * 2
    return pl.pallas_call(
        body,
        name="conclude",
        out_shape=tuple(out),
        in_specs=[SMEM_SPEC, VMEM_SPEC, VMEM_SPEC],
        out_specs=(VMEM_SPEC,) * len(out),
        compiler_params=params(16),
    )(core, mine, came)


def attn_fwd(weights, seq, tok, dims):
    n_tok, width, buffers = tok.shape[0], tok.shape[1], seq.shape[0]
    length = n_tok // buffers
    nq, nv, cols = dims
    n_qkv = 2 * nq + nv
    n_in = len(weights)

    def body(seq_ref, tok_ref, *refs):
        w_in = refs[:n_in]
        normed_ref, qkv_ref, y_ref, dinv_ref, gain_ref = refs[n_in : n_in + 5]
        part_refs = refs[n_in + 5 : n_in + 5 + 2 * buffers]
        mask_ref = refs[n_in + 5 + 2 * buffers]
        w_gain = stacked(w_in, n_qkv + nv, LANES).astype(F32).T
        gain_ref[0:1, :] = w_gain[0:1] + w_gain[1:2]
        gain_ref[1:2, :] = w_gain[2:3] + w_gain[3:4]
        gain_ref[2:8, :] = jnp.zeros((6, width), F32)
        gain = gain_ref[0:1, :]

        def project(at):
            x = tok_ref[at, :].astype(F32)
            inverse = lax.rsqrt(jnp.mean(x * x, axis=-1, keepdims=True) + EPS)
            normed = (x * inverse * gain).astype(BF16)
            normed_ref[at, :] = normed
            qkv_ref[at, :] = dot_nn(normed, stacked(w_in, 0, n_qkv)).astype(BF16)

        row_chunks(n_tok, 256, project)

        for b in range(buffers):
            total = make_mask(seq_ref, b, mask_ref)
            base = b * length

            def pair(hp, carry):
                lane = lax.broadcasted_iota(jnp.int32, (1, LANES), 1)
                k = qkv_ref[base : base + length, nq : 2 * nq]
                v_at = pl.ds(pl.multiple_of(2 * nq + hp * LANES, LANES), LANES)
                v = qkv_ref[base : base + length, v_at]
                step = length // 2
                for tb in range(2):
                    rows = slice(base + tb * step, base + (tb + 1) * step)
                    seen = (tb + 1) * step
                    q = qkv_ref[rows, :nq] * jnp.asarray(0.25, BF16)
                    mask = mask_ref[tb * step : (tb + 1) * step, :seen]
                    row = lax.broadcasted_iota(jnp.int32, (step, 1), 0) + tb * step
                    pad = (row >= total).astype(F32)
                    found = []
                    for j in range(2):
                        k_h = jnp.where(lane // F == 2 * hp + j, k[:seen], jnp.zeros((), BF16))
                        v_h = jnp.where(lane // 64 == j, v[:seen], jnp.ones((), BF16))
                        one = dot_nt(q, k_h) + 1.0
                        share = ((one * one + 1.0) * mask).astype(BF16)
                        mixed = dot_nn(share, v_h)
                        inverse = 1.0 / (pltpu.roll(mixed, 64, 1) + pad)
                        found.append((mixed * inverse, inverse))
                    low = lane < 64
                    y_at = pl.ds(pl.multiple_of(hp * LANES, LANES), LANES)
                    y_ref[rows, y_at] = jnp.where(low, found[0][0], found[1][0]).astype(BF16)
                    dinv_ref[rows, y_at] = jnp.where(low, found[0][1], found[1][1])
                return carry

            lax.fori_loop(0, nv // LANES, pair, 0)
            for half in range(2):
                at = slice(base + half * (length // 2), base + (half + 1) * (length // 2))
                part = dot_nt(y_ref[at, :], stacked(w_in, n_qkv, nv))
                part_refs[2 * b + half][...] = part.astype(BF16)

    return pl.pallas_call(
        body,
        name="attn_fwd",
        out_shape=(
            pltpu.VMEM((n_tok, width), BF16),
            pltpu.VMEM((n_tok, n_qkv), BF16),
            pltpu.VMEM((n_tok, nv), BF16),
            pltpu.VMEM((n_tok, nv), F32),
            jax.ShapeDtypeStruct((8, width), F32),
            *(jax.ShapeDtypeStruct((length // 2, width), BF16) for _ in range(2 * buffers)),
        ),
        in_specs=[SMEM_SPEC] + [VMEM_SPEC] * (1 + n_in),
        out_specs=(VMEM_SPEC,) * (5 + 2 * buffers),
        scratch_shapes=[pltpu.VMEM((length, length), F32)],
        compiler_params=params(28),
        cost_estimate=cost("attn_fwd"),
    )(seq, *near(tok), *weights)


def residual(tok, part, came, gains):
    n_tok, width = tok.shape
    steps = 4
    size = n_tok // steps

    n = len(part)

    def body(tok_ref, *refs):
        part_refs, came_refs = refs[:n], refs[n : 2 * n]
        gain_ref, hres_ref, normed_ref = refs[2 * n :]
        gain = gain_ref[1:2, :]

        def rows(at, part_ref, came_ref):
            x = tok_ref[at, :].astype(F32)
            x = x + (part_ref[at, :].astype(F32) + came_ref[at, :].astype(F32))
            hres_ref[at, :] = x
            inverse = lax.rsqrt(jnp.mean(x * x, axis=-1, keepdims=True) + EPS)
            normed_ref[at, :] = (x * inverse * gain).astype(BF16)

        pairs = list(zip(part_refs, came_refs[n // 2 :] + came_refs[: n // 2]))
        with_piece(pairs, steps, lambda pair: row_chunks(size, 64, lambda at: rows(at, *pair)))

    at = rows_spec(size, width)
    return pl.pallas_call(
        body,
        name="residual",
        grid=(steps,),
        out_shape=(pltpu.VMEM((n_tok, width), F32), pltpu.VMEM((n_tok, width), BF16)),
        in_specs=[at]
        + piece_specs(n, steps, size, width)
        + piece_specs(n, steps, size, width, True)
        + [pl.BlockSpec((8, width), lambda i: (0, 0))],
        out_specs=(at, at),
        compiler_params=params(16),
        cost_estimate=cost("residual"),
    )(*near(tok), *part, *came, gains)


def in_order(refs, places, rows):
    if places is None:
        return jnp.concatenate([r[...] for r in refs], axis=0)
    return jnp.concatenate([refs[j][i * rows : (i + 1) * rows, :] for j, i in places], axis=0)


def down_back(weights, places, rows, grad_out):
    n_tok, width = grad_out.shape
    cols = weights[0].shape[1]
    steps = 4
    size = n_tok // steps

    def body(grad_ref, *refs):
        w = in_order(refs[:-1], places, rows)
        refs[-1][...] = dot_nn(grad_ref[...], w).astype(BF16)

    return pl.pallas_call(
        body,
        name="down_back",
        grid=(steps,),
        out_shape=pltpu.VMEM((n_tok, cols), BF16),
        in_specs=[rows_spec(size, width)] + whole_specs(weights),
        out_specs=rows_spec(size, cols),
        compiler_params=params(20),
        cost_estimate=cost("down_back"),
    )(*near(grad_out), *weights)


def gated(weights, normed, d_act):
    n_tok, width = normed.shape
    cols = d_act.shape[1]
    n_in = len(weights)
    steps = 4
    size = n_tok // steps

    def body(normed_ref, d_act_ref, *refs):
        act_ref, d_gate_ref, d_up_ref = refs[n_in:]
        x = normed_ref[...]
        gate = dot_nn(x, stacked(refs[:n_in], 0, cols))
        up = dot_nn(x, stacked(refs[:n_in], cols, cols))
        sig = 1.0 / (1.0 + jnp.exp(-gate))
        silu = gate * sig
        act_ref[...] = (silu * up).astype(BF16)
        d = d_act_ref[...].astype(F32)
        d_gate_ref[...] = (d * up * sig * (1.0 + gate * (1.0 - sig))).astype(BF16)
        d_up_ref[...] = (d * silu).astype(BF16)

    out = pltpu.VMEM((n_tok, cols), BF16)
    at = rows_spec(size, cols)
    return pl.pallas_call(
        body,
        name="gated",
        grid=(steps,),
        out_shape=(out, out, out),
        in_specs=[rows_spec(size, width), at] + whole_specs(weights),
        out_specs=(at, at, at),
        compiler_params=params(30),
        cost_estimate=cost("gated"),
    )(*near(normed, d_act), *weights)


def weight_grad(lefts, rights, gain=None, name="weight_grad"):
    n_tok, width = lefts[0].shape
    sizes = [r.shape[1] for r in rights]
    cols = sum(sizes) + (LANES if gain is not None else 0)
    n, pieces = len(lefts), 4
    chunk = width // pieces
    extras, specs = [], []
    if gain is not None:
        weights, gains, other = gain
        extras = [gains, other, *weights]
        specs = [pl.BlockSpec((8, chunk), lambda i: (0, i))] * 2 + whole_specs(weights)

    def body(*refs):
        left_refs, right_refs = refs[:n], refs[n : 2 * n]
        ins, outs = refs[2 * n : 2 * n + len(extras)], refs[2 * n + len(extras) :]

        values = [dot_tn(left[...], right[...]) for left, right in zip(left_refs, right_refs)]

        def put(out, w_ref):
            start = 0
            for value, size in zip(values, sizes):
                out[:, start : start + size] = value.astype(BF16)
                start += size
            if gain is not None:
                one = values[0] * w_ref[:, : sizes[0]].astype(F32)
                one = jnp.sum(one, axis=-1, keepdims=True)
                two = jnp.sum(ins[1][...], axis=0, keepdims=True)
                lines = [ins[0][0:1, :], two, jnp.zeros((LANES - 2, chunk), F32)]
                turned = jnp.concatenate(lines).T
                lane = lax.broadcasted_iota(jnp.int32, turned.shape, 1)
                turned = jnp.where(lane == 0, one / turned, turned)
                out[:, cols - LANES :] = turned.astype(BF16)

        for q, out in enumerate(outs):
            w_ref = ins[2 + q] if gain is not None else None
            pl.when(pl.program_id(0) == q)(functools.partial(put, out, w_ref))

    return pl.pallas_call(
        body,
        name=name,
        grid=(pieces,),
        out_shape=(jax.ShapeDtypeStruct((chunk, cols), BF16),) * pieces,
        in_specs=[pl.BlockSpec((n_tok, chunk), lambda i: (0, i))] * n
        + [pl.BlockSpec(r.shape, lambda i: (0, 0)) for r in rights]
        + specs,
        out_specs=(pl.BlockSpec((chunk, cols), lambda i: (0, 0)),) * pieces,
        compiler_params=params(26),
        cost_estimate=cost(name),
    )(*near(*lefts, *rights), *extras)


def sum_nt(weights, lefts, starts, pieces, name, places=None, rows=0):
    n_tok, cols = lefts[0].shape
    width = sum(w.shape[0] for w in weights)
    n, n_in = len(lefts), len(weights)
    steps = 4
    size = n_tok // steps

    def body(*refs):
        left_refs, w_refs, out_refs = refs[:n], refs[n : n + n_in], refs[n + n_in :]

        if places is not None:
            values = [dot_nt(left_refs[0][...], in_order(w_refs, places, rows))]
        else:
            values = []
            for w in w_refs:
                value = None
                for left, start in zip(left_refs, starts):
                    term = dot_nt(left[...], w[:, start : start + cols])
                    value = term if value is None else value + term
                values.append(value)

        def put(ref):
            at = 0
            for value in values:
                ref[:, at : at + value.shape[1]] = value.astype(BF16)
                at += value.shape[1]

        with_piece(out_refs, steps, put)

    return pl.pallas_call(
        body,
        name=name,
        grid=(steps,),
        out_shape=(jax.ShapeDtypeStruct((n_tok // pieces, width), BF16),) * pieces,
        in_specs=[rows_spec(size, cols)] * n + whole_specs(weights),
        out_specs=tuple(piece_specs(pieces, steps, size, width)),
        compiler_params=params(20),
        cost_estimate=cost(name),
    )(*near(*lefts), *weights)


def norm_back(weights, part, came, hres, grad_out, gains, dims):
    n_tok, width = hres.shape
    nq, nv, _ = dims
    n_qkv = 2 * nq + nv
    n_in = len(weights)
    steps = 4
    size = n_tok // steps
    n = len(part)

    def body(hres_ref, c_ref, gain_ref, *refs):
        part_refs, came_refs, refs = refs[:n], refs[n : 2 * n], refs[2 * n :]
        dh_ref, do_ref, dy_ref, gg_ref = refs[n_in:]
        gain = gain_ref[1:2, :]
        i = pl.program_id(0)

        @pl.when(i == 0)
        def _():
            gg_ref[...] = jnp.zeros_like(gg_ref)

        def rows(at, part_ref, came_ref):
            d = part_ref[at, :].astype(F32) + came_ref[at, :].astype(F32)
            h = hres_ref[at, :]
            inverse = lax.rsqrt(jnp.mean(h * h, axis=-1, keepdims=True) + EPS)
            hr = h * inverse
            gg_ref[...] += jnp.sum((d * hr).reshape(-1, 8, width), axis=0)
            dg = d * gain
            back = inverse * (dg - hr * jnp.mean(dg * hr, axis=-1, keepdims=True))
            dh = c_ref[at, :].astype(F32) + back

            @pl.when(i < steps // 2)
            def _():
                dh_ref[at, :] = dh

            do_ref[at, :] = dh.astype(BF16)

        pairs = list(zip(part_refs, came_refs[n // 2 :] + came_refs[: n // 2]))
        with_piece(pairs, steps, lambda pair: row_chunks(size, 64, lambda at: rows(at, *pair)))

        dy_ref[...] = dot_nn(do_ref[...], stacked(refs[:n_in], n_qkv, nv)).astype(BF16)

    at = rows_spec(size, width)
    keep = pl.BlockSpec((8, width), lambda i: (0, 0))
    return pl.pallas_call(
        body,
        name="norm_back",
        grid=(steps,),
        out_shape=(
            pltpu.VMEM((n_tok // 2, width), F32),
            pltpu.VMEM((n_tok, width), BF16),
            pltpu.VMEM((n_tok, nv), BF16),
            jax.ShapeDtypeStruct((8, width), F32),
        ),
        in_specs=[at, at, keep]
        + piece_specs(n, steps, size, width)
        + piece_specs(n, steps, size, width, True)
        + whole_specs(weights),
        out_specs=(
            rows_spec(size, width, last=steps // 2 - 1),
            at,
            rows_spec(size, nv),
            keep,
        ),
        compiler_params=params(20),
        cost_estimate=cost("norm_back"),
    )(*near(hres, grad_out), gains, *part, *came, *weights)


def attn_bwd(seq, qkv, y, dy, dinv, dims):
    n_tok, buffers = qkv.shape[0], seq.shape[0]
    length = n_tok // buffers
    nq, nv, _ = dims

    def body(seq_ref, qkv_ref, y_ref, dy_ref, dinv_ref, out_ref, mask_ref, dq_acc, dk_acc, dv_acc):
        for b in range(buffers):
            make_mask(seq_ref, b, mask_ref)
            base = b * length
            dq_acc[...] = jnp.zeros_like(dq_acc)
            dk_acc[...] = jnp.zeros_like(dk_acc)

            def pair(hp, carry):
                lane = lax.broadcasted_iota(jnp.int32, (1, LANES), 1)
                zero = jnp.zeros((), BF16)
                k = qkv_ref[base : base + length, nq : 2 * nq]
                v_at = pl.ds(pl.multiple_of(2 * nq + hp * LANES, LANES), LANES)
                y_at = pl.ds(pl.multiple_of(hp * LANES, LANES), LANES)
                v = qkv_ref[base : base + length, v_at]
                dv_acc[...] = jnp.zeros_like(dv_acc)
                step = length // 2
                for tb in range(2):
                    rows = slice(base + tb * step, base + (tb + 1) * step)
                    here = slice(tb * step, (tb + 1) * step)
                    seen = (tb + 1) * step
                    q = qkv_ref[rows, :nq] * jnp.asarray(0.25, BF16)
                    mask = mask_ref[here, :seen]
                    dyn = dy_ref[rows, y_at].astype(F32) * dinv_ref[rows, y_at]
                    dot_y = dyn * y_ref[rows, y_at].astype(F32)
                    dyn = dyn.astype(BF16)
                    for j in range(2):
                        mine = lane // F == 2 * hp + j
                        side = lane // 64 == j
                        k_h = jnp.where(mine, k[:seen], zero)
                        v_h = jnp.where(side, v[:seen], zero)
                        one = dot_nt(q, k_h) + 1.0
                        half_one = one * mask
                        weights = (half_one * one + mask).astype(BF16)
                        d_p = dot_nt(dyn, v_h)
                        shift = jnp.sum(jnp.where(side, dot_y, 0.0), axis=-1, keepdims=True)
                        d_a = ((d_p - shift) * half_one).astype(BF16)
                        dv_acc[:seen, :] += dot_tn(weights, jnp.where(side, dyn, zero))
                        dq_acc[here, :] += dot_nn(d_a, k_h)
                        dk_acc[:seen, :] += dot_tn(d_a, jnp.where(mine, q, zero))
                out_ref[base : base + length, v_at] = dv_acc[...].astype(BF16)
                return carry

            lax.fori_loop(0, nv // LANES, pair, 0)
            out_ref[base : base + length, :nq] = (dq_acc[...] * 0.5).astype(BF16)
            out_ref[base : base + length, nq : 2 * nq] = (dk_acc[...] * 2.0).astype(BF16)

    return pl.pallas_call(
        body,
        name="attn_bwd",
        out_shape=pltpu.VMEM(qkv.shape, BF16),
        in_specs=[SMEM_SPEC] + [VMEM_SPEC] * 4,
        out_specs=VMEM_SPEC,
        scratch_shapes=[
            pltpu.VMEM((length, length), F32),
            pltpu.VMEM((length, nq), F32),
            pltpu.VMEM((length, nq), F32),
            pltpu.VMEM((length, LANES), F32),
        ],
        compiler_params=params(20),
        cost_estimate=cost("attn_bwd"),
    )(seq, *near(qkv, y, dy, dinv))


def finish(part, came, tok, dh, gains, hres, out_part, out_came, placing):
    n_tok, width = part.shape
    steps = 4
    size = n_tok // steps

    def body(
        part_ref, came_ref, tok_ref, dh_ref, gain_ref, h_ref, op_ref, oc_ref, p_ref,
        grad_ref, out_ref, grad_low, out_low,
    ):
        gain = gain_ref[0:1, :]

        def rows(at):
            d = (part_ref[at, :].astype(F32) + came_ref[at, :].astype(F32)) * gain
            x = tok_ref[at, :].astype(F32)
            inverse = lax.rsqrt(jnp.mean(x * x, axis=-1, keepdims=True) + EPS)
            xr = x * inverse
            back = inverse * (d - xr * jnp.mean(d * xr, axis=-1, keepdims=True))
            grad_low[at, :] = (dh_ref[at, :] + back).astype(BF16)
            both = op_ref[at, :].astype(F32) + oc_ref[at, :].astype(F32)
            out_low[at, :] = (h_ref[at, :] + both).astype(BF16)

        row_chunks(size, 64, rows)
        grad_ref[...] = dot_nt(grad_low[...], p_ref[...]).astype(BF16)
        out_ref[...] = dot_nt(out_low[...], p_ref[...]).astype(BF16)

    at = rows_spec(size, width)
    out = jax.ShapeDtypeStruct((n_tok, width), BF16)
    return pl.pallas_call(
        body,
        name="finish",
        grid=(steps,),
        out_shape=(out, out),
        in_specs=[at, at, at, at, pl.BlockSpec((8, width), lambda i: (0, 0)), at, at, at]
        + [pl.BlockSpec((width, width), lambda i: (0, 0))],
        out_specs=(at, at),
        scratch_shapes=[pltpu.VMEM((size, width), BF16)] * 2,
        compiler_params=params(16),
        cost_estimate=cost("finish"),
    )(part, came, *near(tok, dh), gains, *near(hres), out_part, out_came, *near(placing))


def local(
    lay,
    tokens,
    seq_lengths,
    w_query,
    w_key,
    w_value,
    w_output,
    w_gate,
    w_up,
    w_down,
    gain_attn,
    gain_mlp,
    cotangent,
):
    me = lax.axis_index(AXES).astype(jnp.int32)
    core = me % 2
    index = (me - core).reshape(1)
    rows, length = w_query.shape[0], tokens.shape[0]
    nq, nv, nf = w_query.shape[1] // 2, w_value.shape[1] // 2, w_gate.shape[1] // 2
    stride = nf + -nf % LANES
    order = Order()
    masks = split_masks(lay)
    flat_masks = sum(masks, [])
    both = sum(plane_masks(lay, [0]), [])
    places_z = {m | z: (j, i) for j, z in enumerate(masks_of(lay.z)) for i, m in enumerate(both)}
    places_z = [places_z[m] for m in flat_masks]

    def flat(arrays):
        return [a.reshape(-1, a.shape[-1]) for a in arrays]

    def blocks(arrays):
        return [a.reshape(-1, rows, a.shape[-1]) for a in arrays]
    dims = (nq, nv, 2 * nq + 2 * nv + LANES)

    keep_0, keep_gu, keep_d, give = prepare(
        core.reshape(1),
        [[w_query, w_key, w_value, w_output.T], [w_gate, w_up], [w_down.T]],
        [gain_attn, gain_mlp],
    )
    came = lay.swap(give, 1)
    tok_other, seq_other = lay.swap(tokens, 1), lay.swap(seq_lengths, 1)
    cot_other = lay.swap(cotangent, 1)
    came = order(came)
    at_d = dims[2] + 2 * stride

    def by_core(own, other):
        return jnp.where(core == 0, jnp.stack([own, other]), jnp.stack([other, own]))

    z_0 = GatherZ(lay, by_core(keep_0, came[:, : dims[2]]))
    z_0.first()
    z_0.second()
    halves_d = by_core(keep_d, came[:, at_d:])
    p_d = GatherPlane(lay, halves_d[:1], halves_d[1:])
    tok_other, seq_other, cot_other = order(tok_other, seq_other, cot_other)
    z_gu = GatherZ(lay, order(by_core(keep_gu, came[:, dims[2] : at_d])))
    z_gu.first()
    z_0.third(order)
    p_d.second(order)

    def halves(z):
        blocks = z.done(order)
        return [jnp.stack([b[h] for b in blocks]) for h in range(2)]

    p_0 = GatherPlane(lay, *halves(z_0))
    z_gu.second(order)
    held_d = p_d.joined(order)
    p_0.second(order)
    z_gu.third(order)
    z_d = GatherZ(lay, order(held_d))
    z_d.first()
    halves_gu = halves(z_gu)
    *arrays_0, low_gu, high_gu = order(*p_0.arrays(), *halves_gu)
    p_gu = GatherPlane(lay, low_gu, high_gu)
    z_d.second(order)
    w_0 = flat(arrays_0)
    seq = jnp.concatenate([seq_lengths, seq_other], axis=0)
    tok = jnp.concatenate([tokens, tok_other], axis=0)
    grad_out = jnp.concatenate([cotangent, cot_other], axis=0)
    tok, grad_out, placing = order(*shuffle(index, flat_masks, [tok, grad_out]))
    z_d.third(order, True)
    p_gu.second(order)
    def swap_all(values):
        return [lay.swap(v, 1) for v in values]

    normed_one, qkv, y, dinv, gains, *part_o = attn_fwd(w_0, seq, tok, dims)
    part_o = order(*part_o)
    came_o = swap_all(part_o)
    w_d = z_d.done(order)
    if rows % 16:
        order_d = [j * len(both) + i for j, i in places_z]
        w_d = jnp.take(jnp.concatenate(w_d), jnp.asarray(order_d), axis=0)
        w_d, places_z = jnp.split(w_d, 4), None
    w_d = flat(w_d)
    d_act = order(down_back(w_d, places_z, rows, grad_out))
    w_gu = flat(order(*p_gu.arrays()))
    came_o = order(*came_o)
    hres, normed_two = residual(tok, part_o, came_o, gains)
    normed_two = order(normed_two)
    act, d_gate, d_up = order(*gated(w_gu, normed_two, d_act))

    def grad(lefts, rights, gain=None, name="weight_grad"):
        return blocks(order(*weight_grad(lefts, rights, gain, name)))

    wanted = [masks_of(lay.z).index(m) for m in low_first(lay)]

    def along_z(stream):
        return ReduceZ(lay, *fold_plane(stream.pairs(order), wanted))

    r_g = ReducePlane(lay, grad([normed_two], [d_gate], name="grad_gate"))
    d_up = order(d_up)
    part_n2 = order(*sum_nt(w_gu, [d_gate, d_up], [0, stride], 2, "d_norm2"))
    came_n2 = swap_all(part_n2)
    r_g.second(order)
    act = order(act)
    r_d = ReducePlane(lay, grad([grad_out], [act], name="grad_down"))
    came_n2 = order(*came_n2)
    d_h, d_o, d_y, gg_mlp = norm_back(w_0, part_n2, came_n2, hres, grad_out, gains, dims)
    d_y = order(d_y)
    outs_u = grad([normed_two, d_o], [d_up, y], name="grad_up")
    zr_g = along_z(r_g)
    r_u = ReducePlane(lay, order(*outs_u))
    d_qkv = order(attn_bwd(seq, qkv, y, order(d_y), dinv, dims))
    wait_for(order, r_d, zr_g)
    r_d.second(order)
    wait_for(order, r_u)
    r_u.second(order)
    zr_g.second(order)
    d_qkv = order(d_qkv)
    outs_0 = grad([normed_one], [d_qkv], (w_0, gains, gg_mlp), name="grad_attn")
    zr_d = along_z(r_d)
    r_0 = ReducePlane(lay, order(*outs_0))
    part_n1 = order(*sum_nt(w_0, [order(d_qkv)], [0], 2, "norm_one_part"))
    wait_for(order, zr_g, zr_d, r_u, r_0)
    r_0.second(order)
    zr_u = along_z(r_u)
    zr_d.second(order)
    part_out = order(*sum_nt(w_d, [order(act)], [0], 2, "down", places_z, rows))
    came_rows = swap_all(order(part_n1[1], part_out[1]))
    wait_for(order, zr_u, r_0)
    zr_0 = along_z(r_0)
    zr_u.second(order)
    came_rows = order(*came_rows)
    grad_tokens, layer_out = finish(
        part_n1[0], came_rows[0], tok, d_h, gains, hres, part_out[0], came_rows[1], placing
    )
    grad_tokens = order(grad_tokens)
    zr_0.second(order)
    end_d = zr_d.last(order)
    end_g = zr_g.last(order)
    end_u = zr_u.last(order)
    end_0 = zr_0.last(order)
    mine, give = add_up(core.reshape(1), [end_0, end_d, end_g, end_u])
    came = lay.swap(give, 1)
    at = 2 * nq + nv
    at_d = at + LANES
    at_gu = at_d + stride
    places = [
        (0, nq),
        (nq, nq),
        (2 * nq, nv),
        (at_gu + 2 * stride, nv),
        (at_gu, nf),
        (at_gu + stride, nf),
        (at_d, nf),
        (at, LANES),
    ]
    *grads, g_one, g_two = conclude(core.reshape(1), mine, came, places)
    grads[3], grads[6] = grads[3].T, grads[6].T
    return (layer_out, grad_tokens, *grads, g_one[0], g_two[0])


def solution(mesh):
    rows, cols, flat = P(AXES, None), P(None, AXES), P(AXES)
    return jax.shard_map(
        functools.partial(local, Layout(mesh)),
        mesh=mesh,
        in_specs=(rows, rows, rows, rows, rows, cols, rows, rows, cols, flat, flat, rows),
        out_specs=(rows, rows, rows, rows, rows, cols, rows, rows, cols, flat, flat),
        check_vma=False,
    )
```

```python
import functools
import math

import jax
import jax.numpy as jnp
from jax import lax
from jax.experimental import pallas as pl
from jax.experimental.pallas import tpu as pltpu
from jax.sharding import PartitionSpec as P

H = 16
F = 16
EPS = 1e-05
AXES = ("dp", "fsdp")
LANES = 128
F32 = jnp.float32
BF16 = jnp.bfloat16

VMEM_SPEC = pl.BlockSpec(memory_space=pltpu.VMEM)
SMEM_SPEC = pl.BlockSpec(memory_space=pltpu.SMEM)
ANY_SPEC = pl.BlockSpec(memory_space=pl.ANY)


def dot_nn(a, b):
    return lax.dot_general(a, b, (((1,), (0,)), ((), ())), preferred_element_type=F32)


def dot_nt(a, b):
    return lax.dot_general(a, b, (((1,), (1,)), ((), ())), preferred_element_type=F32)


def dot_tn(a, b):
    return lax.dot_general(a, b, (((0,), (0,)), ((), ())), preferred_element_type=F32)


class Layout:
    def __init__(self, mesh):
        dp, fsdp = mesh.shape["dp"], mesh.shape["fsdp"]
        self.count = dp * fsdp
        x_bits = int(math.log2(fsdp)) - 1
        y_bits = int(math.log2(dp)) // 3
        all_bits = int(math.log2(self.count))
        self.x = [1 << (1 + i) for i in range(x_bits)]
        self.y = [1 << (1 + x_bits + i) for i in range(y_bits)]
        self.z = [1 << i for i in range(1 + x_bits + y_bits, all_bits)]

    def swap(self, value, bit):
        return lax.ppermute(value, AXES, [(i, i ^ bit) for i in range(self.count)])


def masks_of(bits):
    masks = [0]
    for bit in bits:
        masks = masks + [m | bit for m in masks]
    return masks


class Order:
    def __init__(self):
        self.last = None

    def __call__(self, *values):
        held = values if self.last is None else (*values, self.last)
        held = lax.optimization_barrier(held)
        self.last = held[0]
        return held[: len(values)] if len(values) > 1 else held[0]


def behind(value, order=None):
    return value if order is None else order(value)


def plane_masks(lay, base):
    found = []
    for half, bits in enumerate((lay.x + lay.y, lay.y + lay.x)):
        masks = [m | half for m in base]
        for bit in bits:
            masks = masks + [m | bit for m in masks]
        found.append(masks)
    return found


def split_masks(lay):
    return [
        part
        for masks in plane_masks(lay, masks_of(lay.z))
        for part in (masks[: len(masks) // 2], masks[len(masks) // 2 :])
    ]


class GatherZ:
    def __init__(self, lay, block):
        self.lay = lay
        self.bits = list(reversed(lay.z))
        self.found = {0: block}

    def first(self, *order):
        bit = self.bits[0]
        self.found[bit] = self.lay.swap(behind(self.found[0], *order), bit)

    def second(self, *order):
        for bit in self.bits[1:]:
            self.found[bit] = self.lay.swap(behind(self.found[0], *order), bit)

    def third(self, order, everything=False):
        if everything:
            for bit, value in zip(self.bits, order(*[self.found[bit] for bit in self.bits])):
                self.found[bit] = value
        else:
            self.found[self.bits[0]] = order(self.found[self.bits[0]])
        for i, bit in enumerate(self.bits[1:], 1):
            for m in masks_of(self.bits[:i])[1:]:
                self.found[m | bit] = self.lay.swap(self.found[m], bit)

    def done(self, order):
        masks = masks_of(self.lay.z)
        return order(*[self.found[m] for m in masks])


class GatherPlane:
    def __init__(self, lay, *halves):
        self.lay, self.halves = lay, halves
        self.orders = (lay.x + lay.y, lay.y + lay.x)
        self.came = [lay.swap(h, bits[0]) for h, bits in zip(halves, self.orders)]

    def second(self, order):
        came = order(*self.came)
        self.held, self.came = [], []
        for held, got, bits in zip(self.halves, came, self.orders):
            held = jnp.concatenate([held, got], axis=0)
            for bit in bits[1:-1]:
                held = jnp.concatenate([held, self.lay.swap(held, bit)], axis=0)
            self.held.append(held)
            self.came.append(self.lay.swap(held, bits[-1]))

    def arrays(self):
        return [self.held[0], self.came[0], self.held[1], self.came[1]]

    def joined(self, order):
        came = order(*self.came)
        return jnp.concatenate([self.held[0], came[0], self.held[1], came[1]], axis=0)


def add_low(a, b):
    return (a.astype(F32) + b.astype(F32)).astype(BF16)


def fold(pairs, name="fold"):
    n = len(pairs)

    def body(*refs):
        ins, outs = refs[: 2 * n], refs[2 * n :]
        step = pl.program_id(0)
        for i in range(n):
            value = add_low(ins[2 * i][...], ins[2 * i + 1][...])

            def put(ref, value=value):
                ref[...] = value

            pl.when(step == 0)(functools.partial(put, outs[2 * i + 1]))
            pl.when(step == 1)(functools.partial(put, outs[2 * i]))

    def half(a):
        return (a.shape[0] // 2, *a.shape[1:])

    def spec(a, there):
        rest = (0,) * (a.ndim - 1)
        return pl.BlockSpec(half(a), (lambda i: (1 - i, *rest)) if there else (lambda i: (0, *rest)))

    flat = [a for pair in pairs for a in pair]
    outs = pl.pallas_call(
        body,
        name=name,
        grid=(2,),
        out_shape=tuple(jax.ShapeDtypeStruct(half(a), BF16) for a in flat),
        in_specs=[spec(a, True) for a in flat],
        out_specs=tuple(spec(a, False) for a in flat),
        compiler_params=params(FOLD_MEGABYTES),
        cost_estimate=cost(name),
    )(*flat)
    return [(outs[2 * i], outs[2 * i + 1]) for i in range(n)]


def fold_plane(pairs, wanted, name="fold_plane"):
    shape = (len(wanted) // 2, 2, *pairs[0][0].shape[1:])
    n = shape[0]

    def body(*refs):
        ins, outs = refs[:4], refs[4:]
        for place, i in enumerate(wanted):
            for h in range(2):
                outs[place // n][place % n, h] = add_low(ins[2 * h][i], ins[2 * h + 1][i])

    return pl.pallas_call(
        body,
        name=name,
        out_shape=(jax.ShapeDtypeStruct(shape, BF16),) * 2,
        in_specs=[VMEM_SPEC] * 4,
        out_specs=(VMEM_SPEC,) * 2,
        compiler_params=params(FOLD_MEGABYTES),
        cost_estimate=cost(name),
    )(*[a for pair in pairs for a in pair])


class ReducePlane:
    def __init__(self, lay, arrays):
        self.lay = lay
        self.kept = [arrays[0], arrays[2]]
        self.orders = (lay.x + lay.y, lay.y + lay.x)
        self.came = [lay.swap(a, bits[-1]) for a, bits in zip(arrays[1::2], self.orders)]

    def second(self, order, name="fold"):
        for level in reversed(range(len(self.orders[0]) - 1)):
            came = order(*self.came)
            found = fold(list(zip(self.kept, came)), name)
            flat = order(*[a for pair in found for a in pair])
            found = list(zip(flat[::2], flat[1::2]))
            self.kept = [kept for kept, _ in found]
            self.came = [
                self.lay.swap(sent, bits[level]) for (_, sent), bits in zip(found, self.orders)
            ]

    def pairs(self, order):
        return list(zip(self.kept, order(*self.came)))


class ReduceZ:
    def __init__(self, lay, kept, sent):
        self.lay = lay
        self.bits = list(lay.z)
        self.kept = kept
        self.came = lay.swap(sent, self.bits[0])

    def second(self, order):
        while len(self.bits) > 1:
            self.bits.pop(0)
            self.kept, sent = order(*fold([(self.kept, order(self.came))], "fold_z")[0])
            self.came = self.lay.swap(sent, self.bits[0])

    def last(self, order):
        return self.kept, order(self.came)


def fold_four(kept, came):
    n = kept.shape[0] // 4

    def body(kept_ref, came_ref, *outs):
        for i, out in enumerate(outs):
            out[...] = add_low(kept_ref[i * n : (i + 1) * n], came_ref[i * n : (i + 1) * n])

    return pl.pallas_call(
        body,
        name="fold_four",
        out_shape=(jax.ShapeDtypeStruct((n, *kept.shape[1:]), BF16),) * 4,
        in_specs=[VMEM_SPEC] * 2,
        out_specs=(VMEM_SPEC,) * 4,
        compiler_params=params(FOLD_MEGABYTES),
        cost_estimate=cost("fold_four"),
    )(kept, came)


def add_up(core, ends):
    rows = ends[0][0].shape[2]
    widths = [end[0].shape[-1] for end in ends]
    flat = [a for end in ends for a in end]

    def body(core_ref, *refs):
        first = core_ref[0] == 0
        ins = list(refs[:-2])
        at = 0
        for end, width in zip(ends, widths):
            used = [ins.pop(0)[0].astype(F32) for _ in end]
            if len(end) == 2:
                total = used[0] + used[1]
                low, high = total[0], total[1]
            else:
                low, high = used[0] + used[1], used[2] + used[3]
            refs[-2][:, at : at + width] = jnp.where(first, low, high)
            refs[-1][:, at : at + width] = jnp.where(first, high, low)
            at += width

    return pl.pallas_call(
        body,
        name="add_up",
        out_shape=(jax.ShapeDtypeStruct((rows, sum(widths)), F32),) * 2,
        in_specs=[SMEM_SPEC] + [VMEM_SPEC] * len(flat),
        out_specs=(VMEM_SPEC,) * 2,
        compiler_params=params(FOLD_MEGABYTES),
        cost_estimate=cost("add_up"),
    )(core, *flat)


def wait_for(order, *streams):
    values = [v for s in streams for v in (s.came if isinstance(s.came, list) else [s.came])]
    values = list(order(*values)) if len(values) > 1 else [order(values[0])]
    for s in streams:
        if isinstance(s.came, list):
            s.came = [values.pop(0) for _ in s.came]
        else:
            s.came = values.pop(0)


def low_first(lay):
    bits = lay.z
    masks = [0]
    for bit in reversed(bits):
        masks = masks + [m | bit for m in masks]
    return masks


SAID_FLOPS = {"shuffle": 10**10, "attn_fwd": 10**10, "down_back": 10**10, "residual": 10**10, "gated": 10**10, "fold_first": 5 * 10**9, "fold_next": 10**10}
FOLD_FLOPS = 10**9
FOLD_MEGABYTES = 16


def cost(name):
    flops = SAID_FLOPS.get(name, FOLD_FLOPS if name.startswith("fold") else 1)
    return pl.CostEstimate(flops=flops, bytes_accessed=1, transcendentals=0)


def near(*values):
    return [pltpu.with_memory_space_constraint(v, pltpu.VMEM) for v in values]


def params(megabytes):
    return pltpu.CompilerParams(vmem_limit_bytes=megabytes << 20)


def rows_spec(size, cols, last=None):
    return pl.BlockSpec((size, cols), lambda i: (i if last is None else jnp.minimum(i, last), 0))


def piece_of(i, pieces, steps, turn):
    block = lax.rem(i + steps // 2, steps) if turn else i
    return block // (steps // pieces), lax.rem(block, steps // pieces)


def piece_specs(pieces, steps, size, width, turn=False):
    def spec(q):
        def at(i):
            piece, block = piece_of(i, pieces, steps, turn)
            last = steps // pieces - 1
            return (jnp.where(piece == q, block, jnp.where(piece < q, 0, last)), 0)

        return pl.BlockSpec((size, width), at)

    return [spec(q) for q in range(pieces)]


def with_piece(refs, steps, body, turn=False):
    piece, _ = piece_of(pl.program_id(0), len(refs), steps, turn)
    for q, ref in enumerate(refs):
        pl.when(piece == q)(functools.partial(body, ref))


def row_chunks(total, size, body):
    def step(i, carry):
        body(pl.ds(pl.multiple_of(i * size, size), size))
        return carry

    lax.fori_loop(0, total // size, step, 0)


def make_mask(seq_ref, b, mask_ref):
    rows, cols = mask_ref.shape
    slots = seq_ref.shape[1]
    ends = []
    total = jnp.int32(0)
    for j in range(slots):
        total = total + seq_ref[b, j]
        ends.append(total)

    def body(at):
        t = lax.broadcasted_iota(jnp.int32, (at.size, cols), 0) + at.start
        s = lax.broadcasted_iota(jnp.int32, (at.size, cols), 1)
        seg_t = jnp.zeros_like(t)
        seg_s = jnp.zeros_like(s)
        for e in ends:
            seg_t = seg_t + (t >= e).astype(jnp.int32)
            seg_s = seg_s + (s >= e).astype(jnp.int32)
        seen = (s <= t) & (seg_t == seg_s) & (t < total)
        mask_ref[at, :] = jnp.where(seen, 0.5, 0.0).astype(F32)

    row_chunks(rows, 64, body)
    return total


def stacked(refs, start, size):
    return jnp.concatenate([r[:, start : start + size] for r in refs], axis=0)


def whole_specs(arrays):
    return [pl.BlockSpec(a.shape, lambda i: (0,) * a.ndim) for a in arrays]


def shuffle(index, masks, values):
    n, width = values[0].shape
    rows = width // len(masks)
    steps = n // 256
    count = len(values)

    def body(index_ref, masks_ref, *refs):
        ins, outs, order_ref = refs[:count], refs[count:-1], refs[-1]

        @pl.when(pl.program_id(0) == 0)
        def _():
            def fill(at):
                r = lax.broadcasted_iota(jnp.int32, (at.size, width), 0) + at.start
                c = lax.broadcasted_iota(jnp.int32, (at.size, width), 1)
                block = jnp.bitwise_xor(masks_ref[...], index_ref[0])
                here = (r // rows == block) & (r % rows == c % rows)
                order_ref[at, :] = jnp.where(here, 1.0, 0.0).astype(BF16)

            row_chunks(width, 128, fill)

        for i, o in zip(ins, outs):
            o[...] = dot_nn(i[...], order_ref[...]).astype(BF16)

    table = jnp.repeat(jnp.asarray(masks, jnp.int32), rows)[None]
    at = rows_spec(256, width)
    keep = pl.BlockSpec((width, width), lambda i: (0, 0))
    return pl.pallas_call(
        body,
        name="shuffle",
        grid=(steps,),
        out_shape=(*[pltpu.HBM(v.shape, BF16) for v in values], pltpu.HBM((width, width), BF16)),
        in_specs=[SMEM_SPEC, pl.BlockSpec((1, width), lambda i: (0, 0))] + [at] * count,
        out_specs=(*[at] * count, keep),
        compiler_params=params(20),
        cost_estimate=cost("shuffle"),
    )(index, table, *values)


def prepare(core, groups, gains):
    rows = groups[0][0].shape[0]
    flat = [w for group in groups for w in group]
    padded = [w.shape[1] // 2 + -(w.shape[1] // 2) % LANES for w in flat]
    n_in = len(flat)
    widths, at = [], 0
    for group in groups:
        widths.append(sum(padded[at : at + len(group)]))
        at += len(group)
    widths[0] += LANES

    def body(core_ref, one_ref, two_ref, *refs):
        ins, keeps, give_ref = refs[:n_in], refs[n_in:-1], refs[-1]
        first = core_ref[0] == 0
        place, start = 0, 0
        for number, (group, keep_ref) in enumerate(zip(groups, keeps)):
            at = 0
            for _ in group:
                value = ins[place][...]
                half = value.shape[1] // 2
                low, high = value[:, :half].astype(F32), value[:, half:].astype(F32)
                spare = padded[place] - half
                for ref, base, one, two in (
                    (keep_ref, 0, low, high),
                    (give_ref, start, high, low),
                ):
                    ref[:, base + at : base + at + half] = jnp.where(first, one, two).astype(BF16)
                    if spare:
                        zeros = jnp.zeros((rows, spare), BF16)
                        ref[:, base + at + half : base + at + half + spare] = zeros
                at += padded[place]
                place += 1
            if number == 0:
                lines = []
                for ref in (one_ref, two_ref):
                    gain = ref[...]
                    high = gain.astype(BF16).astype(F32)
                    lines += [high, gain - high]
                lines = jnp.concatenate(lines + [jnp.zeros((LANES - 4, rows), F32)], axis=0)
                turned = lines.T.astype(BF16)
                keep_ref[:, at : at + LANES] = turned
                give_ref[:, at : at + LANES] = turned
                at += LANES
            start += at

    out = [jax.ShapeDtypeStruct((rows, n), BF16) for n in [*widths, sum(widths)]]
    return pl.pallas_call(
        body,
        name="prepare",
        out_shape=tuple(out),
        in_specs=[SMEM_SPEC] + [VMEM_SPEC] * (n_in + 2),
        out_specs=(VMEM_SPEC,) * len(out),
        compiler_params=params(60),
    )(core, *[g[None] for g in gains], *flat)


def conclude(core, mine, came, places):
    rows = mine.shape[0]
    n = len(places) - 1

    def body(core_ref, mine_ref, came_ref, *refs):
        first = core_ref[0] == 0
        for (at, half), ref in zip(places[:n], refs):
            own, other = mine_ref[:, at : at + half], came_ref[:, at : at + half]
            ref[:, :half] = jnp.where(first, own, other)
            ref[:, half:] = jnp.where(first, other, own)
        at = places[n][0]
        own = mine_ref[:, at : at + LANES].T
        other = came_ref[:, at : at + LANES].T
        refs[n][...] = own[0:1] + other[0:1]
        refs[n + 1][...] = own[1:2]

    out = [jax.ShapeDtypeStruct((rows, 2 * half), F32) for _, half in places[:n]]
    out += [jax.ShapeDtypeStruct((1, rows), F32)] * 2
    return pl.pallas_call(
        body,
        name="conclude",
        out_shape=tuple(out),
        in_specs=[SMEM_SPEC, VMEM_SPEC, VMEM_SPEC],
        out_specs=(VMEM_SPEC,) * len(out),
        compiler_params=params(16),
    )(core, mine, came)


def attn_fwd(weights, seq, tok, dims):
    n_tok, width, buffers = tok.shape[0], tok.shape[1], seq.shape[0]
    length = n_tok // buffers
    nq, nv, cols = dims
    n_qkv = 2 * nq + nv
    n_in = len(weights)

    def body(seq_ref, tok_ref, *refs):
        w_in = refs[:n_in]
        normed_ref, qkv_ref, y_ref, dinv_ref, gain_ref = refs[n_in : n_in + 5]
        part_refs = refs[n_in + 5 : n_in + 5 + 2 * buffers]
        mask_ref = refs[n_in + 5 + 2 * buffers]
        w_gain = stacked(w_in, n_qkv + nv, LANES).astype(F32).T
        gain_ref[0:1, :] = w_gain[0:1] + w_gain[1:2]
        gain_ref[1:2, :] = w_gain[2:3] + w_gain[3:4]
        gain_ref[2:8, :] = jnp.zeros((6, width), F32)
        gain = gain_ref[0:1, :]

        def project(at):
            x = tok_ref[at, :].astype(F32)
            inverse = lax.rsqrt(jnp.mean(x * x, axis=-1, keepdims=True) + EPS)
            normed = (x * inverse * gain).astype(BF16)
            normed_ref[at, :] = normed
            qkv_ref[at, :] = dot_nn(normed, stacked(w_in, 0, n_qkv)).astype(BF16)

        row_chunks(n_tok, 256, project)

        for b in range(buffers):
            total = make_mask(seq_ref, b, mask_ref)
            base = b * length

            def pair(hp, carry):
                lane = lax.broadcasted_iota(jnp.int32, (1, LANES), 1)
                k = qkv_ref[base : base + length, nq : 2 * nq]
                v_at = pl.ds(pl.multiple_of(2 * nq + hp * LANES, LANES), LANES)
                v = qkv_ref[base : base + length, v_at]
                step = length // 2
                for tb in range(2):
                    rows = slice(base + tb * step, base + (tb + 1) * step)
                    seen = (tb + 1) * step
                    q = qkv_ref[rows, :nq] * jnp.asarray(0.25, BF16)
                    mask = mask_ref[tb * step : (tb + 1) * step, :seen]
                    row = lax.broadcasted_iota(jnp.int32, (step, 1), 0) + tb * step
                    pad = (row >= total).astype(F32)
                    found = []
                    for j in range(2):
                        k_h = jnp.where(lane // F == 2 * hp + j, k[:seen], jnp.zeros((), BF16))
                        v_h = jnp.where(lane // 64 == j, v[:seen], jnp.ones((), BF16))
                        one = dot_nt(q, k_h) + 1.0
                        share = ((one * one + 1.0) * mask).astype(BF16)
                        mixed = dot_nn(share, v_h)
                        inverse = 1.0 / (pltpu.roll(mixed, 64, 1) + pad)
                        found.append((mixed * inverse, inverse))
                    low = lane < 64
                    y_at = pl.ds(pl.multiple_of(hp * LANES, LANES), LANES)
                    y_ref[rows, y_at] = jnp.where(low, found[0][0], found[1][0]).astype(BF16)
                    dinv_ref[rows, y_at] = jnp.where(low, found[0][1], found[1][1])
                return carry

            lax.fori_loop(0, nv // LANES, pair, 0)
            for half in range(2):
                at = slice(base + half * (length // 2), base + (half + 1) * (length // 2))
                part = dot_nt(y_ref[at, :], stacked(w_in, n_qkv, nv))
                part_refs[2 * b + half][...] = part.astype(BF16)

    return pl.pallas_call(
        body,
        name="attn_fwd",
        out_shape=(
            pltpu.HBM((n_tok, width), BF16),
            pltpu.VMEM((n_tok, n_qkv), BF16),
            pltpu.VMEM((n_tok, nv), BF16),
            pltpu.VMEM((n_tok, nv), F32),
            jax.ShapeDtypeStruct((8, width), F32),
            *(jax.ShapeDtypeStruct((length // 2, width), BF16) for _ in range(2 * buffers)),
        ),
        in_specs=[SMEM_SPEC] + [VMEM_SPEC] * (1 + n_in),
        out_specs=(VMEM_SPEC,) * (5 + 2 * buffers),
        scratch_shapes=[pltpu.VMEM((length, length), F32)],
        compiler_params=params(28),
        cost_estimate=cost("attn_fwd"),
    )(seq, tok, *weights)


def residual(tok, part, came, gains):
    n_tok, width = tok.shape
    steps = 4
    size = n_tok // steps

    n = len(part)

    def body(tok_ref, *refs):
        part_refs, came_refs = refs[:n], refs[n : 2 * n]
        gain_ref, hres_ref, normed_ref = refs[2 * n :]
        gain = gain_ref[1:2, :]

        def rows(at, part_ref, came_ref):
            x = tok_ref[at, :].astype(F32)
            x = x + (part_ref[at, :].astype(F32) + came_ref[at, :].astype(F32))
            hres_ref[at, :] = x
            inverse = lax.rsqrt(jnp.mean(x * x, axis=-1, keepdims=True) + EPS)
            normed_ref[at, :] = (x * inverse * gain).astype(BF16)

        pairs = list(zip(part_refs, came_refs[n // 2 :] + came_refs[: n // 2]))
        with_piece(pairs, steps, lambda pair: row_chunks(size, 64, lambda at: rows(at, *pair)))

    at = rows_spec(size, width)
    return pl.pallas_call(
        body,
        name="residual",
        grid=(steps,),
        out_shape=(pltpu.VMEM((n_tok, width), F32), pltpu.VMEM((n_tok, width), BF16)),
        in_specs=[at]
        + piece_specs(n, steps, size, width)
        + piece_specs(n, steps, size, width, True)
        + [pl.BlockSpec((8, width), lambda i: (0, 0))],
        out_specs=(at, at),
        compiler_params=params(16),
        cost_estimate=cost("residual"),
    )(tok, *part, *came, gains)


def in_order(refs, places, rows):
    if places is None:
        return jnp.concatenate([r[...] for r in refs], axis=0)
    return jnp.concatenate([refs[j][i * rows : (i + 1) * rows, :] for j, i in places], axis=0)


def down_back(weights, places, rows, grad_out):
    n_tok, width = grad_out.shape
    cols = weights[0].shape[1]
    steps = 4
    size = n_tok // steps

    def body(grad_ref, *refs):
        w = in_order(refs[:-1], places, rows)
        refs[-1][...] = dot_nn(grad_ref[...], w).astype(BF16)

    return pl.pallas_call(
        body,
        name="down_back",
        grid=(steps,),
        out_shape=pltpu.VMEM((n_tok, cols), BF16),
        in_specs=[rows_spec(size, width)] + whole_specs(weights),
        out_specs=rows_spec(size, cols),
        compiler_params=params(20),
        cost_estimate=cost("down_back"),
    )(grad_out, *weights)


def gated(weights, normed, d_act):
    n_tok, width = normed.shape
    cols = d_act.shape[1]
    n_in = len(weights)
    steps = 4
    size = n_tok // steps

    def body(normed_ref, d_act_ref, *refs):
        act_ref, d_gate_ref, d_up_ref = refs[n_in:]
        x = normed_ref[...]
        gate = dot_nn(x, stacked(refs[:n_in], 0, cols))
        up = dot_nn(x, stacked(refs[:n_in], cols, cols))
        sig = 1.0 / (1.0 + jnp.exp(-gate))
        silu = gate * sig
        act_ref[...] = (silu * up).astype(BF16)
        d = d_act_ref[...].astype(F32)
        d_gate_ref[...] = (d * up * sig * (1.0 + gate * (1.0 - sig))).astype(BF16)
        d_up_ref[...] = (d * silu).astype(BF16)

    out = pltpu.VMEM((n_tok, cols), BF16)
    at = rows_spec(size, cols)
    return pl.pallas_call(
        body,
        name="gated",
        grid=(steps,),
        out_shape=(out, out, out),
        in_specs=[rows_spec(size, width), at] + whole_specs(weights),
        out_specs=(at, at, at),
        compiler_params=params(30),
        cost_estimate=cost("gated"),
    )(*near(normed, d_act), *weights)


def weight_grad(lefts, rights, gain=None, name="weight_grad", places=None, rows=0):
    n_tok, width = lefts[0].shape
    sizes = [r.shape[1] for r in rights]
    cols = sum(sizes) + (LANES if gain is not None else 0)
    n, pieces = len(lefts), 4
    chunk = width // pieces
    out_rows = chunk if places is None else width // 2
    extras, specs = [], []
    if gain is not None:
        weights, gains, other = gain
        extras = [gains, other, *weights]
        specs = [pl.BlockSpec((8, chunk), lambda i: (0, i))] * 2 + whole_specs(weights)

    def body(*refs):
        left_refs, right_refs = refs[:n], refs[n : 2 * n]
        ins, outs = refs[2 * n : 2 * n + len(extras)], refs[2 * n + len(extras) :]

        values = [dot_tn(left[...], right[...]) for left, right in zip(left_refs, right_refs)]

        def put(out, w_ref):
            start = 0
            for value, size in zip(values, sizes):
                out[:, start : start + size] = value.astype(BF16)
                start += size
            if gain is not None:
                one = values[0] * w_ref[:, : sizes[0]].astype(F32)
                one = jnp.sum(one, axis=-1, keepdims=True)
                two = jnp.sum(ins[1][...], axis=0, keepdims=True)
                lines = [ins[0][0:1, :], two, jnp.zeros((LANES - 2, chunk), F32)]
                turned = jnp.concatenate(lines).T
                lane = lax.broadcasted_iota(jnp.int32, turned.shape, 1)
                turned = jnp.where(lane == 0, one / turned, turned)
                out[:, cols - LANES :] = turned.astype(BF16)

        if places is not None:
            value = values[0].astype(BF16)
            for p, (j, i) in enumerate(places):
                at = p * rows % chunk

                @pl.when(pl.program_id(0) == p * rows // chunk)
                def _(j=j, i=i, at=at):
                    outs[j][i * rows : (i + 1) * rows, :] = value[at : at + rows]

            return

        for q, out in enumerate(outs):
            w_ref = ins[2 + q] if gain is not None else None
            pl.when(pl.program_id(0) == q)(functools.partial(put, out, w_ref))

    return pl.pallas_call(
        body,
        name=name,
        grid=(pieces,),
        out_shape=(jax.ShapeDtypeStruct((out_rows, cols), BF16),) * (width // out_rows),
        in_specs=[pl.BlockSpec((n_tok, chunk), lambda i: (0, i))] * n
        + [pl.BlockSpec(r.shape, lambda i: (0, 0)) for r in rights]
        + specs,
        out_specs=(pl.BlockSpec((out_rows, cols), lambda i: (0, 0)),) * (width // out_rows),
        compiler_params=params(26),
        cost_estimate=cost(name),
    )(*lefts, *near(*rights), *extras)


def sum_nt(weights, lefts, starts, pieces, name, places=None, rows=0):
    n_tok, cols = lefts[0].shape
    width = sum(w.shape[0] for w in weights)
    n, n_in = len(lefts), len(weights)
    steps = 4
    size = n_tok // steps

    def body(*refs):
        left_refs, w_refs, out_refs = refs[:n], refs[n : n + n_in], refs[n + n_in :]

        if places is not None:
            values = [dot_nt(left_refs[0][...], in_order(w_refs, places, rows))]
        else:
            values = []
            for w in w_refs:
                value = None
                for left, start in zip(left_refs, starts):
                    term = dot_nt(left[...], w[:, start : start + cols])
                    value = term if value is None else value + term
                values.append(value)

        def put(ref):
            at = 0
            for value in values:
                ref[:, at : at + value.shape[1]] = value.astype(BF16)
                at += value.shape[1]

        with_piece(out_refs, steps, put)

    return pl.pallas_call(
        body,
        name=name,
        grid=(steps,),
        out_shape=(jax.ShapeDtypeStruct((n_tok // pieces, width), BF16),) * pieces,
        in_specs=[rows_spec(size, cols)] * n + whole_specs(weights),
        out_specs=tuple(piece_specs(pieces, steps, size, width)),
        compiler_params=params(20),
        cost_estimate=cost(name),
    )(*near(*lefts), *weights)


def norm_back(weights, part, came, hres, grad_out, gains, dims):
    n_tok, width = hres.shape
    nq, nv, _ = dims
    n_qkv = 2 * nq + nv
    n_in = len(weights)
    steps = 4
    size = n_tok // steps
    n = len(part)

    def body(hres_ref, c_ref, gain_ref, *refs):
        part_refs, came_refs, refs = refs[:n], refs[n : 2 * n], refs[2 * n :]
        dh_ref, do_ref, dy_ref, gg_ref = refs[n_in:]
        gain = gain_ref[1:2, :]
        i = pl.program_id(0)

        @pl.when(i == 0)
        def _():
            gg_ref[...] = jnp.zeros_like(gg_ref)

        def rows(at, part_ref, came_ref):
            d = part_ref[at, :].astype(F32) + came_ref[at, :].astype(F32)
            h = hres_ref[at, :]
            inverse = lax.rsqrt(jnp.mean(h * h, axis=-1, keepdims=True) + EPS)
            hr = h * inverse
            gg_ref[...] += jnp.sum((d * hr).reshape(-1, 8, width), axis=0)
            dg = d * gain
            back = inverse * (dg - hr * jnp.mean(dg * hr, axis=-1, keepdims=True))
            dh = c_ref[at, :].astype(F32) + back

            @pl.when(i < steps // 2)
            def _():
                dh_ref[at, :] = dh

            do_ref[at, :] = dh.astype(BF16)

        pairs = list(zip(part_refs, came_refs[n // 2 :] + came_refs[: n // 2]))
        with_piece(pairs, steps, lambda pair: row_chunks(size, 64, lambda at: rows(at, *pair)))

        dy_ref[...] = dot_nn(do_ref[...], stacked(refs[:n_in], n_qkv, nv)).astype(BF16)

    at = rows_spec(size, width)
    keep = pl.BlockSpec((8, width), lambda i: (0, 0))
    return pl.pallas_call(
        body,
        name="norm_back",
        grid=(steps,),
        out_shape=(
            pltpu.VMEM((n_tok // 2, width), F32),
            pltpu.VMEM((n_tok, width), BF16),
            pltpu.VMEM((n_tok, nv), BF16),
            jax.ShapeDtypeStruct((8, width), F32),
        ),
        in_specs=[at, at, keep]
        + piece_specs(n, steps, size, width)
        + piece_specs(n, steps, size, width, True)
        + whole_specs(weights),
        out_specs=(
            rows_spec(size, width, last=steps // 2 - 1),
            at,
            rows_spec(size, nv),
            keep,
        ),
        compiler_params=params(20),
        cost_estimate=cost("norm_back"),
    )(*near(hres), grad_out, gains, *part, *came, *weights)


def attn_bwd(seq, qkv, y, dy, dinv, dims):
    n_tok, buffers = qkv.shape[0], seq.shape[0]
    length = n_tok // buffers
    nq, nv, _ = dims

    def body(seq_ref, qkv_ref, y_ref, dy_ref, dinv_ref, out_ref, mask_ref, dq_acc, dk_acc, dv_acc):
        for b in range(buffers):
            make_mask(seq_ref, b, mask_ref)
            base = b * length
            dq_acc[...] = jnp.zeros_like(dq_acc)
            dk_acc[...] = jnp.zeros_like(dk_acc)

            def pair(hp, carry):
                lane = lax.broadcasted_iota(jnp.int32, (1, LANES), 1)
                zero = jnp.zeros((), BF16)
                k = qkv_ref[base : base + length, nq : 2 * nq]
                v_at = pl.ds(pl.multiple_of(2 * nq + hp * LANES, LANES), LANES)
                y_at = pl.ds(pl.multiple_of(hp * LANES, LANES), LANES)
                v = qkv_ref[base : base + length, v_at]
                dv_acc[...] = jnp.zeros_like(dv_acc)
                step = length // 2
                for tb in range(2):
                    rows = slice(base + tb * step, base + (tb + 1) * step)
                    here = slice(tb * step, (tb + 1) * step)
                    seen = (tb + 1) * step
                    q = qkv_ref[rows, :nq] * jnp.asarray(0.25, BF16)
                    mask = mask_ref[here, :seen]
                    dyn = dy_ref[rows, y_at].astype(F32) * dinv_ref[rows, y_at]
                    dot_y = dyn * y_ref[rows, y_at].astype(F32)
                    dyn = dyn.astype(BF16)
                    for j in range(2):
                        mine = lane // F == 2 * hp + j
                        side = lane // 64 == j
                        k_h = jnp.where(mine, k[:seen], zero)
                        v_h = jnp.where(side, v[:seen], zero)
                        one = dot_nt(q, k_h) + 1.0
                        half_one = one * mask
                        weights = (half_one * one + mask).astype(BF16)
                        d_p = dot_nt(dyn, v_h)
                        shift = jnp.sum(jnp.where(side, dot_y, 0.0), axis=-1, keepdims=True)
                        d_a = ((d_p - shift) * half_one).astype(BF16)
                        dv_acc[:seen, :] += dot_tn(weights, jnp.where(side, dyn, zero))
                        dq_acc[here, :] += dot_nn(d_a, k_h)
                        dk_acc[:seen, :] += dot_tn(d_a, jnp.where(mine, q, zero))
                out_ref[base : base + length, v_at] = dv_acc[...].astype(BF16)
                return carry

            lax.fori_loop(0, nv // LANES, pair, 0)
            out_ref[base : base + length, :nq] = (dq_acc[...] * 0.5).astype(BF16)
            out_ref[base : base + length, nq : 2 * nq] = (dk_acc[...] * 2.0).astype(BF16)

    return pl.pallas_call(
        body,
        name="attn_bwd",
        out_shape=pltpu.VMEM(qkv.shape, BF16),
        in_specs=[SMEM_SPEC] + [VMEM_SPEC] * 4,
        out_specs=VMEM_SPEC,
        scratch_shapes=[
            pltpu.VMEM((length, length), F32),
            pltpu.VMEM((length, nq), F32),
            pltpu.VMEM((length, nq), F32),
            pltpu.VMEM((length, LANES), F32),
        ],
        compiler_params=params(20),
        cost_estimate=cost("attn_bwd"),
    )(seq, *near(qkv, y, dy, dinv))


def finish(part, came, tok, dh, gains, hres, out_part, out_came, placing):
    n_tok, width = part.shape
    steps = 2
    size = n_tok // steps

    def body(
        part_ref, came_ref, tok_ref, dh_ref, gain_ref, h_ref, op_ref, oc_ref, p_ref,
        grad_ref, out_ref, low_ref,
    ):
        gain = gain_ref[0:1, :]

        def rows(at):
            d = (part_ref[at, :].astype(F32) + came_ref[at, :].astype(F32)) * gain
            x = tok_ref[at, :].astype(F32)
            inverse = lax.rsqrt(jnp.mean(x * x, axis=-1, keepdims=True) + EPS)
            xr = x * inverse
            back = inverse * (d - xr * jnp.mean(d * xr, axis=-1, keepdims=True))
            low_ref[at, :] = (dh_ref[at, :] + back).astype(BF16)
            both = op_ref[at, :].astype(F32) + oc_ref[at, :].astype(F32)
            below = pl.ds(pl.multiple_of(size + at.start, 64), at.size)
            low_ref[below, :] = (h_ref[at, :] + both).astype(BF16)

        row_chunks(size, 64, rows)
        placed = dot_nt(low_ref[...], p_ref[...]).astype(BF16)
        grad_ref[...] = placed[:size]
        out_ref[...] = placed[size:]

    at = rows_spec(size, width)
    out = jax.ShapeDtypeStruct((n_tok, width), BF16)
    return pl.pallas_call(
        body,
        name="finish",
        grid=(steps,),
        out_shape=(out, out),
        in_specs=[at, at, at, at, pl.BlockSpec((8, width), lambda i: (0, 0)), at, at, at]
        + [pl.BlockSpec((width, width), lambda i: (0, 0))],
        out_specs=(at, at),
        scratch_shapes=[pltpu.VMEM((2 * size, width), BF16)],
        compiler_params=params(28),
        cost_estimate=cost("finish"),
    )(part, came, tok, *near(dh), gains, *near(hres), out_part, out_came, placing)


def local(
    lay,
    tokens,
    seq_lengths,
    w_query,
    w_key,
    w_value,
    w_output,
    w_gate,
    w_up,
    w_down,
    gain_attn,
    gain_mlp,
    cotangent,
):
    me = lax.axis_index(AXES).astype(jnp.int32)
    core = me % 2
    index = (me - core).reshape(1)
    rows, length = w_query.shape[0], tokens.shape[0]
    nq, nv, nf = w_query.shape[1] // 2, w_value.shape[1] // 2, w_gate.shape[1] // 2
    stride = nf + -nf % LANES
    order = Order()
    masks = split_masks(lay)
    flat_masks = sum(masks, [])
    both = sum(plane_masks(lay, [0]), [])
    places_z = {m | z: (j, i) for j, z in enumerate(masks_of(lay.z)) for i, m in enumerate(both)}
    places_z = [places_z[m] for m in flat_masks]

    def flat(arrays):
        return [a.reshape(-1, a.shape[-1]) for a in arrays]

    def blocks(arrays):
        return [a.reshape(-1, rows, a.shape[-1]) for a in arrays]
    dims = (nq, nv, 2 * nq + 2 * nv + LANES)

    keep_0, keep_gu, keep_d, give = prepare(
        core.reshape(1),
        [[w_query, w_key, w_value, w_output.T], [w_gate, w_up], [w_down.T]],
        [gain_attn, gain_mlp],
    )
    came = lay.swap(give, 1)
    tok_other, seq_other = lay.swap(tokens, 1), lay.swap(seq_lengths, 1)
    cot_other = lay.swap(cotangent, 1)
    came = order(came)
    at_d = dims[2] + 2 * stride

    def by_core(own, other):
        return jnp.where(core == 0, jnp.stack([own, other]), jnp.stack([other, own]))

    z_0 = GatherZ(lay, by_core(keep_0, came[:, : dims[2]]))
    z_0.first()
    z_0.second()
    halves_d = by_core(keep_d, came[:, at_d:])
    p_d = GatherPlane(lay, halves_d[:1], halves_d[1:])
    tok_other, seq_other, cot_other = order(tok_other, seq_other, cot_other)
    z_gu = GatherZ(lay, order(by_core(keep_gu, came[:, dims[2] : at_d])))
    z_gu.first()
    z_0.third(order)
    p_d.second(order)

    def halves(z):
        blocks = z.done(order)
        return [jnp.stack([b[h] for b in blocks]) for h in range(2)]

    p_0 = GatherPlane(lay, *halves(z_0))
    z_gu.second(order)
    held_d = p_d.joined(order)
    z_gu.third(order)
    p_0.second(order)
    z_d = GatherZ(lay, order(held_d))
    z_d.first()
    p_gu = GatherPlane(lay, *order(*halves(z_gu)))
    arrays_0 = order(*p_0.arrays())
    z_d.second(order)
    w_0 = flat(arrays_0)
    seq = jnp.concatenate([seq_lengths, seq_other], axis=0)
    tok = jnp.concatenate([tokens, tok_other], axis=0)
    grad_out = jnp.concatenate([cotangent, cot_other], axis=0)
    tok, grad_out, placing = order(*shuffle(index, flat_masks, [tok, grad_out]))
    z_d.third(order)
    p_gu.second(order)
    def swap_all(values):
        return [lay.swap(v, 1) for v in values]

    normed_one, qkv, y, dinv, gains, *part_o = attn_fwd(w_0, seq, tok, dims)
    part_o = order(*part_o)
    came_o = swap_all(part_o)
    w_d = z_d.done(order)
    if rows % 16:
        order_d = [j * len(both) + i for j, i in places_z]
        w_d = jnp.take(jnp.concatenate(w_d), jnp.asarray(order_d), axis=0)
        w_d, places_z = jnp.split(w_d, 4), None
    w_d = flat(w_d)
    d_act = order(down_back(w_d, places_z, rows, grad_out))
    w_gu = flat(order(*p_gu.arrays()))
    came_o = order(*came_o)
    hres, normed_two = residual(tok, part_o, came_o, gains)
    normed_two = order(normed_two)
    act, d_gate, d_up = order(*gated(w_gu, normed_two, d_act))

    def grad(lefts, rights, gain=None, name="weight_grad", places=None):
        return blocks(order(*weight_grad(lefts, rights, gain, name, places, rows)))

    z_order = low_first(lay)
    half_z = len(z_order) // 2
    places_r = {}
    for k, z in enumerate(z_order):
        for i, m in enumerate(both):
            places_r[m | z] = (k // half_z, (k % half_z) * len(both) + i)
    places_r = [places_r[m] for m in flat_masks]

    def down_grad():
        if rows % 16 == 0:
            return grad([grad_out], [act], name="grad_down", places=places_r)
        found = jnp.concatenate(grad([grad_out], [act], name="grad_down"))
        back = [0] * len(places_r)
        for p, (j, i) in enumerate(places_r):
            back[j * len(back) // 2 + i] = p
        return jnp.split(jnp.take(found, jnp.asarray(back), axis=0), 2)

    wanted = [masks_of(lay.z).index(m) for m in low_first(lay)]

    def along_z(stream, name="fold_plane"):
        return ReduceZ(lay, *order(*fold_plane(stream.pairs(order), wanted, name)))

    r_g = ReducePlane(lay, grad(near(normed_two), [d_gate], name="grad_gate"))
    d_up = order(d_up)
    part_n2 = order(*sum_nt(w_gu, [d_gate, d_up], [0, stride], 2, "d_norm2"))
    came_n2 = swap_all(part_n2)
    act = order(act)
    zr_d = ReduceZ(lay, *down_grad())
    r_g.second(order, "fold_first")
    came_n2 = order(*came_n2)
    d_h, d_o, d_y, gg_mlp = norm_back(w_0, part_n2, came_n2, hres, grad_out, gains, dims)
    d_y = order(d_y)
    outs_u = grad(near(normed_two, d_o), [d_up, y], name="grad_up")
    r_u = ReducePlane(lay, order(*outs_u))
    zr_g = along_z(r_g, "fold_next")
    d_qkv = order(attn_bwd(seq, qkv, y, order(d_y), dinv, dims))
    zr_d.second(order)
    outs_0 = grad([normed_one], [order(d_qkv)], (w_0, gains, gg_mlp), name="grad_attn")
    wait_for(order, zr_g)
    r_u.second(order)
    part_n1 = order(*sum_nt(w_0, [order(d_qkv)], [0], 2, "norm_one_part"))
    part_out = order(*sum_nt(w_d, [order(act)], [0], 2, "down", places_z, rows))
    zr_u = along_z(r_u)
    r_0 = ReducePlane(lay, order(*outs_0))
    last_d = order(*fold_four(*zr_d.last(order)))
    zr_u.second(order)
    r_0.second(order)
    r_d = ReducePlane(lay, order(*last_d))
    zr_0 = along_z(r_0)
    r_d.second(order)
    zr_0.second(order)
    zr_g.second(order)
    end_u = zr_u.last(order)
    came_rows = swap_all(order(part_n1[1], part_out[1]))
    end_d = [a for pair in r_d.pairs(order) for a in pair]
    came_rows = order(*came_rows)
    grad_tokens, layer_out = finish(
        part_n1[0], came_rows[0], tok, d_h, gains, hres, part_out[0], came_rows[1], placing
    )
    grad_tokens = order(grad_tokens)
    end_0 = zr_0.last(order)
    end_g = zr_g.last(order)
    mine, give = add_up(core.reshape(1), [end_0, end_d, end_g, end_u])
    came = lay.swap(give, 1)
    at = 2 * nq + nv
    at_d = at + LANES
    at_gu = at_d + stride
    places = [
        (0, nq),
        (nq, nq),
        (2 * nq, nv),
        (at_gu + 2 * stride, nv),
        (at_gu, nf),
        (at_gu + stride, nf),
        (at_d, nf),
        (at, LANES),
    ]
    *grads, g_one, g_two = conclude(core.reshape(1), mine, came, places)
    grads[3], grads[6] = grads[3].T, grads[6].T
    return (layer_out, grad_tokens, *grads, g_one[0], g_two[0])


def solution(mesh):
    rows, cols, flat = P(AXES, None), P(None, AXES), P(AXES)
    return jax.shard_map(
        functools.partial(local, Layout(mesh)),
        mesh=mesh,
        in_specs=(rows, rows, rows, rows, rows, cols, rows, rows, cols, flat, flat, rows),
        out_specs=(rows, rows, rows, rows, rows, cols, rows, rows, cols, flat, flat),
        check_vma=False,
    )
```

```python
import functools
import math

import jax
import jax.numpy as jnp
from jax import lax
from jax.experimental import pallas as pl
from jax.experimental.pallas import tpu as pltpu
from jax.sharding import PartitionSpec as P

H = 16
F = 16
EPS = 1e-05
AXES = ("dp", "fsdp")
LANES = 128
F32 = jnp.float32
BF16 = jnp.bfloat16

VMEM_SPEC = pl.BlockSpec(memory_space=pltpu.VMEM)
SMEM_SPEC = pl.BlockSpec(memory_space=pltpu.SMEM)
ANY_SPEC = pl.BlockSpec(memory_space=pl.ANY)


def dot_nn(a, b):
    return lax.dot_general(a, b, (((1,), (0,)), ((), ())), preferred_element_type=F32)


def dot_nt(a, b):
    return lax.dot_general(a, b, (((1,), (1,)), ((), ())), preferred_element_type=F32)


def dot_tn(a, b):
    return lax.dot_general(a, b, (((0,), (0,)), ((), ())), preferred_element_type=F32)


class Layout:
    def __init__(self, mesh):
        dp, fsdp = mesh.shape["dp"], mesh.shape["fsdp"]
        self.count = dp * fsdp
        x_bits = int(math.log2(fsdp)) - 1
        y_bits = int(math.log2(dp)) // 3
        all_bits = int(math.log2(self.count))
        self.x = [1 << (1 + i) for i in range(x_bits)]
        self.y = [1 << (1 + x_bits + i) for i in range(y_bits)]
        self.z = [1 << i for i in range(1 + x_bits + y_bits, all_bits)]

    def swap(self, value, bit):
        return lax.ppermute(value, AXES, [(i, i ^ bit) for i in range(self.count)])


def masks_of(bits):
    masks = [0]
    for bit in bits:
        masks = masks + [m | bit for m in masks]
    return masks


class Order:
    def __init__(self):
        self.last = None

    def __call__(self, *values):
        held = values if self.last is None else (*values, self.last)
        held = lax.optimization_barrier(held)
        self.last = held[0]
        return held[: len(values)] if len(values) > 1 else held[0]


def behind(value, order=None):
    return value if order is None else order(value)


def plane_masks(lay, base):
    found = []
    for half, bits in enumerate((lay.x + lay.y, lay.y + lay.x)):
        masks = [m | half for m in base]
        for bit in bits:
            masks = masks + [m | bit for m in masks]
        found.append(masks)
    return found


def split_masks(lay):
    return [
        part
        for masks in plane_masks(lay, masks_of(lay.z))
        for part in (masks[: len(masks) // 2], masks[len(masks) // 2 :])
    ]


class GatherZ:
    def __init__(self, lay, block):
        self.lay = lay
        self.bits = list(reversed(lay.z))
        self.found = {0: block}

    def first(self, *order):
        bit = self.bits[0]
        self.found[bit] = self.lay.swap(behind(self.found[0], *order), bit)

    def second(self, *order):
        for bit in self.bits[1:]:
            self.found[bit] = self.lay.swap(behind(self.found[0], *order), bit)

    def third(self, order, everything=False):
        if everything:
            for bit, value in zip(self.bits, order(*[self.found[bit] for bit in self.bits])):
                self.found[bit] = value
        else:
            self.found[self.bits[0]] = order(self.found[self.bits[0]])
        for i, bit in enumerate(self.bits[1:], 1):
            for m in masks_of(self.bits[:i])[1:]:
                self.found[m | bit] = self.lay.swap(self.found[m], bit)

    def done(self, order):
        masks = masks_of(self.lay.z)
        return order(*[self.found[m] for m in masks])


class GatherPlane:
    def __init__(self, lay, *halves):
        self.lay, self.halves = lay, halves
        self.orders = (lay.x + lay.y, lay.y + lay.x)
        self.came = [lay.swap(h, bits[0]) for h, bits in zip(halves, self.orders)]

    def second(self, order):
        came = order(*self.came)
        self.held, self.came = [], []
        for held, got, bits in zip(self.halves, came, self.orders):
            held = jnp.concatenate([held, got], axis=0)
            for bit in bits[1:-1]:
                held = jnp.concatenate([held, self.lay.swap(held, bit)], axis=0)
            self.held.append(held)
            self.came.append(self.lay.swap(held, bits[-1]))

    def arrays(self):
        return [self.held[0], self.came[0], self.held[1], self.came[1]]

    def joined(self, order):
        came = order(*self.came)
        return jnp.concatenate([self.held[0], came[0], self.held[1], came[1]], axis=0)


def add_low(a, b):
    return (a.astype(F32) + b.astype(F32)).astype(BF16)


def fold(pairs, name="fold"):
    n = len(pairs)

    def body(*refs):
        ins, outs = refs[: 2 * n], refs[2 * n :]
        step = pl.program_id(0)
        for i in range(n):
            value = add_low(ins[2 * i][...], ins[2 * i + 1][...])

            def put(ref, value=value):
                ref[...] = value

            pl.when(step == 0)(functools.partial(put, outs[2 * i + 1]))
            pl.when(step == 1)(functools.partial(put, outs[2 * i]))

    def half(a):
        return (a.shape[0] // 2, *a.shape[1:])

    def spec(a, there):
        rest = (0,) * (a.ndim - 1)
        return pl.BlockSpec(half(a), (lambda i: (1 - i, *rest)) if there else (lambda i: (0, *rest)))

    flat = [a for pair in pairs for a in pair]
    outs = pl.pallas_call(
        body,
        name=name,
        grid=(2,),
        out_shape=tuple(jax.ShapeDtypeStruct(half(a), BF16) for a in flat),
        in_specs=[spec(a, True) for a in flat],
        out_specs=tuple(spec(a, False) for a in flat),
        compiler_params=params(FOLD_MEGABYTES),
        cost_estimate=cost(name),
    )(*flat)
    return [(outs[2 * i], outs[2 * i + 1]) for i in range(n)]


def fold_plane(pairs, wanted, name="fold_plane"):
    shape = (len(wanted) // 2, 2, *pairs[0][0].shape[1:])
    n = shape[0]

    def body(*refs):
        ins, outs = refs[:4], refs[4:]
        for place, i in enumerate(wanted):
            for h in range(2):
                outs[place // n][place % n, h] = add_low(ins[2 * h][i], ins[2 * h + 1][i])

    return pl.pallas_call(
        body,
        name=name,
        out_shape=(jax.ShapeDtypeStruct(shape, BF16),) * 2,
        in_specs=[VMEM_SPEC] * 4,
        out_specs=(VMEM_SPEC,) * 2,
        compiler_params=params(FOLD_MEGABYTES),
        cost_estimate=cost(name),
    )(*[a for pair in pairs for a in pair])


class ReducePlane:
    def __init__(self, lay, arrays):
        self.lay = lay
        self.kept = [arrays[0], arrays[2]]
        self.orders = (lay.x + lay.y, lay.y + lay.x)
        self.came = [lay.swap(a, bits[-1]) for a, bits in zip(arrays[1::2], self.orders)]

    def second(self, order, name="fold"):
        for level in reversed(range(len(self.orders[0]) - 1)):
            came = order(*self.came)
            found = fold(list(zip(self.kept, came)), name)
            flat = order(*[a for pair in found for a in pair])
            found = list(zip(flat[::2], flat[1::2]))
            self.kept = [kept for kept, _ in found]
            self.came = [
                self.lay.swap(sent, bits[level]) for (_, sent), bits in zip(found, self.orders)
            ]

    def pairs(self, order):
        return list(zip(self.kept, order(*self.came)))


class ReduceZ:
    def __init__(self, lay, kept, sent):
        self.lay = lay
        self.bits = list(lay.z)
        self.kept = kept
        self.came = lay.swap(sent, self.bits[0])

    def second(self, order):
        while len(self.bits) > 1:
            self.bits.pop(0)
            self.kept, sent = order(*fold([(self.kept, order(self.came))], "fold_z")[0])
            self.came = self.lay.swap(sent, self.bits[0])

    def last(self, order):
        return self.kept, order(self.came)


def fold_four(kept, came):
    n = kept.shape[0] // 4

    def body(kept_ref, came_ref, *outs):
        for i, out in enumerate(outs):
            out[...] = add_low(kept_ref[i * n : (i + 1) * n], came_ref[i * n : (i + 1) * n])

    return pl.pallas_call(
        body,
        name="fold_four",
        out_shape=(jax.ShapeDtypeStruct((n, *kept.shape[1:]), BF16),) * 4,
        in_specs=[VMEM_SPEC] * 2,
        out_specs=(VMEM_SPEC,) * 4,
        compiler_params=params(FOLD_MEGABYTES),
        cost_estimate=cost("fold_four"),
    )(kept, came)


def add_up(core, ends):
    rows = ends[0][0].shape[2]
    widths = [end[0].shape[-1] for end in ends]
    flat = [a for end in ends for a in end]

    def body(core_ref, *refs):
        first = core_ref[0] == 0
        ins = list(refs[:-2])
        at = 0
        for end, width in zip(ends, widths):
            used = [ins.pop(0)[0].astype(F32) for _ in end]
            if len(end) == 2:
                total = used[0] + used[1]
                low, high = total[0], total[1]
            else:
                low, high = used[0] + used[1], used[2] + used[3]
            refs[-2][:, at : at + width] = jnp.where(first, low, high)
            refs[-1][:, at : at + width] = jnp.where(first, high, low)
            at += width

    return pl.pallas_call(
        body,
        name="add_up",
        out_shape=(jax.ShapeDtypeStruct((rows, sum(widths)), F32),) * 2,
        in_specs=[SMEM_SPEC] + [VMEM_SPEC] * len(flat),
        out_specs=(VMEM_SPEC,) * 2,
        compiler_params=params(FOLD_MEGABYTES),
        cost_estimate=cost("add_up"),
    )(core, *flat)


def wait_for(order, *streams):
    values = [v for s in streams for v in (s.came if isinstance(s.came, list) else [s.came])]
    values = list(order(*values)) if len(values) > 1 else [order(values[0])]
    for s in streams:
        if isinstance(s.came, list):
            s.came = [values.pop(0) for _ in s.came]
        else:
            s.came = values.pop(0)


def low_first(lay):
    bits = lay.z
    masks = [0]
    for bit in reversed(bits):
        masks = masks + [m | bit for m in masks]
    return masks


SAID_FLOPS = {"shuffle": 10**10, "attn_fwd": 10**10, "down_back": 10**10, "residual": 10**10, "gated": 10**10, "fold_first": 5 * 10**9, "fold_next": 10**9, "fold_far": 5 * 10**9}
FOLD_FLOPS = 10**9
FOLD_MEGABYTES = 16


def cost(name):
    flops = SAID_FLOPS.get(name, FOLD_FLOPS if name.startswith("fold") else 1)
    return pl.CostEstimate(flops=flops, bytes_accessed=1, transcendentals=0)


def near(*values):
    return [pltpu.with_memory_space_constraint(v, pltpu.VMEM) for v in values]


def params(megabytes):
    return pltpu.CompilerParams(vmem_limit_bytes=megabytes << 20)


def rows_spec(size, cols, last=None):
    return pl.BlockSpec((size, cols), lambda i: (i if last is None else jnp.minimum(i, last), 0))


def piece_of(i, pieces, steps, turn):
    block = lax.rem(i + steps // 2, steps) if turn else i
    return block // (steps // pieces), lax.rem(block, steps // pieces)


def piece_specs(pieces, steps, size, width, turn=False):
    def spec(q):
        def at(i):
            piece, block = piece_of(i, pieces, steps, turn)
            last = steps // pieces - 1
            return (jnp.where(piece == q, block, jnp.where(piece < q, 0, last)), 0)

        return pl.BlockSpec((size, width), at)

    return [spec(q) for q in range(pieces)]


def with_piece(refs, steps, body, turn=False):
    piece, _ = piece_of(pl.program_id(0), len(refs), steps, turn)
    for q, ref in enumerate(refs):
        pl.when(piece == q)(functools.partial(body, ref))


def row_chunks(total, size, body):
    def step(i, carry):
        body(pl.ds(pl.multiple_of(i * size, size), size))
        return carry

    lax.fori_loop(0, total // size, step, 0)


def make_mask(seq_ref, b, mask_ref):
    rows, cols = mask_ref.shape
    slots = seq_ref.shape[1]
    ends = []
    total = jnp.int32(0)
    for j in range(slots):
        total = total + seq_ref[b, j]
        ends.append(total)

    def body(at):
        t = lax.broadcasted_iota(jnp.int32, (at.size, cols), 0) + at.start
        s = lax.broadcasted_iota(jnp.int32, (at.size, cols), 1)
        seg_t = jnp.zeros_like(t)
        seg_s = jnp.zeros_like(s)
        for e in ends:
            seg_t = seg_t + (t >= e).astype(jnp.int32)
            seg_s = seg_s + (s >= e).astype(jnp.int32)
        seen = (s <= t) & (seg_t == seg_s) & (t < total)
        mask_ref[at, :] = jnp.where(seen, 0.5, 0.0).astype(F32)

    row_chunks(rows, 64, body)
    return total


def stacked(refs, start, size):
    return jnp.concatenate([r[:, start : start + size] for r in refs], axis=0)


def whole_specs(arrays):
    return [pl.BlockSpec(a.shape, lambda i: (0,) * a.ndim) for a in arrays]


def shuffle(index, masks, values):
    n, width = values[0].shape
    rows = width // len(masks)
    steps = n // 256
    count = len(values)

    def body(index_ref, masks_ref, *refs):
        ins, outs, order_ref = refs[:count], refs[count:-1], refs[-1]

        @pl.when(pl.program_id(0) == 0)
        def _():
            def fill(at):
                r = lax.broadcasted_iota(jnp.int32, (at.size, width), 0) + at.start
                c = lax.broadcasted_iota(jnp.int32, (at.size, width), 1)
                block = jnp.bitwise_xor(masks_ref[...], index_ref[0])
                here = (r // rows == block) & (r % rows == c % rows)
                order_ref[at, :] = jnp.where(here, 1.0, 0.0).astype(BF16)

            row_chunks(width, 128, fill)

        for i, o in zip(ins, outs):
            o[...] = dot_nn(i[...], order_ref[...]).astype(BF16)

    table = jnp.repeat(jnp.asarray(masks, jnp.int32), rows)[None]
    at = rows_spec(256, width)
    keep = pl.BlockSpec((width, width), lambda i: (0, 0))
    return pl.pallas_call(
        body,
        name="shuffle",
        grid=(steps,),
        out_shape=(*[pltpu.HBM(v.shape, BF16) for v in values], pltpu.HBM((width, width), BF16)),
        in_specs=[SMEM_SPEC, pl.BlockSpec((1, width), lambda i: (0, 0))] + [at] * count,
        out_specs=(*[at] * count, keep),
        compiler_params=params(20),
        cost_estimate=cost("shuffle"),
    )(index, table, *values)


def prepare(core, groups, gains):
    rows = groups[0][0].shape[0]
    flat = [w for group in groups for w in group]
    padded = [w.shape[1] // 2 + -(w.shape[1] // 2) % LANES for w in flat]
    n_in = len(flat)
    widths, at = [], 0
    for group in groups:
        widths.append(sum(padded[at : at + len(group)]))
        at += len(group)
    widths[0] += LANES

    def body(core_ref, one_ref, two_ref, *refs):
        ins, keeps, give_ref = refs[:n_in], refs[n_in:-1], refs[-1]
        first = core_ref[0] == 0
        place, start = 0, 0
        for number, (group, keep_ref) in enumerate(zip(groups, keeps)):
            at = 0
            for _ in group:
                value = ins[place][...]
                half = value.shape[1] // 2
                low, high = value[:, :half].astype(F32), value[:, half:].astype(F32)
                spare = padded[place] - half
                for ref, base, one, two in (
                    (keep_ref, 0, low, high),
                    (give_ref, start, high, low),
                ):
                    ref[:, base + at : base + at + half] = jnp.where(first, one, two).astype(BF16)
                    if spare:
                        zeros = jnp.zeros((rows, spare), BF16)
                        ref[:, base + at + half : base + at + half + spare] = zeros
                at += padded[place]
                place += 1
            if number == 0:
                lines = []
                for ref in (one_ref, two_ref):
                    gain = ref[...]
                    high = gain.astype(BF16).astype(F32)
                    lines += [high, gain - high]
                lines = jnp.concatenate(lines + [jnp.zeros((LANES - 4, rows), F32)], axis=0)
                turned = lines.T.astype(BF16)
                keep_ref[:, at : at + LANES] = turned
                give_ref[:, at : at + LANES] = turned
                at += LANES
            start += at

    out = [jax.ShapeDtypeStruct((rows, n), BF16) for n in [*widths, sum(widths)]]
    return pl.pallas_call(
        body,
        name="prepare",
        out_shape=tuple(out),
        in_specs=[SMEM_SPEC] + [VMEM_SPEC] * (n_in + 2),
        out_specs=(VMEM_SPEC,) * len(out),
        compiler_params=params(60),
    )(core, *[g[None] for g in gains], *flat)


def conclude(core, mine, came, places):
    rows = mine.shape[0]
    n = len(places) - 1

    def body(core_ref, mine_ref, came_ref, *refs):
        first = core_ref[0] == 0
        for segments, ref in zip(places[:n], refs):
            half, done = sum(size for _, size in segments), 0
            for at, size in segments:
                own, other = mine_ref[:, at : at + size], came_ref[:, at : at + size]
                ref[:, done : done + size] = jnp.where(first, own, other)
                ref[:, half + done : half + done + size] = jnp.where(first, other, own)
                done += size
        at = places[n][0][0]
        own = mine_ref[:, at : at + LANES].T
        other = came_ref[:, at : at + LANES].T
        refs[n][...] = own[0:1] + other[0:1]
        refs[n + 1][...] = own[1:2]

    halves = [sum(size for _, size in segments) for segments in places[:n]]
    out = [jax.ShapeDtypeStruct((rows, 2 * half), F32) for half in halves]
    out += [jax.ShapeDtypeStruct((1, rows), F32)] * 2
    return pl.pallas_call(
        body,
        name="conclude",
        out_shape=tuple(out),
        in_specs=[SMEM_SPEC, VMEM_SPEC, VMEM_SPEC],
        out_specs=(VMEM_SPEC,) * len(out),
        compiler_params=params(16),
    )(core, mine, came)


def attn_fwd(weights, seq, tok, dims):
    n_tok, width, buffers = tok.shape[0], tok.shape[1], seq.shape[0]
    length = n_tok // buffers
    nq, nv, cols = dims
    n_qkv = 2 * nq + nv
    n_in = len(weights)

    def body(seq_ref, tok_ref, *refs):
        w_in = refs[:n_in]
        normed_ref, qkv_ref, y_ref, dinv_ref, gain_ref = refs[n_in : n_in + 5]
        part_refs = refs[n_in + 5 : n_in + 5 + 2 * buffers]
        mask_ref = refs[n_in + 5 + 2 * buffers]
        w_gain = stacked(w_in, n_qkv + nv, LANES).astype(F32).T
        gain_ref[0:1, :] = w_gain[0:1] + w_gain[1:2]
        gain_ref[1:2, :] = w_gain[2:3] + w_gain[3:4]
        gain_ref[2:8, :] = jnp.zeros((6, width), F32)
        gain = gain_ref[0:1, :]

        def project(at):
            x = tok_ref[at, :].astype(F32)
            inverse = lax.rsqrt(jnp.mean(x * x, axis=-1, keepdims=True) + EPS)
            normed = (x * inverse * gain).astype(BF16)
            normed_ref[at, :] = normed
            qkv_ref[at, :] = dot_nn(normed, stacked(w_in, 0, n_qkv)).astype(BF16)

        row_chunks(n_tok, 256, project)

        for b in range(buffers):
            total = make_mask(seq_ref, b, mask_ref)
            base = b * length

            def pair(hp, carry):
                lane = lax.broadcasted_iota(jnp.int32, (1, LANES), 1)
                k = qkv_ref[base : base + length, nq : 2 * nq]
                v_at = pl.ds(pl.multiple_of(2 * nq + hp * LANES, LANES), LANES)
                v = qkv_ref[base : base + length, v_at]
                step = length // 2
                for tb in range(2):
                    rows = slice(base + tb * step, base + (tb + 1) * step)
                    seen = (tb + 1) * step
                    q = qkv_ref[rows, :nq] * jnp.asarray(0.25, BF16)
                    mask = mask_ref[tb * step : (tb + 1) * step, :seen]
                    row = lax.broadcasted_iota(jnp.int32, (step, 1), 0) + tb * step
                    pad = (row >= total).astype(F32)
                    found = []
                    for j in range(2):
                        k_h = jnp.where(lane // F == 2 * hp + j, k[:seen], jnp.zeros((), BF16))
                        v_h = jnp.where(lane // 64 == j, v[:seen], jnp.ones((), BF16))
                        one = dot_nt(q, k_h) + 1.0
                        share = ((one * one + 1.0) * mask).astype(BF16)
                        mixed = dot_nn(share, v_h)
                        inverse = 1.0 / (pltpu.roll(mixed, 64, 1) + pad)
                        found.append((mixed * inverse, inverse))
                    low = lane < 64
                    y_at = pl.ds(pl.multiple_of(hp * LANES, LANES), LANES)
                    y_ref[rows, y_at] = jnp.where(low, found[0][0], found[1][0]).astype(BF16)
                    dinv_ref[rows, y_at] = jnp.where(low, found[0][1], found[1][1])
                return carry

            lax.fori_loop(0, nv // LANES, pair, 0)
            for half in range(2):
                at = slice(base + half * (length // 2), base + (half + 1) * (length // 2))
                part = dot_nt(y_ref[at, :], stacked(w_in, n_qkv, nv))
                part_refs[2 * b + half][...] = part.astype(BF16)

    return pl.pallas_call(
        body,
        name="attn_fwd",
        out_shape=(
            pltpu.HBM((n_tok, width), BF16),
            pltpu.VMEM((n_tok, n_qkv), BF16),
            pltpu.VMEM((n_tok, nv), BF16),
            pltpu.VMEM((n_tok, nv), F32),
            jax.ShapeDtypeStruct((8, width), F32),
            *(jax.ShapeDtypeStruct((length // 2, width), BF16) for _ in range(2 * buffers)),
        ),
        in_specs=[SMEM_SPEC] + [VMEM_SPEC] * (1 + n_in),
        out_specs=(VMEM_SPEC,) * (5 + 2 * buffers),
        scratch_shapes=[pltpu.VMEM((length, length), F32)],
        compiler_params=params(28),
        cost_estimate=cost("attn_fwd"),
    )(seq, tok, *weights)


def residual(tok, part, came, gains):
    n_tok, width = tok.shape
    steps = 4
    size = n_tok // steps

    n = len(part)

    def body(tok_ref, *refs):
        part_refs, came_refs = refs[:n], refs[n : 2 * n]
        gain_ref, hres_ref, normed_ref = refs[2 * n :]
        gain = gain_ref[1:2, :]

        def rows(at, part_ref, came_ref):
            x = tok_ref[at, :].astype(F32)
            x = x + (part_ref[at, :].astype(F32) + came_ref[at, :].astype(F32))
            hres_ref[at, :] = x
            inverse = lax.rsqrt(jnp.mean(x * x, axis=-1, keepdims=True) + EPS)
            normed_ref[at, :] = (x * inverse * gain).astype(BF16)

        pairs = list(zip(part_refs, came_refs[n // 2 :] + came_refs[: n // 2]))
        with_piece(pairs, steps, lambda pair: row_chunks(size, 64, lambda at: rows(at, *pair)))

    at = rows_spec(size, width)
    return pl.pallas_call(
        body,
        name="residual",
        grid=(steps,),
        out_shape=(pltpu.VMEM((n_tok, width), F32), pltpu.VMEM((n_tok, width), BF16)),
        in_specs=[at]
        + piece_specs(n, steps, size, width)
        + piece_specs(n, steps, size, width, True)
        + [pl.BlockSpec((8, width), lambda i: (0, 0))],
        out_specs=(at, at),
        compiler_params=params(16),
        cost_estimate=cost("residual"),
    )(tok, *part, *came, gains)


def in_order(refs, places, rows):
    if places is None:
        return jnp.concatenate([r[...] for r in refs], axis=0)
    return jnp.concatenate([refs[j][i * rows : (i + 1) * rows, :] for j, i in places], axis=0)


def down_back(weights, places, rows, grad_out):
    n_tok, width = grad_out.shape
    cols = weights[0].shape[1]
    steps = 4
    size = n_tok // steps

    def body(grad_ref, *refs):
        w = in_order(refs[:-1], places, rows)
        refs[-1][...] = dot_nn(grad_ref[...], w).astype(BF16)

    return pl.pallas_call(
        body,
        name="down_back",
        grid=(steps,),
        out_shape=pltpu.VMEM((n_tok, cols), BF16),
        in_specs=[rows_spec(size, width)] + whole_specs(weights),
        out_specs=rows_spec(size, cols),
        compiler_params=params(20),
        cost_estimate=cost("down_back"),
    )(grad_out, *weights)


def gated(weights, normed, d_act, first):
    n_tok, width = normed.shape
    cols = d_act.shape[1]
    n_in = len(weights)
    steps = 4
    size = n_tok // steps

    def body(normed_ref, d_act_ref, *refs):
        act_ref, rest_ref, d_gate_ref, d_up_ref = refs[n_in:]
        x = normed_ref[...]
        gate = dot_nn(x, stacked(refs[:n_in], 0, cols))
        up = dot_nn(x, stacked(refs[:n_in], cols, cols))
        sig = 1.0 / (1.0 + jnp.exp(-gate))
        silu = gate * sig
        act = (silu * up).astype(BF16)
        act_ref[...] = act[:, :first]
        rest_ref[...] = act[:, first:]
        d = d_act_ref[...].astype(F32)
        d_gate_ref[...] = (d * up * sig * (1.0 + gate * (1.0 - sig))).astype(BF16)
        d_up_ref[...] = (d * silu).astype(BF16)

    parts = (first, cols - first, cols, cols)
    return pl.pallas_call(
        body,
        name="gated",
        grid=(steps,),
        out_shape=tuple(pltpu.VMEM((n_tok, c), BF16) for c in parts),
        in_specs=[rows_spec(size, width), rows_spec(size, cols)] + whole_specs(weights),
        out_specs=tuple(rows_spec(size, c) for c in parts),
        compiler_params=params(30),
        cost_estimate=cost("gated"),
    )(*near(normed, d_act), *weights)


def weight_grad(lefts, rights, gain=None, name="weight_grad", places=None, rows=0):
    n_tok, width = lefts[0].shape
    sizes = [r.shape[1] for r in rights]
    cols = sum(sizes) + (LANES if gain is not None else 0)
    n, pieces = len(lefts), 4
    chunk = width // pieces
    out_rows = chunk if places is None else width // 2
    extras, specs = [], []
    if gain is not None:
        weights, gains, other = gain
        extras = [gains, other, *weights]
        specs = [pl.BlockSpec((8, chunk), lambda i: (0, i))] * 2 + whole_specs(weights)

    def body(*refs):
        left_refs, right_refs = refs[:n], refs[n : 2 * n]
        ins, outs = refs[2 * n : 2 * n + len(extras)], refs[2 * n + len(extras) :]

        values = [dot_tn(left[...], right[...]) for left, right in zip(left_refs, right_refs)]

        def put(out, w_ref):
            start = 0
            for value, size in zip(values, sizes):
                out[:, start : start + size] = value.astype(BF16)
                start += size
            if gain is not None:
                one = values[0] * w_ref[:, : sizes[0]].astype(F32)
                one = jnp.sum(one, axis=-1, keepdims=True)
                two = jnp.sum(ins[1][...], axis=0, keepdims=True)
                lines = [ins[0][0:1, :], two, jnp.zeros((LANES - 2, chunk), F32)]
                turned = jnp.concatenate(lines).T
                lane = lax.broadcasted_iota(jnp.int32, turned.shape, 1)
                turned = jnp.where(lane == 0, one / turned, turned)
                out[:, cols - LANES :] = turned.astype(BF16)

        if places is not None:
            value = values[0].astype(BF16)
            for p, (j, i) in enumerate(places):
                at = p * rows % chunk

                @pl.when(pl.program_id(0) == p * rows // chunk)
                def _(j=j, i=i, at=at):
                    outs[j][i * rows : (i + 1) * rows, :] = value[at : at + rows]

            return

        for q, out in enumerate(outs):
            w_ref = ins[2 + q] if gain is not None else None
            pl.when(pl.program_id(0) == q)(functools.partial(put, out, w_ref))

    return pl.pallas_call(
        body,
        name=name,
        grid=(pieces,),
        out_shape=(jax.ShapeDtypeStruct((out_rows, cols), BF16),) * (width // out_rows),
        in_specs=[pl.BlockSpec((n_tok, chunk), lambda i: (0, i))] * n
        + [pl.BlockSpec(r.shape, lambda i: (0, 0)) for r in rights]
        + specs,
        out_specs=(pl.BlockSpec((out_rows, cols), lambda i: (0, 0)),) * (width // out_rows),
        compiler_params=params(26),
        cost_estimate=cost(name),
    )(*lefts, *near(*rights), *extras)


def sum_nt(weights, lefts, starts, pieces, name, places=None, rows=0):
    n_tok = lefts[0].shape[0]
    width = sum(w.shape[0] for w in weights)
    n, n_in = len(lefts), len(weights)
    steps = 4
    size = n_tok // steps

    def body(*refs):
        left_refs, w_refs, out_refs = refs[:n], refs[n : n + n_in], refs[n + n_in :]

        if places is not None:
            left = jnp.concatenate([ref[...] for ref in left_refs], axis=1)
            values = [dot_nt(left, in_order(w_refs, places, rows))]
        else:
            values = []
            for w in w_refs:
                value = None
                for left, start in zip(left_refs, starts):
                    term = dot_nt(left[...], w[:, start : start + left.shape[1]])
                    value = term if value is None else value + term
                values.append(value)

        def put(ref):
            at = 0
            for value in values:
                ref[:, at : at + value.shape[1]] = value.astype(BF16)
                at += value.shape[1]

        with_piece(out_refs, steps, put)

    return pl.pallas_call(
        body,
        name=name,
        grid=(steps,),
        out_shape=(jax.ShapeDtypeStruct((n_tok // pieces, width), BF16),) * pieces,
        in_specs=[rows_spec(size, x.shape[1]) for x in lefts] + whole_specs(weights),
        out_specs=tuple(piece_specs(pieces, steps, size, width)),
        compiler_params=params(20),
        cost_estimate=cost(name),
    )(*near(*lefts), *weights)


def norm_back(weights, part, came, hres, grad_out, gains, dims):
    n_tok, width = hres.shape
    nq, nv, _ = dims
    n_qkv = 2 * nq + nv
    n_in = len(weights)
    steps = 4
    size = n_tok // steps
    n = len(part)

    def body(hres_ref, c_ref, gain_ref, *refs):
        part_refs, came_refs, refs = refs[:n], refs[n : 2 * n], refs[2 * n :]
        dh_ref, do_ref, dy_ref, gg_ref = refs[n_in:]
        gain = gain_ref[1:2, :]
        i = pl.program_id(0)

        @pl.when(i == 0)
        def _():
            gg_ref[...] = jnp.zeros_like(gg_ref)

        def rows(at, part_ref, came_ref):
            d = part_ref[at, :].astype(F32) + came_ref[at, :].astype(F32)
            h = hres_ref[at, :]
            inverse = lax.rsqrt(jnp.mean(h * h, axis=-1, keepdims=True) + EPS)
            hr = h * inverse
            gg_ref[...] += jnp.sum((d * hr).reshape(-1, 8, width), axis=0)
            dg = d * gain
            back = inverse * (dg - hr * jnp.mean(dg * hr, axis=-1, keepdims=True))
            dh = c_ref[at, :].astype(F32) + back

            @pl.when(i < steps // 2)
            def _():
                dh_ref[at, :] = dh

            do_ref[at, :] = dh.astype(BF16)

        pairs = list(zip(part_refs, came_refs[n // 2 :] + came_refs[: n // 2]))
        with_piece(pairs, steps, lambda pair: row_chunks(size, 64, lambda at: rows(at, *pair)))

        dy_ref[...] = dot_nn(do_ref[...], stacked(refs[:n_in], n_qkv, nv)).astype(BF16)

    at = rows_spec(size, width)
    keep = pl.BlockSpec((8, width), lambda i: (0, 0))
    return pl.pallas_call(
        body,
        name="norm_back",
        grid=(steps,),
        out_shape=(
            pltpu.VMEM((n_tok // 2, width), F32),
            pltpu.VMEM((n_tok, width), BF16),
            pltpu.VMEM((n_tok, nv), BF16),
            jax.ShapeDtypeStruct((8, width), F32),
        ),
        in_specs=[at, at, keep]
        + piece_specs(n, steps, size, width)
        + piece_specs(n, steps, size, width, True)
        + whole_specs(weights),
        out_specs=(
            rows_spec(size, width, last=steps // 2 - 1),
            at,
            rows_spec(size, nv),
            keep,
        ),
        compiler_params=params(20),
        cost_estimate=cost("norm_back"),
    )(*near(hres), grad_out, gains, *part, *came, *weights)


def attn_bwd(seq, qkv, y, dy, dinv, dims):
    n_tok, buffers = qkv.shape[0], seq.shape[0]
    length = n_tok // buffers
    nq, nv, _ = dims

    def body(seq_ref, qkv_ref, y_ref, dy_ref, dinv_ref, out_ref, mask_ref, dq_acc, dk_acc, dv_acc):
        for b in range(buffers):
            make_mask(seq_ref, b, mask_ref)
            base = b * length
            dq_acc[...] = jnp.zeros_like(dq_acc)
            dk_acc[...] = jnp.zeros_like(dk_acc)

            def pair(hp, carry):
                lane = lax.broadcasted_iota(jnp.int32, (1, LANES), 1)
                zero = jnp.zeros((), BF16)
                k = qkv_ref[base : base + length, nq : 2 * nq]
                v_at = pl.ds(pl.multiple_of(2 * nq + hp * LANES, LANES), LANES)
                y_at = pl.ds(pl.multiple_of(hp * LANES, LANES), LANES)
                v = qkv_ref[base : base + length, v_at]
                dv_acc[...] = jnp.zeros_like(dv_acc)
                step = length // 2
                for tb in range(2):
                    rows = slice(base + tb * step, base + (tb + 1) * step)
                    here = slice(tb * step, (tb + 1) * step)
                    seen = (tb + 1) * step
                    q = qkv_ref[rows, :nq] * jnp.asarray(0.25, BF16)
                    mask = mask_ref[here, :seen]
                    dyn = dy_ref[rows, y_at].astype(F32) * dinv_ref[rows, y_at]
                    dot_y = dyn * y_ref[rows, y_at].astype(F32)
                    dyn = dyn.astype(BF16)
                    for j in range(2):
                        mine = lane // F == 2 * hp + j
                        side = lane // 64 == j
                        k_h = jnp.where(mine, k[:seen], zero)
                        v_h = jnp.where(side, v[:seen], zero)
                        one = dot_nt(q, k_h) + 1.0
                        half_one = one * mask
                        weights = (half_one * one + mask).astype(BF16)
                        d_p = dot_nt(dyn, v_h)
                        shift = jnp.sum(jnp.where(side, dot_y, 0.0), axis=-1, keepdims=True)
                        d_a = ((d_p - shift) * half_one).astype(BF16)
                        dv_acc[:seen, :] += dot_tn(weights, jnp.where(side, dyn, zero))
                        dq_acc[here, :] += dot_nn(d_a, k_h)
                        dk_acc[:seen, :] += dot_tn(d_a, jnp.where(mine, q, zero))
                out_ref[base : base + length, v_at] = dv_acc[...].astype(BF16)
                return carry

            lax.fori_loop(0, nv // LANES, pair, 0)
            out_ref[base : base + length, :nq] = (dq_acc[...] * 0.5).astype(BF16)
            out_ref[base : base + length, nq : 2 * nq] = (dk_acc[...] * 2.0).astype(BF16)

    return pl.pallas_call(
        body,
        name="attn_bwd",
        out_shape=pltpu.VMEM(qkv.shape, BF16),
        in_specs=[SMEM_SPEC] + [VMEM_SPEC] * 4,
        out_specs=VMEM_SPEC,
        scratch_shapes=[
            pltpu.VMEM((length, length), F32),
            pltpu.VMEM((length, nq), F32),
            pltpu.VMEM((length, nq), F32),
            pltpu.VMEM((length, LANES), F32),
        ],
        compiler_params=params(20),
        cost_estimate=cost("attn_bwd"),
    )(seq, *near(qkv, y, dy, dinv))


def finish(part, came, tok, dh, gains, hres, out_part, out_came, placing):
    n_tok, width = part.shape
    steps = 2
    size = n_tok // steps

    def body(
        part_ref, came_ref, tok_ref, dh_ref, gain_ref, h_ref, op_ref, oc_ref, p_ref,
        grad_ref, out_ref, low_ref,
    ):
        gain = gain_ref[0:1, :]

        def rows(at):
            d = (part_ref[at, :].astype(F32) + came_ref[at, :].astype(F32)) * gain
            x = tok_ref[at, :].astype(F32)
            inverse = lax.rsqrt(jnp.mean(x * x, axis=-1, keepdims=True) + EPS)
            xr = x * inverse
            back = inverse * (d - xr * jnp.mean(d * xr, axis=-1, keepdims=True))
            low_ref[at, :] = (dh_ref[at, :] + back).astype(BF16)
            both = op_ref[at, :].astype(F32) + oc_ref[at, :].astype(F32)
            below = pl.ds(pl.multiple_of(size + at.start, 64), at.size)
            low_ref[below, :] = (h_ref[at, :] + both).astype(BF16)

        row_chunks(size, 64, rows)
        placed = dot_nt(low_ref[...], p_ref[...]).astype(BF16)
        grad_ref[...] = placed[:size]
        out_ref[...] = placed[size:]

    at = rows_spec(size, width)
    out = jax.ShapeDtypeStruct((n_tok, width), BF16)
    return pl.pallas_call(
        body,
        name="finish",
        grid=(steps,),
        out_shape=(out, out),
        in_specs=[at, at, at, at, pl.BlockSpec((8, width), lambda i: (0, 0)), at, at, at]
        + [pl.BlockSpec((width, width), lambda i: (0, 0))],
        out_specs=(at, at),
        scratch_shapes=[pltpu.VMEM((2 * size, width), BF16)],
        compiler_params=params(28),
        cost_estimate=cost("finish"),
    )(part, came, tok, *near(dh), gains, *near(hres), out_part, out_came, placing)


def local(
    lay,
    tokens,
    seq_lengths,
    w_query,
    w_key,
    w_value,
    w_output,
    w_gate,
    w_up,
    w_down,
    gain_attn,
    gain_mlp,
    cotangent,
):
    me = lax.axis_index(AXES).astype(jnp.int32)
    core = me % 2
    index = (me - core).reshape(1)
    rows, length = w_query.shape[0], tokens.shape[0]
    nq, nv, nf = w_query.shape[1] // 2, w_value.shape[1] // 2, w_gate.shape[1] // 2
    stride = nf + -nf % LANES
    order = Order()
    masks = split_masks(lay)
    flat_masks = sum(masks, [])
    both = sum(plane_masks(lay, [0]), [])
    places_z = {m | z: (j, i) for j, z in enumerate(masks_of(lay.z)) for i, m in enumerate(both)}
    places_z = [places_z[m] for m in flat_masks]

    def flat(arrays):
        return [a.reshape(-1, a.shape[-1]) for a in arrays]

    def blocks(arrays):
        return [a.reshape(-1, rows, a.shape[-1]) for a in arrays]
    dims = (nq, nv, 2 * nq + 2 * nv + LANES)

    keep_0, keep_gu, keep_d, give = prepare(
        core.reshape(1),
        [[w_query, w_key, w_value, w_output.T], [w_gate, w_up], [w_down.T]],
        [gain_attn, gain_mlp],
    )
    came = lay.swap(give, 1)
    tok_other, seq_other = lay.swap(tokens, 1), lay.swap(seq_lengths, 1)
    cot_other = lay.swap(cotangent, 1)
    came = order(came)
    at_d = dims[2] + 2 * stride

    def by_core(own, other):
        return jnp.where(core == 0, jnp.stack([own, other]), jnp.stack([other, own]))

    z_0 = GatherZ(lay, by_core(keep_0, came[:, : dims[2]]))
    z_0.first()
    z_0.second()
    halves_d = by_core(keep_d, came[:, at_d:])
    p_d = GatherPlane(lay, halves_d[:1], halves_d[1:])
    tok_other, seq_other, cot_other = order(tok_other, seq_other, cot_other)
    z_gu = GatherZ(lay, order(by_core(keep_gu, came[:, dims[2] : at_d])))
    z_gu.first()
    z_0.third(order)
    p_d.second(order)

    def halves(z):
        blocks = z.done(order)
        return [jnp.stack([b[h] for b in blocks]) for h in range(2)]

    p_0 = GatherPlane(lay, *halves(z_0))
    z_gu.second(order)
    held_d = p_d.joined(order)
    z_gu.third(order)
    p_0.second(order)
    z_d = GatherZ(lay, order(held_d))
    z_d.first()
    p_gu = GatherPlane(lay, *order(*halves(z_gu)))
    arrays_0 = order(*p_0.arrays())
    z_d.second(order)
    w_0 = flat(arrays_0)
    seq = jnp.concatenate([seq_lengths, seq_other], axis=0)
    tok = jnp.concatenate([tokens, tok_other], axis=0)
    grad_out = jnp.concatenate([cotangent, cot_other], axis=0)
    tok, grad_out, placing = order(*shuffle(index, flat_masks, [tok, grad_out]))
    z_d.third(order)
    p_gu.second(order)
    def swap_all(values):
        return [lay.swap(v, 1) for v in values]

    normed_one, qkv, y, dinv, gains, *part_o = attn_fwd(w_0, seq, tok, dims)
    part_o = order(*part_o)
    came_o = swap_all(part_o)
    w_d = z_d.done(order)
    if rows % 16:
        order_d = [j * len(both) + i for j, i in places_z]
        w_d = jnp.take(jnp.concatenate(w_d), jnp.asarray(order_d), axis=0)
        w_d, places_z = jnp.split(w_d, 4), None
    w_d = flat(w_d)
    d_act = order(down_back(w_d, places_z, rows, grad_out))
    w_gu = flat(order(*p_gu.arrays()))
    came_o = order(*came_o)
    hres, normed_two = residual(tok, part_o, came_o, gains)
    normed_two = order(normed_two)
    first = stride // 2 + -(stride // 2) % LANES
    act, act_rest, d_gate, d_up = order(*gated(w_gu, normed_two, d_act, first))

    def grad(lefts, rights, gain=None, name="weight_grad", places=None):
        return blocks(order(*weight_grad(lefts, rights, gain, name, places, rows)))

    z_order = low_first(lay)
    half_z = len(z_order) // 2
    places_r = {}
    for k, z in enumerate(z_order):
        for i, m in enumerate(both):
            places_r[m | z] = (k // half_z, (k % half_z) * len(both) + i)
    places_r = [places_r[m] for m in flat_masks]

    def down_grad():
        if rows % 16 == 0:
            return grad([grad_out], [act], name="grad_down", places=places_r)
        found = jnp.concatenate(grad([grad_out], [act], name="grad_down"))
        back = [0] * len(places_r)
        for p, (j, i) in enumerate(places_r):
            back[j * len(back) // 2 + i] = p
        return jnp.split(jnp.take(found, jnp.asarray(back), axis=0), 2)

    wanted = [masks_of(lay.z).index(m) for m in low_first(lay)]

    def along_z(stream, name="fold_plane"):
        return ReduceZ(lay, *order(*fold_plane(stream.pairs(order), wanted, name)))

    r_g = ReducePlane(
        lay, grad([*near(normed_two), grad_out], [d_gate, act_rest], name="grad_gate")
    )
    d_up = order(d_up)
    part_n2 = order(*sum_nt(w_gu, [d_gate, d_up], [0, stride], 2, "d_norm2"))
    came_n2 = swap_all(part_n2)
    act = order(act)
    zr_d = ReduceZ(lay, *down_grad())
    outs_u = grad(near(normed_two), [order(d_up)], name="grad_up")
    r_g.second(order, "fold_first")
    came_n2 = order(*came_n2)
    r_u = ReducePlane(lay, order(*outs_u))
    d_h, d_o, d_y, gg_mlp = norm_back(w_0, part_n2, came_n2, hres, order(grad_out), gains, dims)
    d_y = order(d_y)
    zr_d.second(order)
    d_qkv = order(attn_bwd(seq, qkv, y, order(d_y), dinv, dims))
    last_d = zr_d.last(order)
    r_u.second(order)
    wait_for(order, r_g)
    outs_0 = grad([normed_one, *near(d_o)], [order(d_qkv), y], (w_0, gains, gg_mlp), name="grad_attn")
    r_0 = ReducePlane(lay, order(*outs_0))
    zr_u = along_z(r_u, "fold_far")
    zr_g = along_z(r_g, "fold_next")
    part_n1 = order(*sum_nt(w_0, [order(d_qkv)], [0], 2, "norm_one_part"))
    part_out = order(*sum_nt(w_d, [act, order(act_rest)], [0, first], 2, "down", places_z, rows))
    r_0.second(order)
    zr_u.second(order)
    zr_g.second(order)
    zr_0 = along_z(r_0)
    came_rows = order(*swap_all(order(part_n1[1], part_out[1])))
    grad_tokens, layer_out = finish(
        part_n1[0], came_rows[0], tok, d_h, gains, hres, part_out[0], came_rows[1], placing
    )
    grad_tokens = order(grad_tokens)
    r_d = ReducePlane(lay, order(*fold_four(*order(*last_d))))
    zr_0.second(order)
    r_d.second(order)
    end_u = zr_u.last(order)
    end_g = zr_g.last(order)
    end_d = [a for pair in r_d.pairs(order) for a in pair]
    end_0 = zr_0.last(order)
    mine, give = add_up(core.reshape(1), [end_0, end_d, end_g, end_u])
    came = lay.swap(give, 1)
    at = 2 * nq + 2 * nv
    at_d = at + LANES
    at_g = at_d + first
    at_u = at_g + 2 * stride - first
    places = [
        [(0, nq)],
        [(nq, nq)],
        [(2 * nq, nv)],
        [(2 * nq + nv, nv)],
        [(at_g, nf)],
        [(at_u, nf)],
        [(at_d, first), (at_g + stride, nf - first)],
        [(at, LANES)],
    ]
    *grads, g_one, g_two = conclude(core.reshape(1), mine, came, places)
    grads[3], grads[6] = grads[3].T, grads[6].T
    return (layer_out, grad_tokens, *grads, g_one[0], g_two[0])


def solution(mesh):
    rows, cols, flat = P(AXES, None), P(None, AXES), P(AXES)
    return jax.shard_map(
        functools.partial(local, Layout(mesh)),
        mesh=mesh,
        in_specs=(rows, rows, rows, rows, rows, cols, rows, rows, cols, flat, flat, rows),
        out_specs=(rows, rows, rows, rows, rows, cols, rows, rows, cols, flat, flat),
        check_vma=False,
    )
```

```python
import functools
import math

import jax
import jax.numpy as jnp
from jax import lax
from jax.experimental import pallas as pl
from jax.experimental.pallas import tpu as pltpu
from jax.sharding import PartitionSpec as P

H = 16
F = 16
EPS = 1e-05
AXES = ("dp", "fsdp")
LANES = 128
F32 = jnp.float32
BF16 = jnp.bfloat16

VMEM_SPEC = pl.BlockSpec(memory_space=pltpu.VMEM)
SMEM_SPEC = pl.BlockSpec(memory_space=pltpu.SMEM)
ANY_SPEC = pl.BlockSpec(memory_space=pl.ANY)


def dot_nn(a, b):
    return lax.dot_general(a, b, (((1,), (0,)), ((), ())), preferred_element_type=F32)


def dot_nt(a, b):
    return lax.dot_general(a, b, (((1,), (1,)), ((), ())), preferred_element_type=F32)


def dot_tn(a, b):
    return lax.dot_general(a, b, (((0,), (0,)), ((), ())), preferred_element_type=F32)


class Layout:
    def __init__(self, mesh):
        dp, fsdp = mesh.shape["dp"], mesh.shape["fsdp"]
        self.count = dp * fsdp
        x_bits = int(math.log2(fsdp)) - 1
        y_bits = int(math.log2(dp)) // 3
        all_bits = int(math.log2(self.count))
        self.x = [1 << (1 + i) for i in range(x_bits)]
        self.y = [1 << (1 + x_bits + i) for i in range(y_bits)]
        self.z = [1 << i for i in range(1 + x_bits + y_bits, all_bits)]

    def swap(self, value, bit):
        return lax.ppermute(value, AXES, [(i, i ^ bit) for i in range(self.count)])


def masks_of(bits):
    masks = [0]
    for bit in bits:
        masks = masks + [m | bit for m in masks]
    return masks


class Order:
    def __init__(self):
        self.last = None

    def __call__(self, *values):
        held = values if self.last is None else (*values, self.last)
        held = lax.optimization_barrier(held)
        self.last = held[0]
        return held[: len(values)] if len(values) > 1 else held[0]


def behind(value, order=None):
    return value if order is None else order(value)


def plane_masks(lay, base):
    found = []
    for half, bits in enumerate((lay.x + lay.y, lay.y + lay.x)):
        masks = [m | half for m in base]
        for bit in bits:
            masks = masks + [m | bit for m in masks]
        found.append(masks)
    return found


def split_masks(lay):
    return [
        part
        for masks in plane_masks(lay, masks_of(lay.z))
        for part in (masks[: len(masks) // 2], masks[len(masks) // 2 :])
    ]


class GatherZ:
    def __init__(self, lay, block):
        self.lay = lay
        self.bits = list(reversed(lay.z))
        self.found = {0: block}

    def first(self, *order):
        bit = self.bits[0]
        self.found[bit] = self.lay.swap(behind(self.found[0], *order), bit)

    def second(self, *order):
        for bit in self.bits[1:]:
            self.found[bit] = self.lay.swap(behind(self.found[0], *order), bit)

    def third(self, order, everything=False):
        if everything:
            for bit, value in zip(self.bits, order(*[self.found[bit] for bit in self.bits])):
                self.found[bit] = value
        else:
            self.found[self.bits[0]] = order(self.found[self.bits[0]])
        for i, bit in enumerate(self.bits[1:], 1):
            for m in masks_of(self.bits[:i])[1:]:
                self.found[m | bit] = self.lay.swap(self.found[m], bit)

    def done(self, order):
        masks = masks_of(self.lay.z)
        return order(*[self.found[m] for m in masks])


class GatherPlane:
    def __init__(self, lay, *halves):
        self.lay, self.halves = lay, halves
        self.orders = (lay.x + lay.y, lay.y + lay.x)
        self.came = [lay.swap(h, bits[0]) for h, bits in zip(halves, self.orders)]

    def second(self, order):
        came = order(*self.came)
        self.held, self.came = [], []
        for held, got, bits in zip(self.halves, came, self.orders):
            held = jnp.concatenate([held, got], axis=0)
            for bit in bits[1:-1]:
                held = jnp.concatenate([held, self.lay.swap(held, bit)], axis=0)
            self.held.append(held)
            self.came.append(self.lay.swap(held, bits[-1]))

    def arrays(self):
        return [self.held[0], self.came[0], self.held[1], self.came[1]]

    def joined(self, order):
        came = order(*self.came)
        return jnp.concatenate([self.held[0], came[0], self.held[1], came[1]], axis=0)


def add_low(a, b):
    return (a.astype(F32) + b.astype(F32)).astype(BF16)


def fold(pairs, name="fold"):
    n = len(pairs)

    def body(*refs):
        ins, outs = refs[: 2 * n], refs[2 * n :]
        step = pl.program_id(0)
        for i in range(n):
            value = add_low(ins[2 * i][...], ins[2 * i + 1][...])

            def put(ref, value=value):
                ref[...] = value

            pl.when(step == 0)(functools.partial(put, outs[2 * i + 1]))
            pl.when(step == 1)(functools.partial(put, outs[2 * i]))

    def half(a):
        return (a.shape[0] // 2, *a.shape[1:])

    def spec(a, there):
        rest = (0,) * (a.ndim - 1)
        return pl.BlockSpec(half(a), (lambda i: (1 - i, *rest)) if there else (lambda i: (0, *rest)))

    flat = [a for pair in pairs for a in pair]
    outs = pl.pallas_call(
        body,
        name=name,
        grid=(2,),
        out_shape=tuple(jax.ShapeDtypeStruct(half(a), BF16) for a in flat),
        in_specs=[spec(a, True) for a in flat],
        out_specs=tuple(spec(a, False) for a in flat),
        compiler_params=params(FOLD_MEGABYTES),
        cost_estimate=cost(name),
    )(*flat)
    return [(outs[2 * i], outs[2 * i + 1]) for i in range(n)]


def fold_plane(pairs, wanted, name="fold_plane"):
    shape = (len(wanted) // 2, 2, *pairs[0][0].shape[1:])
    n = shape[0]

    def body(*refs):
        ins, outs = refs[:4], refs[4:]
        for place, i in enumerate(wanted):
            for h in range(2):
                outs[place // n][place % n, h] = add_low(ins[2 * h][i], ins[2 * h + 1][i])

    return pl.pallas_call(
        body,
        name=name,
        out_shape=(jax.ShapeDtypeStruct(shape, BF16),) * 2,
        in_specs=[VMEM_SPEC] * 4,
        out_specs=(VMEM_SPEC,) * 2,
        compiler_params=params(FOLD_MEGABYTES),
        cost_estimate=cost(name),
    )(*[a for pair in pairs for a in pair])


class ReducePlane:
    def __init__(self, lay, arrays):
        self.lay = lay
        self.kept = [arrays[0], arrays[2]]
        self.orders = (lay.x + lay.y, lay.y + lay.x)
        self.came = [lay.swap(a, bits[-1]) for a, bits in zip(arrays[1::2], self.orders)]

    def second(self, order, name="fold"):
        for level in reversed(range(len(self.orders[0]) - 1)):
            came = order(*self.came)
            found = fold(list(zip(self.kept, came)), name)
            flat = order(*[a for pair in found for a in pair])
            found = list(zip(flat[::2], flat[1::2]))
            self.kept = [kept for kept, _ in found]
            self.came = [
                self.lay.swap(sent, bits[level]) for (_, sent), bits in zip(found, self.orders)
            ]

    def pairs(self, order):
        return list(zip(self.kept, order(*self.came)))


class ReduceZ:
    def __init__(self, lay, kept, sent):
        self.lay = lay
        self.bits = list(lay.z)
        self.kept = kept
        self.came = lay.swap(sent, self.bits[0])

    def second(self, order):
        while len(self.bits) > 1:
            self.bits.pop(0)
            self.kept, sent = order(*fold([(self.kept, order(self.came))], "fold_z")[0])
            self.came = self.lay.swap(sent, self.bits[0])

    def last(self, order):
        return self.kept, order(self.came)


def fold_four(kept, came):
    n = kept.shape[0] // 4

    def body(kept_ref, came_ref, *outs):
        for i, out in enumerate(outs):
            out[...] = add_low(kept_ref[i * n : (i + 1) * n], came_ref[i * n : (i + 1) * n])

    return pl.pallas_call(
        body,
        name="fold_four",
        out_shape=(jax.ShapeDtypeStruct((n, *kept.shape[1:]), BF16),) * 4,
        in_specs=[VMEM_SPEC] * 2,
        out_specs=(VMEM_SPEC,) * 4,
        compiler_params=params(FOLD_MEGABYTES),
        cost_estimate=cost("fold_four"),
    )(kept, came)


def add_up(core, ends):
    rows = ends[0][0].shape[2]
    widths = [end[0].shape[-1] for end in ends]
    flat = [a for end in ends for a in end]

    def body(core_ref, *refs):
        first = core_ref[0] == 0
        ins = list(refs[:-2])
        at = 0
        for end, width in zip(ends, widths):
            used = [ins.pop(0)[0].astype(F32) for _ in end]
            if len(end) == 2:
                total = used[0] + used[1]
                low, high = total[0], total[1]
            else:
                low, high = used[0] + used[1], used[2] + used[3]
            refs[-2][:, at : at + width] = jnp.where(first, low, high)
            refs[-1][:, at : at + width] = jnp.where(first, high, low)
            at += width

    return pl.pallas_call(
        body,
        name="add_up",
        out_shape=(jax.ShapeDtypeStruct((rows, sum(widths)), F32),) * 2,
        in_specs=[SMEM_SPEC] + [VMEM_SPEC] * len(flat),
        out_specs=(VMEM_SPEC,) * 2,
        compiler_params=params(FOLD_MEGABYTES),
        cost_estimate=cost("add_up"),
    )(core, *flat)


def wait_for(order, *streams):
    values = [v for s in streams for v in (s.came if isinstance(s.came, list) else [s.came])]
    values = list(order(*values)) if len(values) > 1 else [order(values[0])]
    for s in streams:
        if isinstance(s.came, list):
            s.came = [values.pop(0) for _ in s.came]
        else:
            s.came = values.pop(0)


def low_first(lay):
    bits = lay.z
    masks = [0]
    for bit in reversed(bits):
        masks = masks + [m | bit for m in masks]
    return masks


SAID_FLOPS = {"shuffle": 10**10, "attn_fwd": 10**10, "down_back": 10**10, "residual": 10**10, "gated": 10**10, "fold_first": 5 * 10**9, "fold_next": 10**9, "fold_far": 5 * 10**9}
FOLD_FLOPS = 10**9
FOLD_MEGABYTES = 16


def cost(name):
    flops = SAID_FLOPS.get(name, FOLD_FLOPS if name.startswith("fold") else 1)
    return pl.CostEstimate(flops=flops, bytes_accessed=1, transcendentals=0)


def near(*values):
    return [pltpu.with_memory_space_constraint(v, pltpu.VMEM) for v in values]


def params(megabytes):
    return pltpu.CompilerParams(vmem_limit_bytes=megabytes << 20)


def rows_spec(size, cols, last=None):
    return pl.BlockSpec((size, cols), lambda i: (i if last is None else jnp.minimum(i, last), 0))


def piece_of(i, pieces, steps, turn):
    block = lax.rem(i + steps // 2, steps) if turn else i
    return block // (steps // pieces), lax.rem(block, steps // pieces)


def piece_specs(pieces, steps, size, width, turn=False):
    def spec(q):
        def at(i):
            piece, block = piece_of(i, pieces, steps, turn)
            last = steps // pieces - 1
            return (jnp.where(piece == q, block, jnp.where(piece < q, 0, last)), 0)

        return pl.BlockSpec((size, width), at)

    return [spec(q) for q in range(pieces)]


def with_piece(refs, steps, body, turn=False):
    piece, _ = piece_of(pl.program_id(0), len(refs), steps, turn)
    for q, ref in enumerate(refs):
        pl.when(piece == q)(functools.partial(body, ref))


def row_chunks(total, size, body):
    def step(i, carry):
        body(pl.ds(pl.multiple_of(i * size, size), size))
        return carry

    lax.fori_loop(0, total // size, step, 0)


def make_mask(seq_ref, b, mask_ref):
    rows, cols = mask_ref.shape
    slots = seq_ref.shape[1]
    ends = []
    total = jnp.int32(0)
    for j in range(slots):
        total = total + seq_ref[b, j]
        ends.append(total)

    def body(at):
        t = lax.broadcasted_iota(jnp.int32, (at.size, cols), 0) + at.start
        s = lax.broadcasted_iota(jnp.int32, (at.size, cols), 1)
        seg_t = jnp.zeros_like(t)
        seg_s = jnp.zeros_like(s)
        for e in ends:
            seg_t = seg_t + (t >= e).astype(jnp.int32)
            seg_s = seg_s + (s >= e).astype(jnp.int32)
        seen = (s <= t) & (seg_t == seg_s) & (t < total)
        mask_ref[at, :] = jnp.where(seen, 0.5, 0.0).astype(F32)

    row_chunks(rows, 64, body)
    return total


def stacked(refs, start, size):
    return jnp.concatenate([r[:, start : start + size] for r in refs], axis=0)


def whole_specs(arrays):
    return [pl.BlockSpec(a.shape, lambda i: (0,) * a.ndim) for a in arrays]


def shuffle(index, masks, values):
    n, width = values[0].shape
    rows = width // len(masks)
    steps = n // 256
    count = len(values)

    def body(index_ref, masks_ref, *refs):
        ins, outs, order_ref = refs[:count], refs[count:-1], refs[-1]

        @pl.when(pl.program_id(0) == 0)
        def _():
            def fill(at):
                r = lax.broadcasted_iota(jnp.int32, (at.size, width), 0) + at.start
                c = lax.broadcasted_iota(jnp.int32, (at.size, width), 1)
                block = jnp.bitwise_xor(masks_ref[...], index_ref[0])
                here = (r // rows == block) & (r % rows == c % rows)
                order_ref[at, :] = jnp.where(here, 1.0, 0.0).astype(BF16)

            row_chunks(width, 128, fill)

        for i, o in zip(ins, outs):
            o[...] = dot_nn(i[...], order_ref[...]).astype(BF16)

    table = jnp.repeat(jnp.asarray(masks, jnp.int32), rows)[None]
    at = rows_spec(256, width)
    keep = pl.BlockSpec((width, width), lambda i: (0, 0))
    return pl.pallas_call(
        body,
        name="shuffle",
        grid=(steps,),
        out_shape=(*[pltpu.HBM(v.shape, BF16) for v in values], pltpu.HBM((width, width), BF16)),
        in_specs=[SMEM_SPEC, pl.BlockSpec((1, width), lambda i: (0, 0))] + [at] * count,
        out_specs=(*[at] * count, keep),
        compiler_params=params(20),
        cost_estimate=cost("shuffle"),
    )(index, table, *values)


def prepare(core, groups, gains):
    rows = groups[0][0].shape[0]
    flat = [w for group in groups for w in group]
    padded = [w.shape[1] // 2 + -(w.shape[1] // 2) % LANES for w in flat]
    n_in = len(flat)
    widths, at = [], 0
    for group in groups:
        widths.append(sum(padded[at : at + len(group)]))
        at += len(group)
    widths[0] += LANES

    def body(core_ref, one_ref, two_ref, *refs):
        ins, keeps, give_ref = refs[:n_in], refs[n_in:-1], refs[-1]
        first = core_ref[0] == 0
        place, start = 0, 0
        for number, (group, keep_ref) in enumerate(zip(groups, keeps)):
            at = 0
            for _ in group:
                value = ins[place][...]
                half = value.shape[1] // 2
                low, high = value[:, :half].astype(F32), value[:, half:].astype(F32)
                spare = padded[place] - half
                for ref, base, one, two in (
                    (keep_ref, 0, low, high),
                    (give_ref, start, high, low),
                ):
                    ref[:, base + at : base + at + half] = jnp.where(first, one, two).astype(BF16)
                    if spare:
                        zeros = jnp.zeros((rows, spare), BF16)
                        ref[:, base + at + half : base + at + half + spare] = zeros
                at += padded[place]
                place += 1
            if number == 0:
                lines = []
                for ref in (one_ref, two_ref):
                    gain = ref[...]
                    high = gain.astype(BF16).astype(F32)
                    lines += [high, gain - high]
                lines = jnp.concatenate(lines + [jnp.zeros((LANES - 4, rows), F32)], axis=0)
                turned = lines.T.astype(BF16)
                keep_ref[:, at : at + LANES] = turned
                give_ref[:, at : at + LANES] = turned
                at += LANES
            start += at

    out = [jax.ShapeDtypeStruct((rows, n), BF16) for n in [*widths, sum(widths)]]
    return pl.pallas_call(
        body,
        name="prepare",
        out_shape=tuple(out),
        in_specs=[SMEM_SPEC] + [VMEM_SPEC] * (n_in + 2),
        out_specs=(VMEM_SPEC,) * len(out),
        compiler_params=params(60),
    )(core, *[g[None] for g in gains], *flat)


def conclude(core, mine, came, places):
    rows = mine.shape[0]
    n = len(places) - 1

    def body(core_ref, mine_ref, came_ref, *refs):
        first = core_ref[0] == 0
        for segments, ref in zip(places[:n], refs):
            half, done = sum(size for _, size in segments), 0
            for at, size in segments:
                own, other = mine_ref[:, at : at + size], came_ref[:, at : at + size]
                ref[:, done : done + size] = jnp.where(first, own, other)
                ref[:, half + done : half + done + size] = jnp.where(first, other, own)
                done += size
        at = places[n][0][0]
        own = mine_ref[:, at : at + LANES].T
        other = came_ref[:, at : at + LANES].T
        refs[n][...] = own[0:1] + other[0:1]
        refs[n + 1][...] = own[1:2]

    halves = [sum(size for _, size in segments) for segments in places[:n]]
    out = [jax.ShapeDtypeStruct((rows, 2 * half), F32) for half in halves]
    out += [jax.ShapeDtypeStruct((1, rows), F32)] * 2
    return pl.pallas_call(
        body,
        name="conclude",
        out_shape=tuple(out),
        in_specs=[SMEM_SPEC, VMEM_SPEC, VMEM_SPEC],
        out_specs=(VMEM_SPEC,) * len(out),
        compiler_params=params(16),
    )(core, mine, came)


def attn_fwd(weights, seq, tok, dims):
    n_tok, width, buffers = tok.shape[0], tok.shape[1], seq.shape[0]
    length = n_tok // buffers
    nq, nv, cols = dims
    n_qkv = 2 * nq + nv
    n_in = len(weights)

    def body(seq_ref, tok_ref, *refs):
        w_in = refs[:n_in]
        normed_ref, qkv_ref, y_ref, dinv_ref, gain_ref = refs[n_in : n_in + 5]
        part_refs = refs[n_in + 5 : n_in + 5 + 2 * buffers]
        mask_ref = refs[n_in + 5 + 2 * buffers]
        w_gain = stacked(w_in, n_qkv + nv, LANES).astype(F32).T
        gain_ref[0:1, :] = w_gain[0:1] + w_gain[1:2]
        gain_ref[1:2, :] = w_gain[2:3] + w_gain[3:4]
        gain_ref[2:8, :] = jnp.zeros((6, width), F32)
        gain = gain_ref[0:1, :]

        def project(at):
            x = tok_ref[at, :].astype(F32)
            inverse = lax.rsqrt(jnp.mean(x * x, axis=-1, keepdims=True) + EPS)
            normed = (x * inverse * gain).astype(BF16)
            normed_ref[at, :] = normed
            qkv_ref[at, :] = dot_nn(normed, stacked(w_in, 0, n_qkv)).astype(BF16)

        row_chunks(n_tok, 256, project)

        for b in range(buffers):
            total = make_mask(seq_ref, b, mask_ref)
            base = b * length

            def pair(hp, carry):
                lane = lax.broadcasted_iota(jnp.int32, (1, LANES), 1)
                k = qkv_ref[base : base + length, nq : 2 * nq]
                v_at = pl.ds(pl.multiple_of(2 * nq + hp * LANES, LANES), LANES)
                v = qkv_ref[base : base + length, v_at]
                step = length // 2
                for tb in range(2):
                    rows = slice(base + tb * step, base + (tb + 1) * step)
                    seen = (tb + 1) * step
                    q = qkv_ref[rows, :nq] * jnp.asarray(0.25, BF16)
                    mask = mask_ref[tb * step : (tb + 1) * step, :seen]
                    row = lax.broadcasted_iota(jnp.int32, (step, 1), 0) + tb * step
                    pad = (row >= total).astype(F32)
                    found = []
                    for j in range(2):
                        k_h = jnp.where(lane // F == 2 * hp + j, k[:seen], jnp.zeros((), BF16))
                        v_h = jnp.where(lane // 64 == j, v[:seen], jnp.ones((), BF16))
                        one = dot_nt(q, k_h) + 1.0
                        share = ((one * one + 1.0) * mask).astype(BF16)
                        mixed = dot_nn(share, v_h)
                        inverse = 1.0 / (pltpu.roll(mixed, 64, 1) + pad)
                        found.append((mixed * inverse, inverse))
                    low = lane < 64
                    y_at = pl.ds(pl.multiple_of(hp * LANES, LANES), LANES)
                    y_ref[rows, y_at] = jnp.where(low, found[0][0], found[1][0]).astype(BF16)
                    dinv_ref[rows, y_at] = jnp.where(low, found[0][1], found[1][1])
                return carry

            lax.fori_loop(0, nv // LANES, pair, 0)
            for half in range(2):
                at = slice(base + half * (length // 2), base + (half + 1) * (length // 2))
                part = dot_nt(y_ref[at, :], stacked(w_in, n_qkv, nv))
                part_refs[2 * b + half][...] = part.astype(BF16)

    return pl.pallas_call(
        body,
        name="attn_fwd",
        out_shape=(
            pltpu.HBM((n_tok, width), BF16),
            pltpu.VMEM((n_tok, n_qkv), BF16),
            pltpu.VMEM((n_tok, nv), BF16),
            pltpu.VMEM((n_tok, nv), F32),
            jax.ShapeDtypeStruct((8, width), F32),
            *(jax.ShapeDtypeStruct((length // 2, width), BF16) for _ in range(2 * buffers)),
        ),
        in_specs=[SMEM_SPEC] + [VMEM_SPEC] * (1 + n_in),
        out_specs=(VMEM_SPEC,) * (5 + 2 * buffers),
        scratch_shapes=[pltpu.VMEM((length, length), F32)],
        compiler_params=params(28),
        cost_estimate=cost("attn_fwd"),
    )(seq, tok, *weights)


def residual(tok, part, came, gains):
    n_tok, width = tok.shape
    steps = 4
    size = n_tok // steps

    n = len(part)

    def body(tok_ref, *refs):
        part_refs, came_refs = refs[:n], refs[n : 2 * n]
        gain_ref, hres_ref, normed_ref = refs[2 * n :]
        gain = gain_ref[1:2, :]

        def rows(at, part_ref, came_ref):
            x = tok_ref[at, :].astype(F32)
            x = x + (part_ref[at, :].astype(F32) + came_ref[at, :].astype(F32))
            hres_ref[at, :] = x
            inverse = lax.rsqrt(jnp.mean(x * x, axis=-1, keepdims=True) + EPS)
            normed_ref[at, :] = (x * inverse * gain).astype(BF16)

        pairs = list(zip(part_refs, came_refs[n // 2 :] + came_refs[: n // 2]))
        with_piece(pairs, steps, lambda pair: row_chunks(size, 64, lambda at: rows(at, *pair)))

    at = rows_spec(size, width)
    return pl.pallas_call(
        body,
        name="residual",
        grid=(steps,),
        out_shape=(pltpu.VMEM((n_tok, width), F32), pltpu.VMEM((n_tok, width), BF16)),
        in_specs=[at]
        + piece_specs(n, steps, size, width)
        + piece_specs(n, steps, size, width, True)
        + [pl.BlockSpec((8, width), lambda i: (0, 0))],
        out_specs=(at, at),
        compiler_params=params(16),
        cost_estimate=cost("residual"),
    )(tok, *part, *came, gains)


def in_order(refs, places, rows):
    if places is None:
        return jnp.concatenate([r[...] for r in refs], axis=0)
    return jnp.concatenate([refs[j][i * rows : (i + 1) * rows, :] for j, i in places], axis=0)


def down_back(weights, places, rows, grad_out):
    n_tok, width = grad_out.shape
    cols = weights[0].shape[1]
    steps = 4
    size = n_tok // steps

    def body(grad_ref, *refs):
        w = in_order(refs[:-1], places, rows)
        refs[-1][...] = dot_nn(grad_ref[...], w).astype(BF16)

    return pl.pallas_call(
        body,
        name="down_back",
        grid=(steps,),
        out_shape=pltpu.VMEM((n_tok, cols), BF16),
        in_specs=[rows_spec(size, width)] + whole_specs(weights),
        out_specs=rows_spec(size, cols),
        compiler_params=params(20),
        cost_estimate=cost("down_back"),
    )(grad_out, *weights)


def gated(weights, normed, d_act, first):
    n_tok, width = normed.shape
    cols = d_act.shape[1]
    n_in = len(weights)
    steps = 4
    size = n_tok // steps

    def body(normed_ref, d_act_ref, *refs):
        act_ref, rest_ref, d_gate_ref, d_up_ref = refs[n_in:]
        x = normed_ref[...]
        gate = dot_nn(x, stacked(refs[:n_in], 0, cols))
        up = dot_nn(x, stacked(refs[:n_in], cols, cols))
        sig = 1.0 / (1.0 + jnp.exp(-gate))
        silu = gate * sig
        act = (silu * up).astype(BF16)
        act_ref[...] = act[:, :first]
        rest_ref[...] = act[:, first:]
        d = d_act_ref[...].astype(F32)
        d_gate_ref[...] = (d * up * sig * (1.0 + gate * (1.0 - sig))).astype(BF16)
        d_up_ref[...] = (d * silu).astype(BF16)

    parts = (first, cols - first, cols, cols)
    return pl.pallas_call(
        body,
        name="gated",
        grid=(steps,),
        out_shape=tuple(pltpu.VMEM((n_tok, c), BF16) for c in parts),
        in_specs=[rows_spec(size, width), rows_spec(size, cols)] + whole_specs(weights),
        out_specs=tuple(rows_spec(size, c) for c in parts),
        compiler_params=params(30),
        cost_estimate=cost("gated"),
    )(*near(normed, d_act), *weights)


def weight_grad(lefts, rights, gain=None, name="weight_grad", places=None, rows=0):
    n_tok, width = lefts[0].shape
    sizes = [r.shape[1] for r in rights]
    cols = sum(sizes) + (LANES if gain is not None else 0)
    n, pieces = len(lefts), 4
    chunk = width // pieces
    out_rows = chunk if places is None else width // 2
    extras, specs = [], []
    if gain is not None:
        weights, gains, other = gain
        extras = [gains, other, *weights]
        specs = [pl.BlockSpec((8, chunk), lambda i: (0, i))] * 2 + whole_specs(weights)

    def body(*refs):
        left_refs, right_refs = refs[:n], refs[n : 2 * n]
        ins, outs = refs[2 * n : 2 * n + len(extras)], refs[2 * n + len(extras) :]

        values = [dot_tn(left[...], right[...]) for left, right in zip(left_refs, right_refs)]

        def put(out, w_ref):
            start = 0
            for value, size in zip(values, sizes):
                out[:, start : start + size] = value.astype(BF16)
                start += size
            if gain is not None:
                one = values[0] * w_ref[:, : sizes[0]].astype(F32)
                one = jnp.sum(one, axis=-1, keepdims=True)
                two = jnp.sum(ins[1][...], axis=0, keepdims=True)
                lines = [ins[0][0:1, :], two, jnp.zeros((LANES - 2, chunk), F32)]
                turned = jnp.concatenate(lines).T
                lane = lax.broadcasted_iota(jnp.int32, turned.shape, 1)
                turned = jnp.where(lane == 0, one / turned, turned)
                out[:, cols - LANES :] = turned.astype(BF16)

        if places is not None:
            value = values[0].astype(BF16)
            for p, (j, i) in enumerate(places):
                at = p * rows % chunk

                @pl.when(pl.program_id(0) == p * rows // chunk)
                def _(j=j, i=i, at=at):
                    outs[j][i * rows : (i + 1) * rows, :] = value[at : at + rows]

            return

        for q, out in enumerate(outs):
            w_ref = ins[2 + q] if gain is not None else None
            pl.when(pl.program_id(0) == q)(functools.partial(put, out, w_ref))

    return pl.pallas_call(
        body,
        name=name,
        grid=(pieces,),
        out_shape=(jax.ShapeDtypeStruct((out_rows, cols), BF16),) * (width // out_rows),
        in_specs=[pl.BlockSpec((n_tok, chunk), lambda i: (0, i))] * n
        + [pl.BlockSpec(r.shape, lambda i: (0, 0)) for r in rights]
        + specs,
        out_specs=(pl.BlockSpec((out_rows, cols), lambda i: (0, 0)),) * (width // out_rows),
        compiler_params=params(26),
        cost_estimate=cost(name),
    )(*lefts, *near(*rights), *extras)


def sum_nt(weights, lefts, starts, pieces, name, places=None, rows=0):
    n_tok = lefts[0].shape[0]
    width = sum(w.shape[0] for w in weights)
    n, n_in = len(lefts), len(weights)
    steps = 2
    size = n_tok // steps

    def body(*refs):
        left_refs, w_refs, out_refs = refs[:n], refs[n : n + n_in], refs[n + n_in :]

        if places is not None:
            left = jnp.concatenate([ref[...] for ref in left_refs], axis=1)
            values = [dot_nt(left, in_order(w_refs, places, rows))]
        else:
            values = []
            for w in w_refs:
                value = None
                for left, start in zip(left_refs, starts):
                    term = dot_nt(left[...], w[:, start : start + left.shape[1]])
                    value = term if value is None else value + term
                values.append(value)

        def put(ref):
            at = 0
            for value in values:
                ref[:, at : at + value.shape[1]] = value.astype(BF16)
                at += value.shape[1]

        with_piece(out_refs, steps, put)

    return pl.pallas_call(
        body,
        name=name,
        grid=(steps,),
        out_shape=(jax.ShapeDtypeStruct((n_tok // pieces, width), BF16),) * pieces,
        in_specs=[rows_spec(size, x.shape[1]) for x in lefts] + whole_specs(weights),
        out_specs=tuple(piece_specs(pieces, steps, size, width)),
        compiler_params=params(30),
        cost_estimate=cost(name),
    )(*near(*lefts), *weights)


def norm_back(weights, part, came, hres, grad_out, gains, dims):
    n_tok, width = hres.shape
    nq, nv, _ = dims
    n_qkv = 2 * nq + nv
    n_in = len(weights)
    steps = 4
    size = n_tok // steps
    n = len(part)

    def body(hres_ref, c_ref, gain_ref, *refs):
        part_refs, came_refs, refs = refs[:n], refs[n : 2 * n], refs[2 * n :]
        dh_ref, do_ref, dy_ref, gg_ref = refs[n_in:]
        gain = gain_ref[1:2, :]
        i = pl.program_id(0)

        @pl.when(i == 0)
        def _():
            gg_ref[...] = jnp.zeros_like(gg_ref)

        def rows(at, part_ref, came_ref):
            d = part_ref[at, :].astype(F32) + came_ref[at, :].astype(F32)
            h = hres_ref[at, :]
            inverse = lax.rsqrt(jnp.mean(h * h, axis=-1, keepdims=True) + EPS)
            hr = h * inverse
            gg_ref[...] += jnp.sum((d * hr).reshape(-1, 8, width), axis=0)
            dg = d * gain
            back = inverse * (dg - hr * jnp.mean(dg * hr, axis=-1, keepdims=True))
            dh = c_ref[at, :].astype(F32) + back

            @pl.when(i < steps // 2)
            def _():
                dh_ref[at, :] = dh

            do_ref[at, :] = dh.astype(BF16)

        pairs = list(zip(part_refs, came_refs[n // 2 :] + came_refs[: n // 2]))
        with_piece(pairs, steps, lambda pair: row_chunks(size, 64, lambda at: rows(at, *pair)))

        dy_ref[...] = dot_nn(do_ref[...], stacked(refs[:n_in], n_qkv, nv)).astype(BF16)

    at = rows_spec(size, width)
    keep = pl.BlockSpec((8, width), lambda i: (0, 0))
    return pl.pallas_call(
        body,
        name="norm_back",
        grid=(steps,),
        out_shape=(
            pltpu.VMEM((n_tok // 2, width), F32),
            pltpu.VMEM((n_tok, width), BF16),
            pltpu.VMEM((n_tok, nv), BF16),
            jax.ShapeDtypeStruct((8, width), F32),
        ),
        in_specs=[at, at, keep]
        + piece_specs(n, steps, size, width)
        + piece_specs(n, steps, size, width, True)
        + whole_specs(weights),
        out_specs=(
            rows_spec(size, width, last=steps // 2 - 1),
            at,
            rows_spec(size, nv),
            keep,
        ),
        compiler_params=params(20),
        cost_estimate=cost("norm_back"),
    )(*near(hres), grad_out, gains, *part, *came, *weights)


def attn_bwd(seq, qkv, y, dy, dinv, dims):
    n_tok, buffers = qkv.shape[0], seq.shape[0]
    length = n_tok // buffers
    nq, nv, _ = dims

    def body(seq_ref, qkv_ref, y_ref, dy_ref, dinv_ref, out_ref, mask_ref, dq_acc, dk_acc, dv_acc):
        for b in range(buffers):
            make_mask(seq_ref, b, mask_ref)
            base = b * length
            dq_acc[...] = jnp.zeros_like(dq_acc)
            dk_acc[...] = jnp.zeros_like(dk_acc)

            def pair(hp, carry):
                lane = lax.broadcasted_iota(jnp.int32, (1, LANES), 1)
                zero = jnp.zeros((), BF16)
                k = qkv_ref[base : base + length, nq : 2 * nq]
                v_at = pl.ds(pl.multiple_of(2 * nq + hp * LANES, LANES), LANES)
                y_at = pl.ds(pl.multiple_of(hp * LANES, LANES), LANES)
                v = qkv_ref[base : base + length, v_at]
                dv_acc[...] = jnp.zeros_like(dv_acc)
                step = length // 2
                for tb in range(2):
                    rows = slice(base + tb * step, base + (tb + 1) * step)
                    here = slice(tb * step, (tb + 1) * step)
                    seen = (tb + 1) * step
                    q = qkv_ref[rows, :nq] * jnp.asarray(0.25, BF16)
                    mask = mask_ref[here, :seen]
                    dyn = dy_ref[rows, y_at].astype(F32) * dinv_ref[rows, y_at]
                    dot_y = dyn * y_ref[rows, y_at].astype(F32)
                    dyn = dyn.astype(BF16)
                    for j in range(2):
                        mine = lane // F == 2 * hp + j
                        side = lane // 64 == j
                        k_h = jnp.where(mine, k[:seen], zero)
                        v_h = jnp.where(side, v[:seen], zero)
                        one = dot_nt(q, k_h) + 1.0
                        half_one = one * mask
                        weights = (half_one * one + mask).astype(BF16)
                        d_p = dot_nt(dyn, v_h)
                        shift = jnp.sum(jnp.where(side, dot_y, 0.0), axis=-1, keepdims=True)
                        d_a = ((d_p - shift) * half_one).astype(BF16)
                        dv_acc[:seen, :] += dot_tn(weights, jnp.where(side, dyn, zero))
                        dq_acc[here, :] += dot_nn(d_a, k_h)
                        dk_acc[:seen, :] += dot_tn(d_a, jnp.where(mine, q, zero))
                out_ref[base : base + length, v_at] = dv_acc[...].astype(BF16)
                return carry

            lax.fori_loop(0, nv // LANES, pair, 0)
            out_ref[base : base + length, :nq] = (dq_acc[...] * 0.5).astype(BF16)
            out_ref[base : base + length, nq : 2 * nq] = (dk_acc[...] * 2.0).astype(BF16)

    return pl.pallas_call(
        body,
        name="attn_bwd",
        out_shape=pltpu.VMEM(qkv.shape, BF16),
        in_specs=[SMEM_SPEC] + [VMEM_SPEC] * 4,
        out_specs=VMEM_SPEC,
        scratch_shapes=[
            pltpu.VMEM((length, length), F32),
            pltpu.VMEM((length, nq), F32),
            pltpu.VMEM((length, nq), F32),
            pltpu.VMEM((length, LANES), F32),
        ],
        compiler_params=params(20),
        cost_estimate=cost("attn_bwd"),
    )(seq, *near(qkv, y, dy, dinv))


def finish(part, came, tok, dh, gains, hres, out_part, out_came, placing):
    n_tok, width = part.shape
    steps = 2
    size = n_tok // steps

    def body(
        part_ref, came_ref, tok_ref, dh_ref, gain_ref, h_ref, op_ref, oc_ref, p_ref,
        grad_ref, out_ref, low_ref,
    ):
        gain = gain_ref[0:1, :]

        def rows(at):
            d = (part_ref[at, :].astype(F32) + came_ref[at, :].astype(F32)) * gain
            x = tok_ref[at, :].astype(F32)
            inverse = lax.rsqrt(jnp.mean(x * x, axis=-1, keepdims=True) + EPS)
            xr = x * inverse
            back = inverse * (d - xr * jnp.mean(d * xr, axis=-1, keepdims=True))
            low_ref[at, :] = (dh_ref[at, :] + back).astype(BF16)
            both = op_ref[at, :].astype(F32) + oc_ref[at, :].astype(F32)
            below = pl.ds(pl.multiple_of(size + at.start, 64), at.size)
            low_ref[below, :] = (h_ref[at, :] + both).astype(BF16)

        row_chunks(size, 64, rows)
        placed = dot_nt(low_ref[...], p_ref[...]).astype(BF16)
        grad_ref[...] = placed[:size]
        out_ref[...] = placed[size:]

    at = rows_spec(size, width)
    out = jax.ShapeDtypeStruct((n_tok, width), BF16)
    return pl.pallas_call(
        body,
        name="finish",
        grid=(steps,),
        out_shape=(out, out),
        in_specs=[at, at, at, at, pl.BlockSpec((8, width), lambda i: (0, 0)), at, at, at]
        + [pl.BlockSpec((width, width), lambda i: (0, 0))],
        out_specs=(at, at),
        scratch_shapes=[pltpu.VMEM((2 * size, width), BF16)],
        compiler_params=params(28),
        cost_estimate=cost("finish"),
    )(part, came, tok, *near(dh), gains, *near(hres), out_part, out_came, placing)


def local(
    lay,
    tokens,
    seq_lengths,
    w_query,
    w_key,
    w_value,
    w_output,
    w_gate,
    w_up,
    w_down,
    gain_attn,
    gain_mlp,
    cotangent,
):
    me = lax.axis_index(AXES).astype(jnp.int32)
    core = me % 2
    index = (me - core).reshape(1)
    rows, length = w_query.shape[0], tokens.shape[0]
    nq, nv, nf = w_query.shape[1] // 2, w_value.shape[1] // 2, w_gate.shape[1] // 2
    stride = nf + -nf % LANES
    order = Order()
    masks = split_masks(lay)
    flat_masks = sum(masks, [])
    both = sum(plane_masks(lay, [0]), [])
    places_z = {m | z: (j, i) for j, z in enumerate(masks_of(lay.z)) for i, m in enumerate(both)}
    places_z = [places_z[m] for m in flat_masks]

    def flat(arrays):
        return [a.reshape(-1, a.shape[-1]) for a in arrays]

    def blocks(arrays):
        return [a.reshape(-1, rows, a.shape[-1]) for a in arrays]
    dims = (nq, nv, 2 * nq + 2 * nv + LANES)

    keep_0, keep_gu, keep_d, give = prepare(
        core.reshape(1),
        [[w_query, w_key, w_value, w_output.T], [w_gate, w_up], [w_down.T]],
        [gain_attn, gain_mlp],
    )
    came = lay.swap(give, 1)
    tok_other, seq_other = lay.swap(tokens, 1), lay.swap(seq_lengths, 1)
    cot_other = lay.swap(cotangent, 1)
    came = order(came)
    at_d = dims[2] + 2 * stride

    def by_core(own, other):
        return jnp.where(core == 0, jnp.stack([own, other]), jnp.stack([other, own]))

    z_0 = GatherZ(lay, by_core(keep_0, came[:, : dims[2]]))
    z_0.first()
    z_0.second()
    halves_d = by_core(keep_d, came[:, at_d:])
    p_d = GatherPlane(lay, halves_d[:1], halves_d[1:])
    tok_other, seq_other, cot_other = order(tok_other, seq_other, cot_other)
    z_gu = GatherZ(lay, order(by_core(keep_gu, came[:, dims[2] : at_d])))
    z_gu.first()
    z_0.third(order)
    p_d.second(order)

    def halves(z):
        blocks = z.done(order)
        return [jnp.stack([b[h] for b in blocks]) for h in range(2)]

    p_0 = GatherPlane(lay, *halves(z_0))
    z_gu.second(order)
    held_d = p_d.joined(order)
    z_gu.third(order)
    p_0.second(order)
    z_d = GatherZ(lay, order(held_d))
    z_d.first()
    p_gu = GatherPlane(lay, *order(*halves(z_gu)))
    arrays_0 = order(*p_0.arrays())
    z_d.second(order)
    w_0 = flat(arrays_0)
    seq = jnp.concatenate([seq_lengths, seq_other], axis=0)
    tok = jnp.concatenate([tokens, tok_other], axis=0)
    grad_out = jnp.concatenate([cotangent, cot_other], axis=0)
    tok, grad_out, placing = order(*shuffle(index, flat_masks, [tok, grad_out]))
    z_d.third(order)
    p_gu.second(order)
    def swap_all(values):
        return [lay.swap(v, 1) for v in values]

    normed_one, qkv, y, dinv, gains, *part_o = attn_fwd(w_0, seq, tok, dims)
    part_o = order(*part_o)
    came_o = swap_all(part_o)
    w_d = z_d.done(order)
    if rows % 16:
        order_d = [j * len(both) + i for j, i in places_z]
        w_d = jnp.take(jnp.concatenate(w_d), jnp.asarray(order_d), axis=0)
        w_d, places_z = jnp.split(w_d, 4), None
    w_d = flat(w_d)
    d_act = order(down_back(w_d, places_z, rows, grad_out))
    w_gu = flat(order(*p_gu.arrays()))
    came_o = order(*came_o)
    hres, normed_two = residual(tok, part_o, came_o, gains)
    normed_two = order(normed_two)
    first = stride // 2 + -(stride // 2) % LANES
    act, act_rest, d_gate, d_up = order(*gated(w_gu, normed_two, d_act, first))

    def grad(lefts, rights, gain=None, name="weight_grad", places=None):
        return blocks(order(*weight_grad(lefts, rights, gain, name, places, rows)))

    z_order = low_first(lay)
    half_z = len(z_order) // 2
    places_r = {}
    for k, z in enumerate(z_order):
        for i, m in enumerate(both):
            places_r[m | z] = (k // half_z, (k % half_z) * len(both) + i)
    places_r = [places_r[m] for m in flat_masks]

    def down_grad():
        if rows % 16 == 0:
            return grad([grad_out], [act], name="grad_down", places=places_r)
        found = jnp.concatenate(grad([grad_out], [act], name="grad_down"))
        back = [0] * len(places_r)
        for p, (j, i) in enumerate(places_r):
            back[j * len(back) // 2 + i] = p
        return jnp.split(jnp.take(found, jnp.asarray(back), axis=0), 2)

    wanted = [masks_of(lay.z).index(m) for m in low_first(lay)]

    def along_z(stream, name="fold_plane"):
        return ReduceZ(lay, *order(*fold_plane(stream.pairs(order), wanted, name)))

    r_g = ReducePlane(
        lay, grad([*near(normed_two), grad_out], [d_gate, act_rest], name="grad_gate")
    )
    d_up = order(d_up)
    part_n2 = order(*sum_nt(w_gu, [d_gate, d_up], [0, stride], 2, "d_norm2"))
    came_n2 = swap_all(part_n2)
    act = order(act)
    zr_d = ReduceZ(lay, *down_grad())
    outs_u = grad(near(normed_two), [order(d_up)], name="grad_up")
    r_g.second(order, "fold_first")
    came_n2 = order(*came_n2)
    r_u = ReducePlane(lay, order(*outs_u))
    d_h, d_o, d_y, gg_mlp = norm_back(w_0, part_n2, came_n2, hres, order(grad_out), gains, dims)
    d_y = order(d_y)
    zr_d.second(order)
    d_qkv = order(attn_bwd(seq, qkv, y, order(d_y), dinv, dims))
    last_d = zr_d.last(order)
    r_u.second(order)
    wait_for(order, r_g)
    outs_0 = grad([normed_one, *near(d_o)], [order(d_qkv), y], (w_0, gains, gg_mlp), name="grad_attn")
    r_0 = ReducePlane(lay, order(*outs_0))
    zr_u = along_z(r_u, "fold_far")
    zr_g = along_z(r_g, "fold_next")
    part_n1 = order(*sum_nt(w_0, [order(d_qkv)], [0], 2, "norm_one_part"))
    part_out = order(*sum_nt(w_d, [act, order(act_rest)], [0, first], 2, "down", places_z, rows))
    r_0.second(order)
    zr_u.second(order)
    zr_g.second(order)
    zr_0 = along_z(r_0)
    came_rows = order(*swap_all(order(part_n1[1], part_out[1])))
    grad_tokens, layer_out = finish(
        part_n1[0], came_rows[0], tok, d_h, gains, hres, part_out[0], came_rows[1], placing
    )
    grad_tokens = order(grad_tokens)
    r_d = ReducePlane(lay, order(*fold_four(*order(*last_d))))
    zr_0.second(order)
    r_d.second(order)
    end_u = zr_u.last(order)
    end_g = zr_g.last(order)
    end_d = [a for pair in r_d.pairs(order) for a in pair]
    end_0 = zr_0.last(order)
    mine, give = add_up(core.reshape(1), [end_0, end_d, end_g, end_u])
    came = lay.swap(give, 1)
    at = 2 * nq + 2 * nv
    at_d = at + LANES
    at_g = at_d + first
    at_u = at_g + 2 * stride - first
    places = [
        [(0, nq)],
        [(nq, nq)],
        [(2 * nq, nv)],
        [(2 * nq + nv, nv)],
        [(at_g, nf)],
        [(at_u, nf)],
        [(at_d, first), (at_g + stride, nf - first)],
        [(at, LANES)],
    ]
    *grads, g_one, g_two = conclude(core.reshape(1), mine, came, places)
    grads[3], grads[6] = grads[3].T, grads[6].T
    return (layer_out, grad_tokens, *grads, g_one[0], g_two[0])


def solution(mesh):
    rows, cols, flat = P(AXES, None), P(None, AXES), P(AXES)
    return jax.shard_map(
        functools.partial(local, Layout(mesh)),
        mesh=mesh,
        in_specs=(rows, rows, rows, rows, rows, cols, rows, rows, cols, flat, flat, rows),
        out_specs=(rows, rows, rows, rows, rows, cols, rows, rows, cols, flat, flat),
        check_vma=False,
    )
```
